128 devices in a mesh: seq: 16 (over x, y_hi, core), head: 8 (over z, y_lo).
Axes of the slice: x: 4, y: 4 (y_hi: 2, y_lo: 2; y = y_hi * 2 + y_lo), z: 4, core: 2. Of those that a mesh axis runs over, the one named last changes fastest.
Arguments:
- queries: bfloat16 [8192, 4096], P('seq', 'head'), may hold values from -15 to 15
- keys: bfloat16 [8192, 2048], P('seq', 'head'), may hold values from -6 to 6
- values: bfloat16 [8192, 2048], P('seq', 'head'), may hold values from -6 to 6
- out_grad: bfloat16 [8192, 4096], P('seq', 'head'), may hold values from -48 to 48
- normed: bfloat16 [8192, 4608], P('seq'), may hold values from -1.1953125 to 1.1953125
- w_query: bfloat16 [4608, 4096], P(None, 'head'), may hold values from -0.125 to 0.125
- w_key: bfloat16 [4608, 2048], P(None, 'head'), may hold values from -0.125 to 0.125
- w_value: bfloat16 [4608, 2048], P(None, 'head'), may hold values from -0.125 to 0.125
- valid_len: int32 [16], replicated, may hold values from 128 to 512, as said below
Outputs:
- grad_x: bfloat16 [8192, 4608], P('seq', 'head')
- grad_wq: bfloat16 [4608, 4096], P('seq', 'head')
- grad_wk: bfloat16 [4608, 2048], P('seq', 'head')
- grad_wv: bfloat16 [4608, 2048], P('seq', 'head')
The draws below stay inside these ranges and needn't reach their ends.
Inputs may be any that keep to these rules, and one draw needn't show every extreme that they name: `valid_len`: every entry lies between 128 and 512; some shard is full and some shard has exactly 128 live slots.
All inputs are finite; a program needn't handle non-finite values.
Results may differ from the reference program's by a relative error of at most 0.024.
Values may be sent and summed in bfloat16 or wider, within the bound.
A program may use at most 192 MiB of HBM per device.

```python
import jax
import jax.numpy as jnp
from jax import lax

D = 4608
H = 32
KVH = 16
HD = 128
WINDOW = 4096
TOK_DEV = 512
SHARDS = 16
TOKENS = 8192
REACH = 8


def draw_valid_len(key, part):
    shortest = TOK_DEV // 4
    lengths = jax.random.randint(jax.random.fold_in(key, 11), (SHARDS,), shortest, TOK_DEV + 1)
    chosen = jax.random.permutation(jax.random.fold_in(key, 12), SHARDS)
    lengths = lengths.at[chosen[0]].set(TOK_DEV)
    lengths = lengths.at[chosen[1]].set(shortest)
    return lengths.astype(jnp.int32)


def raised(entries, rng, source, target, blocks, factor):
    def block_of(dim):
        return (jnp.arange(entries.shape[dim]) // (entries.shape[dim] // blocks)).reshape((-1,) + (1,) * (entries.ndim - 1 - dim))

    near = jax.random.permutation(rng, blocks)[block_of(target)]
    other_side = (block_of(target) + blocks // 2) % blocks
    return jnp.where((block_of(source) == near) | (block_of(source) == other_side), factor * entries, entries)


def steps_of(key, extent, shards, smallest, high):
    factor_of = 1.0
    for position, blocks in shards:
        heights = jax.random.uniform(jax.random.fold_in(jax.random.fold_in(key, 6), position), (blocks,), jnp.float32, smallest / len(shards), high / len(shards))
        factor_of = factor_of * jnp.repeat(jnp.exp(heights), extent[position] // blocks).reshape((-1,) + (1,) * (len(extent) - 1 - position))
    return factor_of


def scatter_about(key, shape, width, bound, shards=(), kind=jnp.bfloat16):
    level = steps_of(key, shape, shards, -0.22, 0.18) if shards else 1.0
    values = jax.random.normal(key, shape, jnp.float32) * width * level
    return jnp.minimum(jnp.maximum(values, -bound), bound).astype(kind)


def heavy_noise(own_key, extent, width, most, cuts, heavy, kind=jnp.bfloat16):
    values = width * jax.random.normal(own_key, extent, jnp.float32)
    if cuts:
        values = values * steps_of(own_key, extent, cuts, -0.22, 0.18)
    return jnp.clip(raised(values, jax.random.fold_in(own_key, 3), *heavy), -most, most).astype(kind)


def setup_inputs(seed: int = 0) -> dict:
    seeds = jax.random.split(jax.random.key(seed), 10)
    queries = scatter_about(seeds[0], (TOKENS, H * HD), 2.5, 15.0, ((0, 16), (1, 8)))
    keys = scatter_about(seeds[1], (TOKENS, KVH * HD), 1.0, 6.0, ((0, 16), (1, 8)))
    values = scatter_about(seeds[2], (TOKENS, KVH * HD), 1.0, 6.0, ((0, 16), (1, 8)))
    out_grad = scatter_about(seeds[3], (TOKENS, H * HD), 8.0, 48.0, ((0, 16), (1, 8)))
    normed = heavy_noise(seeds[4], (TOKENS, D), 0.2, 1.1953125, ((0, 16),), (0, 1, 16, 2.0))
    w_query = heavy_noise(seeds[5], (D, H * HD), D ** -0.5, 0.125, ((1, 8),), (1, 0, 8, 2.0))
    w_key = heavy_noise(seeds[6], (D, KVH * HD), D ** -0.5, 0.125, ((1, 8),), (1, 0, 8, 2.0))
    w_value = heavy_noise(seeds[7], (D, KVH * HD), D ** -0.5, 0.125, ((1, 8),), (1, 0, 8, 2.0))
    valid_len = draw_valid_len(jax.random.fold_in(seeds[9], 71), 0)
    return dict(queries=queries, keys=keys, values=values, out_grad=out_grad, normed=normed, w_query=w_query, w_key=w_key, w_value=w_value, valid_len=valid_len)


SOFT_CAP = 50.0
ROPE_BASE = 10000.0


def to_bfloat(array_in):
    return lax.optimization_barrier(array_in.astype(jnp.bfloat16)).astype(jnp.float32)


def rotate_back(gradient, positions, head_count):
    row_count = gradient.shape[0]
    half_width = HD // 2
    inverse_freq = ROPE_BASE ** (-(jnp.arange(half_width, dtype=jnp.float32) * (2.0 / HD)))
    angles = positions.astype(jnp.float32)[:, None] * inverse_freq[None, :]
    cosine = jnp.cos(angles)[:, None, :]
    sine_part = jnp.sin(angles)[:, None, :]
    per_head = gradient.reshape(row_count, head_count, HD)
    leading = per_head[:, :, :half_width]
    trailing = per_head[:, :, half_width:]
    rotated = jnp.concatenate([leading * cosine + trailing * sine_part, trailing * cosine - leading * sine_part], axis=2)
    return rotated.reshape(row_count, head_count * HD)


def times_t(left, right):
    return lax.dot_general(left, right, (((1,), (1,)), ((), ())), preferred_element_type=jnp.float32)


def inner_rows(left, right):
    return lax.dot_general(left, right, (((0,), (0,)), ((), ())), preferred_element_type=jnp.float32)


def reference(queries, keys, values, out_grad, normed, w_query, w_key, w_value, valid_len):
    group_size = H // KVH
    lead_rows = REACH * TOK_DEV
    span_rows = (REACH + 1) * TOK_DEV
    score_scale = (D // H) ** -0.5
    kv_width = KVH * HD
    positions = jnp.arange(TOKENS, dtype=jnp.int32)
    token_valid = (positions % TOK_DEV) < valid_len[positions // TOK_DEV]
    grad_rows = jnp.where(token_valid[:, None], out_grad, jnp.zeros_like(out_grad))
    key_value = jnp.concatenate([keys, values], axis=1)
    padded_kv = jnp.concatenate([jnp.zeros((lead_rows, 2 * kv_width), key_value.dtype), key_value], axis=0)
    padded_valid = jnp.concatenate([jnp.zeros((lead_rows,), dtype=bool), token_valid])

    def one_shard(carried, shard_index):
        first_row = (shard_index * TOK_DEV).astype(jnp.int32)
        query_blocks = lax.dynamic_slice_in_dim(queries, first_row, TOK_DEV, 0).astype(jnp.float32).reshape(TOK_DEV, KVH, group_size, HD)
        grad_blocks = lax.dynamic_slice_in_dim(grad_rows, first_row, TOK_DEV, 0).astype(jnp.float32).reshape(TOK_DEV, KVH, group_size, HD)
        window_kv = lax.dynamic_slice_in_dim(padded_kv, first_row, span_rows, 0).astype(jnp.float32)
        key_block = window_kv[:, :kv_width].reshape(span_rows, KVH, HD)
        value_block = window_kv[:, kv_width:].reshape(span_rows, KVH, HD)
        key_valid = lax.dynamic_slice_in_dim(padded_valid, first_row, span_rows, 0)
        query_pos = first_row + jnp.arange(TOK_DEV, dtype=jnp.int32)
        key_pos = first_row - lead_rows + jnp.arange(span_rows, dtype=jnp.int32)
        offset_gap = query_pos[:, None] - key_pos[None, :]
        allowed = (offset_gap >= 0) & (offset_gap < WINDOW) & (key_pos[None, :] >= 0) & (key_valid[None, :] | (offset_gap == 0))
        raw_scores = jnp.einsum("qhgd,khd->hgqk", query_blocks, key_block) * score_scale
        capped = SOFT_CAP * jnp.tanh(raw_scores / SOFT_CAP)
        running = jnp.sum(jnp.where(allowed, jnp.exp(capped), 0.0), axis=-1, keepdims=True)
        exact = jnp.where(allowed, jnp.exp(capped - jnp.log(running)), 0.0)
        rounded = to_bfloat(exact)
        attended = jnp.einsum("hgqk,khd->qhgd", rounded, value_block)
        row_delta = jnp.sum(grad_blocks * attended, axis=-1)
        grad_probs = jnp.einsum("qhgd,khd->hgqk", grad_blocks, value_block)
        grad_scores = exact * (grad_probs - jnp.transpose(row_delta, (1, 2, 0))[..., None]) * (1.0 - (capped / SOFT_CAP) ** 2)
        grad_scores = to_bfloat(grad_scores)
        query_grad = jnp.einsum("hgqk,khd->qhgd", grad_scores, key_block) * score_scale
        key_grad = jnp.einsum("hgqk,qhgd->khd", grad_scores, query_blocks) * score_scale
        value_grad = jnp.einsum("hgqk,qhgd->khd", rounded, grad_blocks)
        update = jnp.concatenate([key_grad.reshape(span_rows, kv_width), value_grad.reshape(span_rows, kv_width)], axis=1)
        current = lax.dynamic_slice_in_dim(carried, first_row, span_rows, 0)
        carried = lax.dynamic_update_slice_in_dim(carried, current + update, first_row, 0)
        return carried, query_grad.reshape(TOK_DEV, H * HD)

    initial = jnp.zeros((lead_rows + TOKENS, 2 * kv_width), jnp.float32)
    summed, query_parts = lax.scan(one_shard, initial, jnp.arange(SHARDS, dtype=jnp.int32))
    summed = summed[lead_rows:]
    query_grad = query_parts.reshape(TOKENS, H * HD)
    query_pre = rotate_back(query_grad, positions, H).astype(jnp.bfloat16)
    key_pre = rotate_back(summed[:, :kv_width], positions, KVH).astype(jnp.bfloat16)
    value_pre = summed[:, kv_width:].astype(jnp.bfloat16)
    grad_x = (times_t(query_pre, w_query) + times_t(key_pre, w_key) + times_t(value_pre, w_value)).astype(jnp.bfloat16)
    grad_wq = inner_rows(normed, query_pre).astype(jnp.bfloat16)
    grad_wk = inner_rows(normed, key_pre).astype(jnp.bfloat16)
    grad_wv = inner_rows(normed, value_pre).astype(jnp.bfloat16)
    return (grad_x, grad_wq, grad_wk, grad_wv)
```

```python
import functools

import jax
import jax.numpy as jnp
from jax import lax
from jax.experimental import pallas as pl
from jax.experimental.pallas import tpu as pltpu
from jax.sharding import PartitionSpec as P

D = 4608
H = 32
HD = 128
WINDOW = 4096
SOFT_CAP = 50.0
ROPE_BASE = 10000.0
SCALE = (D // H) ** (-0.5)

TOK = 512
NB = 10
TILE = 256
CHUNK = D // 4
HALF = CHUNK // 2
QTR = HALF // 2

BF = jnp.bfloat16
F32 = jnp.float32
MESH = pl.DeviceIdType.MESH
LOG2E = 1.4426950408889634


def nt(left, right):
    return lax.dot_general(left, right, (((1,), (1,)), ((), ())), preferred_element_type=F32)


def nn(left, right):
    return lax.dot_general(left, right, (((1,), (0,)), ((), ())), preferred_element_type=F32)


def here():
    s, h = lax.axis_index("seq"), lax.axis_index("head")
    return s // 4, (s // 2) % 2, s % 2, h // 2, h % 2


def at_seq(x, yh, core):
    return {"seq": (lax.rem(x + 4, 4) * 2 + yh) * 2 + core, "head": lax.axis_index("head")}


def at_head(z, yl):
    return {"seq": lax.axis_index("seq"), "head": lax.rem(z + 4, 4) * 2 + yl}


def remote(src, dst, send, recv, device):
    return pltpu.make_async_remote_copy(
        src_ref=src, dst_ref=dst, send_sem=send, recv_sem=recv, device_id=device, device_id_type=MESH
    )


def greet(devices):
    barrier = pltpu.get_barrier_semaphore()
    for device in devices:
        pl.semaphore_signal(barrier, inc=1, device_id=device, device_id_type=MESH)
    pl.semaphore_wait(barrier, len(devices))


def gather_kernel(
    q, g, k, v, n_ref, qx, gx, kv, nt_out, turned,
    loc_sem, swap_send, swap_recv, x_send, x_recv, y_send, y_recv, n_sem, n_send, n_recv,
):
    x, yh, core, _, _ = here()
    other = 1 - core
    partner = at_seq(x, yh, other)
    across = at_seq(x, 1 - yh, core)
    greet(
        [partner, across]
        + [at_seq(x + step, yh, c) for step in (1, -1, 2) for c in range(2)]
    )

    def head_cols(ref, head, width):
        return ref.at[:, pl.ds(pl.multiple_of(head * width, width), width)]

    local = [
        pltpu.make_async_copy(head_cols(k, core, HD), kv.at[8 + core, 0], loc_sem.at[0]),
        pltpu.make_async_copy(head_cols(v, core, HD), kv.at[8 + core, 1], loc_sem.at[1]),
        pltpu.make_async_copy(head_cols(q, core, 2 * HD), qx.at[core], loc_sem.at[2]),
        pltpu.make_async_copy(head_cols(g, core, 2 * HD), gx.at[core], loc_sem.at[3]),
    ]
    pairs = [
        (head_cols(k, other, HD), kv.at[8 + core, 0]),
        (head_cols(v, other, HD), kv.at[8 + core, 1]),
        (head_cols(q, other, 2 * HD), qx.at[core]),
        (head_cols(g, other, 2 * HD), gx.at[core]),
    ]
    swaps = [
        remote(src, dst, swap_send.at[i], swap_recv.at[i], partner)
        for i, (src, dst) in enumerate(pairs)
    ]
    for copy in local + swaps:
        copy.start()
    along = []
    for step in (1, 2):
        hops = []
        for kind, ref in enumerate((k, v)):
            for head in range(2):
                hops.append(
                    remote(
                        ref.at[:, head * HD : (head + 1) * HD],
                        kv.at[8 - 4 * step + core, kind],
                        x_send.at[step - 1, kind, head],
                        x_recv.at[step - 1, kind, core],
                        at_seq(x + step, yh, head),
                    )
                )
        along.append(hops)
        for copy in hops:
            copy.start()

    def arrived(step):
        for kind in range(2):
            for c in range(2):
                dst = kv.at[8 - 4 * step + c, kind]
                remote(dst, dst, x_send.at[step - 1, kind, c], x_recv.at[step - 1, kind, c], partner).wait_recv()

    def turn(i, carry):
        cols = pl.ds(pl.multiple_of(i * HD, HD), HD)
        turned[cols, :] = n_ref[:, cols].T
        return carry

    first_src = jnp.where(yh == 0, 8, 4)
    second_src = jnp.where(yh == 0, 4, 0)
    first = remote(kv.at[pl.ds(first_src, 2)], kv.at[pl.ds(6, 2)], y_send.at[0], y_recv.at[0], across)
    second = remote(kv.at[pl.ds(second_src, 2)], kv.at[pl.ds(2, 2)], y_send.at[1], y_recv.at[1], across)

    for copy in local:
        copy.wait()
    for copy in swaps:
        copy.wait_recv()

    @pl.when(yh == 0)
    def _():
        first.start()

    lax.fori_loop(0, D // HD, turn, 0)
    n_local = pltpu.make_async_copy(turned, nt_out.at[core], n_sem)
    n_swap = remote(turned, nt_out.at[core], n_send, n_recv, partner)
    n_local.start()
    n_swap.start()
    arrived(1)

    @pl.when(yh == 0)
    def _():
        second.start()

    @pl.when(yh == 1)
    def _():
        first.start()

    arrived(2)

    @pl.when(yh == 1)
    def _():
        second.start()

    n_local.wait()
    n_swap.wait()
    first.wait()
    second.wait()
    for copy in swaps + along[0] + along[1]:
        copy.wait_send()


def gather(queries, keys, values, grads, normed):
    any_space = pl.BlockSpec(memory_space=pl.ANY)
    dma = pltpu.SemaphoreType.DMA
    return pl.pallas_call(
        gather_kernel,
        out_shape=(
            jax.ShapeDtypeStruct((2, TOK, 2 * HD), BF),
            jax.ShapeDtypeStruct((2, TOK, 2 * HD), BF),
            jax.ShapeDtypeStruct((NB, 2, TOK, HD), BF),
            jax.ShapeDtypeStruct((2, D, TOK), BF),
        ),
        in_specs=[any_space] * 4 + [pl.BlockSpec(memory_space=pltpu.VMEM)],
        out_specs=(any_space,) * 4,
        scratch_shapes=[
            pltpu.VMEM((D, TOK), BF),
            dma((4,)), dma((4,)), dma((4,)), dma((2, 2, 2)), dma((2, 2, 2)),
            dma((2,)), dma((2,)), dma, dma, dma,
        ],
        compiler_params=pltpu.CompilerParams(
            collective_id=0, has_side_effects=True, vmem_limit_bytes=40 << 20
        ),
        name="gather",
    )(queries, grads, keys, values, normed)


def attend_kernel(
    valid, base, q, g, kv, cos, sin, dq_out, dkv_out, own_out,
    e_s, w_s, kt_s, vt_s, o_acc, dq_acc, dk_acc, dv_acc,
):
    first_shard = base[0]
    dk_acc[...] = jnp.zeros_like(dk_acc)
    dv_acc[...] = jnp.zeros_like(dv_acc)
    vt_s[:, HD:, :] = jnp.ones((2 * NB, 16, TILE), BF)

    def turn(b, carry):
        for kt in range(2):
            rows = slice(kt * TILE, (kt + 1) * TILE)
            kt_s[2 * b + kt] = kv[b, 0, rows, :].T
            vt_s[2 * b + kt, :HD, :] = kv[b, 1, rows, :].T
        return carry

    lax.fori_loop(0, NB, turn, 0)
    key_iota = lax.broadcasted_iota(jnp.int32, (TILE, 2 * TILE), 0)
    query_iota = lax.rem(lax.broadcasted_iota(jnp.int32, (TILE, 2 * TILE), 1), TILE)

    def query_tile(i, carry):
        r, qt = i // 2, lax.rem(i, 2)
        q_valid = valid[jnp.maximum(first_shard + 8 + r, 0)]
        q_rows = pl.ds(pl.multiple_of(qt * TILE, TILE), TILE)
        lanes = q_rows

        def info(t):
            j, kt = t // 2, lax.rem(t, 2)
            b = r + j
            shard = first_shard + b
            k_valid = valid[jnp.maximum(shard, 0)]
            active = (
                (shard >= 0)
                & (kt * TILE < k_valid)
                & jnp.logical_not((j == 8) & (kt > qt))
                & jnp.logical_not((j == 0) & (kt < qt))
            )
            edge = (((j == 8) | (j == 0)) & (kt == qt)) | ((kt + 1) * TILE > k_valid)
            return j, kt, b, k_valid, active, edge

        @pl.when(qt * TILE >= q_valid)
        def _():
            dq_out[r, :, lanes] = jnp.zeros((2 * HD, TILE), BF)

        @pl.when(qt * TILE < q_valid)
        def _():
            q_two = q[r, q_rows, :]
            g_two = g[r, q_rows, :]
            q_rows2 = jnp.concatenate([q_two[:, :HD], q_two[:, HD:]], axis=0)
            o_acc[...] = jnp.zeros_like(o_acc)

            def forward(t, carry):
                j, kt, b, k_valid, active, edge = info(t)
                rows = pl.ds(pl.multiple_of(kt * TILE, TILE), TILE)
                slot = pl.ds(pl.multiple_of(t * TILE, TILE), TILE)

                def tile(masked):
                    s = nt(kv[b, 0, rows, :], q_rows2)
                    th = jnp.tanh(s * (SCALE / SOFT_CAP))
                    e = jnp.exp2(th * (SOFT_CAP * LOG2E))
                    if masked:
                        gap = (query_iota + qt * TILE) - (key_iota + kt * TILE) + (8 - j) * TOK
                        allowed = (
                            (gap >= 0)
                            & (gap < WINDOW)
                            & ((key_iota + kt * TILE < k_valid) | (gap == 0))
                        )
                        e = jnp.where(allowed, e, 0.0)
                    eb = e.astype(BF)
                    e_s[slot, :] = eb
                    w_s[slot, :] = (e * (1.0 - th * th)).astype(BF)
                    o_acc[...] += nn(vt_s[2 * b + kt], eb)

                @pl.when(active & jnp.logical_not(edge))
                def _():
                    tile(False)

                @pl.when(active & edge)
                def _():
                    tile(True)

                return carry

            lax.fori_loop(0, 18, forward, 0)
            inv = 1.0 / o_acc[HD : HD + 1, :]
            g_rows2 = jnp.concatenate([g_two[:, :HD], g_two[:, HD:]], axis=0).astype(F32)
            live = query_iota[:1, :] + qt * TILE < q_valid
            g_t = jnp.where(live, g_rows2.T, 0.0) * inv
            delta = jnp.sum(g_t * o_acc[:HD, :], axis=0, keepdims=True) * inv
            gs_t = g_t.astype(BF)
            gs = g_t.T.astype(BF)
            dq_acc[...] = jnp.zeros_like(dq_acc)

            def backward(t, carry):
                j, kt, b, k_valid, active, edge = info(t)
                rows = pl.ds(pl.multiple_of(kt * TILE, TILE), TILE)
                slot = pl.ds(pl.multiple_of(t * TILE, TILE), TILE)

                @pl.when(active)
                def _():
                    dp = nn(kv[b, 1, rows, :], gs_t)
                    ds = (w_s[slot, :].astype(F32) * (dp - delta)).astype(BF)
                    dq_acc[...] += nn(kt_s[2 * b + kt], ds)
                    dk_acc[b, rows, :] += nn(ds, q_rows2)
                    dv_acc[b, rows, :] += nn(e_s[slot, :], gs)

                return carry

            lax.fori_loop(0, 18, backward, 0)
            dq = dq_acc[...] * SCALE
            c, s = cos[r, :, lanes], sin[r, :, lanes]
            for head in range(2):
                a = dq[: HD // 2, head * TILE : (head + 1) * TILE]
                z = dq[HD // 2 :, head * TILE : (head + 1) * TILE]
                dq_out[r, head * HD : head * HD + HD // 2, lanes] = (a * c + z * s).astype(BF)
                dq_out[r, head * HD + HD // 2 : (head + 1) * HD, lanes] = (z * c - a * s).astype(BF)

        return carry

    lax.fori_loop(0, 4, query_tile, 0)

    def give(b, carry):
        dkv_out[b, 0] = (dk_acc[b] * SCALE).astype(BF)
        dkv_out[b, 1] = dv_acc[b].astype(BF)
        return carry

    lax.fori_loop(0, 8, give, 0)
    for r in range(2):
        own_out[r, 0] = dk_acc[8 + r] * SCALE
        own_out[r, 1] = dv_acc[8 + r]


def attend(valid_len, base, qx, gx, kv, cos, sin):
    vmem = pl.BlockSpec(memory_space=pltpu.VMEM)
    smem = pl.BlockSpec(memory_space=pltpu.SMEM)
    return pl.pallas_call(
        attend_kernel,
        out_shape=(
            jax.ShapeDtypeStruct((2, 2 * HD, TOK), BF),
            jax.ShapeDtypeStruct((8, 2, TOK, HD), BF),
            jax.ShapeDtypeStruct((2, 2, TOK, HD), F32),
        ),
        in_specs=[smem, smem] + [vmem] * 5,
        out_specs=(vmem,) * 3,
        scratch_shapes=[
            pltpu.VMEM((18 * TILE, 2 * TILE), BF),
            pltpu.VMEM((18 * TILE, 2 * TILE), BF),
            pltpu.VMEM((2 * NB, HD, TILE), BF),
            pltpu.VMEM((2 * NB, HD + 16, TILE), BF),
            pltpu.VMEM((HD + 16, 2 * TILE), F32),
            pltpu.VMEM((HD, 2 * TILE), F32),
            pltpu.VMEM((NB, TOK, HD), F32),
            pltpu.VMEM((NB, TOK, HD), F32),
        ],
        compiler_params=pltpu.CompilerParams(vmem_limit_bytes=50 << 20),
        name="attend",
    )(valid_len, base, qx, gx, kv, cos, sin)


def finish_kernel(
    dq, dkv, own, turned_hbm, wq, wk, wv, cos, sin, gx_out, gq_out, gk_out, gv_out,
    n_buf, w_buf, t_buf, d_buf, y_buf, x_buf, near, far,
    xs, xr, zs, zr, xy, zy, half_buf, half_recv,
    load_sem, dq_sems, dk_sems, y_sems, x_sems, ring_send, ring_recv, pair_sems, core_sems,
):
    x, yh, core, z, yl = here()
    other = 1 - core
    partner = at_seq(x, yh, other)
    across = at_seq(x, 1 - yh, core)
    beside = at_head(z, 1 - yl)
    x_next, x_prev, x_far = at_seq(x + 1, yh, core), at_seq(x - 1, yh, core), at_seq(x + 2, yh, core)
    z_next, z_prev = at_head(z + 1, yl), at_head(z - 1, yl)
    greet([partner, across, beside, x_next, x_prev, x_far, z_next, z_prev])

    y_copies = [
        remote(dkv.at[pl.ds(6 - 4 * i, 2)], y_buf.at[i], y_sems.at[0, i], y_sems.at[1, i], across)
        for i in range(2)
    ]
    for copy in y_copies:
        copy.start()
    loads = [
        pltpu.make_async_copy(dkv.at[pl.ds(4, 2)], near, load_sem.at[0]),
        pltpu.make_async_copy(dkv.at[pl.ds(0, 2)], far, load_sem.at[1]),
        pltpu.make_async_copy(turned_hbm, n_buf, load_sem.at[2]),
        pltpu.make_async_copy(wq, w_buf.at[:, : 4 * HD], load_sem.at[3]),
        pltpu.make_async_copy(wk, w_buf.at[:, 4 * HD : 6 * HD], load_sem.at[4]),
        pltpu.make_async_copy(wv, w_buf.at[:, 6 * HD :], load_sem.at[5]),
    ]
    for copy in loads:
        copy.start()
    head_rows = pl.ds(pl.multiple_of(core * 2 * HD, 2 * HD), 2 * HD)
    dq_swap = remote(dq.at[other], d_buf.at[head_rows], dq_sems.at[0], dq_sems.at[1], partner)
    dq_swap.start()
    d_buf[head_rows, :] = dq[core]
    for r in range(2):
        t_buf[r, : 2 * HD, :] = dq[r]
    loads[0].wait()
    loads[1].wait()
    back_near = remote(near, x_buf.at[0], x_sems.at[0, 0], x_sems.at[1, 0], x_prev)
    back_far = remote(far, x_buf.at[1], x_sems.at[0, 1], x_sems.at[1, 1], x_far)

    def add_to(ref, index):
        ref[...] = (ref[...].astype(F32) + y_buf[index].astype(F32)).astype(BF)

    @pl.when(yh == 0)
    def _():
        back_far.start()

    y_copies[0].wait()

    @pl.when(yh == 1)
    def _():
        add_to(near, 0)
        back_near.start()

    y_copies[1].wait()

    @pl.when(yh == 0)
    def _():
        add_to(near, 1)
        back_near.start()

    @pl.when(yh == 1)
    def _():
        add_to(far, 1)
        back_far.start()

    keep = (yh == 0).astype(F32)
    back_near.wait()
    back_far.wait()
    for r in range(2):
        for kind in range(2):
            total = (
                own[r, kind]
                + y_buf[0, r, kind].astype(F32) * keep
                + x_buf[0, r, kind].astype(F32)
                + x_buf[1, r, kind].astype(F32)
            ).T
            if kind == 0:
                a, b = total[: HD // 2, :], total[HD // 2 :, :]
                c, s = cos[r], sin[r]
                total = jnp.concatenate([a * c + b * s, b * c - a * s], axis=0)
            t_buf[r, (2 + kind) * HD : (3 + kind) * HD, :] = total.astype(BF)
    dk_swaps = []
    for kind in range(2):
        rows = pl.ds(pl.multiple_of((4 + 2 * kind) * HD + core * HD, HD), HD)
        mine = pl.ds((2 + kind) * HD, HD)
        copy = remote(
            t_buf.at[other, mine], d_buf.at[rows], dk_sems.at[0, kind], dk_sems.at[1, kind], partner
        )
        copy.start()
        dk_swaps.append(copy)
        d_buf[rows, :] = t_buf[core, mine, :]

    for copy in loads[2:]:
        copy.wait()

    def weight_rows(place, half):
        rows = pl.ds(pl.multiple_of(place * CHUNK + half * HALF, QTR), HALF)
        return nt(n_buf[0, rows, :], t_buf[0]) + nt(n_buf[1, rows, :], t_buf[1])

    def input_rows(place, half):
        rows = pl.ds(pl.multiple_of(place * CHUNK + half * HALF, QTR), HALF)
        return nn(w_buf[rows, :], d_buf[...])

    send, recv = (xs, zs), (xr, zr)
    ahead, behind = (x_next, z_next), (x_prev, z_prev)
    place = (x, z)
    terms = (weight_rows, input_rows)

    def compute(axis, slot, step):
        where = lax.rem(place[axis] + step, 4)

        def one(half, carry):
            rows = pl.ds(pl.multiple_of(half * HALF, HALF), HALF)
            send[axis][slot, rows, :] = terms[axis](where, half).astype(BF)
            return carry

        lax.fori_loop(0, 2, one, 0)

    def halves(axis):
        top, low = pl.ds(0, HALF), pl.ds(HALF, HALF)
        return (
            remote(send[axis].at[0, top], recv[axis].at[0, top], ring_send.at[axis, 0], ring_recv.at[axis, 0], ahead[axis]),
            remote(send[axis].at[0, low], recv[axis].at[0, low], ring_send.at[axis, 1], ring_recv.at[axis, 1], behind[axis]),
        )

    def wholes(axis):
        return (
            remote(send[axis].at[1], recv[axis].at[1], ring_send.at[axis, 2], ring_recv.at[axis, 2], ahead[axis]),
            remote(send[axis].at[2], recv[axis].at[2], ring_send.at[axis, 3], ring_recv.at[axis, 3], behind[axis]),
        )

    half_copies = [None, None]
    whole_copies = [None, None]
    for axis in range(2):
        if axis == 1:
            dq_swap.wait()
            for copy in dk_swaps:
                copy.wait()
        compute(axis, 0, 2)
        half_copies[axis] = halves(axis)
        for copy in half_copies[axis]:
            copy.start()
    for axis in range(2):
        compute(axis, 1, 1)
        compute(axis, 2, 3)
    for axis in range(2):
        whole_copies[axis] = wholes(axis)
        half_copies[axis][0].wait()
        top = slice(0, HALF)
        send[axis][1, top, :] = (send[axis][1, top, :].astype(F32) + recv[axis][0, top, :].astype(F32)).astype(BF)
        whole_copies[axis][0].start()
        half_copies[axis][1].wait()
        low = slice(HALF, CHUNK)
        send[axis][2, low, :] = (send[axis][2, low, :].astype(F32) + recv[axis][0, low, :].astype(F32)).astype(BF)
        whole_copies[axis][1].start()
    side = (yh, yl)
    side_device = (across, beside)
    pair_buf = (xy, zy)
    for axis in range(2):
        compute(axis, 3, 0)
    pair_copies = []
    for axis in range(2):
        for copy in whole_copies[axis]:
            copy.wait()

        def summed(half):
            rows = pl.ds(pl.multiple_of(half * HALF, HALF), HALF)
            return (
                send[axis][3, rows, :].astype(F32)
                + recv[axis][1, rows, :].astype(F32)
                + recv[axis][2, rows, :].astype(F32)
            )

        pair_buf[axis][0] = summed(1 - side[axis]).astype(BF)
        copy = remote(pair_buf[axis].at[0], pair_buf[axis].at[1], pair_sems.at[0, axis], pair_sems.at[1, axis], side_device[axis])
        copy.start()
        pair_copies.append(copy)
        pair_buf[axis][2] = summed(side[axis]).astype(BF)
    pair_copies[0].wait()
    half_buf[...] = (xy[1].astype(F32) + xy[2].astype(F32)).astype(BF)
    my_rows = pl.ds(pl.multiple_of(core * QTR, QTR), QTR)
    its_rows = pl.ds(pl.multiple_of(other * QTR, QTR), QTR)
    last = remote(half_buf.at[its_rows], half_recv, core_sems.at[0], core_sems.at[1], partner)
    last.start()
    pair_copies[1].wait()
    gx_out[...] = (zy[1].astype(F32) + zy[2].astype(F32)).T.astype(BF)
    last.wait()
    for block, head in ((half_buf[my_rows, :], core), (half_recv[...], other)):
        gq_out[:, pl.ds(pl.multiple_of(head * 2 * HD, 2 * HD), 2 * HD)] = block[:, : 2 * HD]
        gk_out[:, pl.ds(pl.multiple_of(head * HD, HD), HD)] = block[:, 2 * HD : 3 * HD]
        gv_out[:, pl.ds(pl.multiple_of(head * HD, HD), HD)] = block[:, 3 * HD :]


def finish(dq, dkv, own, turned, wq, wk, wv, cos, sin):
    vmem = pl.BlockSpec(memory_space=pltpu.VMEM)
    any_space = pl.BlockSpec(memory_space=pl.ANY)
    dma = pltpu.SemaphoreType.DMA
    return pl.pallas_call(
        finish_kernel,
        out_shape=(
            jax.ShapeDtypeStruct((TOK, HALF), BF),
            jax.ShapeDtypeStruct((QTR, 4 * HD), BF),
            jax.ShapeDtypeStruct((QTR, 2 * HD), BF),
            jax.ShapeDtypeStruct((QTR, 2 * HD), BF),
        ),
        in_specs=[vmem, any_space, vmem, any_space, any_space, any_space, any_space, vmem, vmem],
        out_specs=(vmem,) * 4,
        scratch_shapes=[
            pltpu.VMEM((2, D, TOK), BF),
            pltpu.VMEM((D, 8 * HD), BF),
            pltpu.VMEM((2, 4 * HD, TOK), BF),
            pltpu.VMEM((8 * HD, TOK), BF),
            pltpu.VMEM((2, 2, 2, TOK, HD), BF),
            pltpu.VMEM((2, 2, 2, TOK, HD), BF),
            pltpu.VMEM((2, 2, TOK, HD), BF),
            pltpu.VMEM((2, 2, TOK, HD), BF),
            pltpu.VMEM((4, CHUNK, TOK), BF),
            pltpu.VMEM((3, CHUNK, TOK), BF),
            pltpu.VMEM((4, CHUNK, TOK), BF),
            pltpu.VMEM((3, CHUNK, TOK), BF),
            pltpu.VMEM((3, HALF, TOK), BF),
            pltpu.VMEM((3, HALF, TOK), BF),
            pltpu.VMEM((HALF, TOK), BF),
            pltpu.VMEM((QTR, TOK), BF),
            dma((6,)), dma((2,)), dma((2, 2)), dma((2, 2)), dma((2, 2)),
            dma((2, 4)), dma((2, 4)), dma((2, 2)), dma((2,)),
        ],
        compiler_params=pltpu.CompilerParams(
            collective_id=1, has_side_effects=True, vmem_limit_bytes=58 << 20
        ),
        name="finish",
    )(dq, dkv, own, turned, wq, wk, wv, cos, sin)


def body(queries, keys, values, out_grad, normed, w_query, w_key, w_value, valid_len):
    chip = lax.axis_index("seq") // 2
    inverse_freq = ROPE_BASE ** (-(jnp.arange(HD // 2, dtype=F32) * (2.0 / HD)))
    slots = (chip * 2 * TOK + jnp.arange(2 * TOK, dtype=jnp.int32)).astype(F32).reshape(2, 1, TOK)
    angles = slots * inverse_freq[None, :, None]
    cos, sin = jnp.cos(angles), jnp.sin(angles)
    base = (2 * chip - 8).astype(jnp.int32).reshape(1)
    qx, gx, kv, turned = gather(queries, keys, values, out_grad, normed)
    dq, dkv, own = attend(valid_len, base, qx, gx, kv, cos, sin)
    return finish(dq, dkv, own, turned, w_query, w_key, w_value, cos, sin)


def solution(mesh):
    both = P("seq", "head")
    placed = (both, both, both, both, P("seq", None), P(None, "head"), P(None, "head"), P(None, "head"), P())
    return jax.shard_map(
        body, mesh=mesh, in_specs=placed, out_specs=(both,) * 4, check_vma=False
    )
```

```python
import functools

import jax
import jax.numpy as jnp
from jax import lax
from jax.experimental import pallas as pl
from jax.experimental.pallas import tpu as pltpu
from jax.sharding import PartitionSpec as P

D = 4608
H = 32
HD = 128
WINDOW = 4096
SOFT_CAP = 50.0
ROPE_BASE = 10000.0
SCALE = (D // H) ** (-0.5)

TOK = 512
NB = 10
TILE = 256
CHUNK = D // 4
HALF = CHUNK // 2
QTR = HALF // 2

BF = jnp.bfloat16
F32 = jnp.float32
MESH = pl.DeviceIdType.MESH
LOG2E = 1.4426950408889634


def nt(left, right):
    return lax.dot_general(left, right, (((1,), (1,)), ((), ())), preferred_element_type=F32)


def nn(left, right):
    return lax.dot_general(left, right, (((1,), (0,)), ((), ())), preferred_element_type=F32)


def here():
    s, h = lax.axis_index("seq"), lax.axis_index("head")
    return s // 4, (s // 2) % 2, s % 2, h // 2, h % 2


def at_seq(x, yh, core):
    return {"seq": (lax.rem(x + 4, 4) * 2 + yh) * 2 + core, "head": lax.axis_index("head")}


def at_head(z, yl):
    return {"seq": lax.axis_index("seq"), "head": lax.rem(z + 4, 4) * 2 + yl}


def remote(src, dst, send, recv, device):
    return pltpu.make_async_remote_copy(
        src_ref=src, dst_ref=dst, send_sem=send, recv_sem=recv, device_id=device, device_id_type=MESH
    )


def greet(devices):
    barrier = pltpu.get_barrier_semaphore()
    for device in devices:
        pl.semaphore_signal(barrier, inc=1, device_id=device, device_id_type=MESH)
    pl.semaphore_wait(barrier, len(devices))


def gather_kernel(
    q, g, k, v, n_hbm, qx, gx, kv, nt_out, n_ref, turned,
    n_load_sem, loc_sem, swap_send, swap_recv, x_send, x_recv, y_send, y_recv, n_sem, n_send, n_recv,
):
    x, yh, core, _, _ = here()
    other = 1 - core
    partner = at_seq(x, yh, other)
    across = at_seq(x, 1 - yh, core)
    greet(
        [partner, across]
        + [at_seq(x + step, yh, c) for step in (1, -1, 2) for c in range(2)]
    )

    def head_cols(ref, head, width):
        return ref.at[:, pl.ds(pl.multiple_of(head * width, width), width)]

    local = [
        pltpu.make_async_copy(head_cols(k, core, HD), kv.at[8 + core, 0], loc_sem.at[0]),
        pltpu.make_async_copy(head_cols(v, core, HD), kv.at[8 + core, 1], loc_sem.at[1]),
        pltpu.make_async_copy(head_cols(q, core, 2 * HD), qx.at[core], loc_sem.at[2]),
        pltpu.make_async_copy(head_cols(g, core, 2 * HD), gx.at[core], loc_sem.at[3]),
    ]
    pairs = [
        (head_cols(k, other, HD), kv.at[8 + core, 0]),
        (head_cols(v, other, HD), kv.at[8 + core, 1]),
        (head_cols(q, other, 2 * HD), qx.at[core]),
        (head_cols(g, other, 2 * HD), gx.at[core]),
    ]
    swaps = [
        remote(src, dst, swap_send.at[i], swap_recv.at[i], partner)
        for i, (src, dst) in enumerate(pairs)
    ]
    for copy in local + swaps:
        copy.start()
    along = []
    for step in (1, 2):
        hops = []
        for kind, ref in enumerate((k, v)):
            for head in range(2):
                hops.append(
                    remote(
                        ref.at[:, head * HD : (head + 1) * HD],
                        kv.at[8 - 4 * step + core, kind],
                        x_send.at[step - 1, kind, head],
                        x_recv.at[step - 1, kind, core],
                        at_seq(x + step, yh, head),
                    )
                )
        along.append(hops)
    for copy in along[0]:
        copy.start()
    n_load = pltpu.make_async_copy(n_hbm, n_ref, n_load_sem)
    n_load.start()

    def arrived(step, c):
        for kind in range(2):
            dst = kv.at[8 - 4 * step + c, kind]
            remote(dst, dst, x_send.at[step - 1, kind, c], x_recv.at[step - 1, kind, c], partner).wait_recv()

    def turn(i, carry):
        cols = pl.ds(pl.multiple_of(i * HD, HD), HD)
        turned[cols, :] = n_ref[:, cols].T
        return carry

    first_src = jnp.where(yh == 0, 8, 4)
    second_src = jnp.where(yh == 0, 4, 0)
    first = [
        remote(kv.at[first_src + c], kv.at[6 + c], y_send.at[0, c], y_recv.at[0, c], across)
        for c in range(2)
    ]
    second = [
        remote(kv.at[second_src + c], kv.at[2 + c], y_send.at[1, c], y_recv.at[1, c], across)
        for c in range(2)
    ]
    for copy in local:
        copy.wait()
    for copy in swaps:
        copy.wait_recv()

    @pl.when(yh == 0)
    def _():
        for copy in first:
            copy.start()

    n_load.wait()
    lax.fori_loop(0, D // HD, turn, 0)
    n_local = pltpu.make_async_copy(turned, nt_out.at[core], n_sem)
    n_swap = remote(turned, nt_out.at[core], n_send, n_recv, partner)
    for c in range(2):
        arrived(1, c)

        @pl.when(yh == 0)
        def _():
            second[c].start()

        @pl.when(yh == 1)
        def _():
            first[c].start()

    for copy in along[1]:
        copy.start()
    n_local.start()
    n_swap.start()
    for c in range(2):
        arrived(2, c)

        @pl.when(yh == 1)
        def _():
            second[c].start()

    n_local.wait()
    n_swap.wait()
    for copy in first + second:
        copy.wait()
    for copy in swaps + along[0] + along[1]:
        copy.wait_send()


def gather(queries, keys, values, grads, normed):
    hbm = pl.BlockSpec(memory_space=pltpu.HBM)
    dma = pltpu.SemaphoreType.DMA
    return pl.pallas_call(
        gather_kernel,
        out_shape=(
            jax.ShapeDtypeStruct((2, TOK, 2 * HD), BF),
            jax.ShapeDtypeStruct((2, TOK, 2 * HD), BF),
            jax.ShapeDtypeStruct((NB, 2, TOK, HD), BF),
            jax.ShapeDtypeStruct((2, D, TOK), BF),
        ),
        in_specs=[hbm] * 5,
        out_specs=(hbm,) * 4,
        scratch_shapes=[
            pltpu.VMEM((TOK, D), BF), pltpu.VMEM((D, TOK), BF),
            dma, dma((4,)), dma((4,)), dma((4,)), dma((2, 2, 2)), dma((2, 2, 2)),
            dma((2, 2)), dma((2, 2)), dma, dma, dma,
        ],
        compiler_params=pltpu.CompilerParams(
            collective_id=0, has_side_effects=True, vmem_limit_bytes=60 << 20
        ),
        name="gather",
    )(queries, grads, keys, values, normed)


STEP = 8
PIECES = 4 * NB
EMPTY = PIECES
OWN = PIECES + STEP


def attend_kernel(
    valid, base, q, g, kv_hbm, cos, sin, dq_out, dkv_out, own_out,
    kv, e_s, w_s, kt_s, vt_s, o_acc, dq_acc, dk_acc, dv_acc, listed, sem,
):
    first_shard = base[0]
    load = pltpu.make_async_copy(kv_hbm, kv.at[pl.ds(0, NB)], sem)
    load.start()
    dk_acc[...] = jnp.zeros_like(dk_acc)
    dv_acc[...] = jnp.zeros_like(dv_acc)
    for k in range(STEP):
        kv[NB + k // 4, 0, k % 4] = jnp.zeros((HD, HD), BF)
        kv[NB + k // 4, 1, k % 4] = jnp.zeros((HD, HD), BF)
        kt_s[EMPTY + k] = jnp.zeros((HD, HD), BF)
        vt_s[EMPTY + k] = jnp.zeros((HD + 16, HD), BF)
    load.wait()

    def valid_of(b):
        return valid[jnp.maximum(first_shard + b, 0)]

    def turn(b, carry):
        for k in range(4):
            live = lax.broadcasted_iota(jnp.int32, (HD + 16, HD), 1) + k * HD < valid_of(b)
            k_t = kv[b, 0, k].T
            v_t = jnp.concatenate([kv[b, 1, k].T, jnp.ones((16, HD), BF)], axis=0)
            kt_s[4 * b + k] = jnp.where(live[:HD], k_t.astype(F32), 0.0).astype(BF)
            vt_s[4 * b + k] = jnp.where(live, v_t.astype(F32), 0.0).astype(BF)

            @pl.when(b >= 8)
            def _():
                kt_s[OWN + 4 * (b - 8) + k] = k_t
                vt_s[OWN + 4 * (b - 8) + k] = v_t

        return carry

    lax.fori_loop(0, NB, turn, 0)
    key_iota = lax.broadcasted_iota(jnp.int32, (TILE, 2 * TILE), 0)
    query_iota = lax.rem(lax.broadcasted_iota(jnp.int32, (TILE, 2 * TILE), 1), TILE)

    def query_tile(i, carry):
        r, qt = i // 2, lax.rem(i, 2)
        q_valid = valid_of(8 + r)
        q_rows = pl.ds(pl.multiple_of(qt * TILE, TILE), TILE)
        lanes = q_rows

        @pl.when(qt * TILE >= q_valid)
        def _():
            dq_out[r, :, lanes] = jnp.zeros((2 * HD, TILE), BF)

        @pl.when(qt * TILE < q_valid)
        def _():
            def note(t, count):
                j, k = t // 4, lax.rem(t, 4)
                b = r + j
                wanted = (
                    (first_shard + b >= 0)
                    & (k * HD < valid_of(b))
                    & jnp.logical_not((j == 0) & (k < 2 * qt + 2))
                    & jnp.logical_not((j == 8) & (k >= 2 * qt))
                )
                listed[count] = jnp.where(wanted, 4 * b + k, EMPTY)
                return count + wanted.astype(jnp.int32)

            count = lax.fori_loop(0, 36, note, 0)
            for extra in range(STEP - 1):
                listed[count + extra] = EMPTY + extra
            steps = (count + STEP - 1) // STEP
            doubles = steps // 2

            q_two = q[r, q_rows, :]
            g_two = g[r, q_rows, :]
            q_rows2 = jnp.concatenate([q_two[:, :HD], q_two[:, HD:]], axis=0)
            q_t = q_rows2.T

            def keys_of(kind, pieces):
                return jnp.concatenate([kv[p // 4, kind, lax.rem(p, 4)] for p in pieces], axis=0)

            def turned_of(ref, pieces):
                return jnp.concatenate([ref[p] for p in pieces], axis=1)

            def forward(pieces, turned, slot, mask):
                parts = []
                for n in range(0, len(pieces), 2):
                    keys = keys_of(0, pieces[n : n + 2])
                    rows = pl.ds(pl.multiple_of(slot + n * HD, TILE), TILE)
                    heads = []
                    for head in range(2):
                        cols = slice(head * TILE, (head + 1) * TILE)
                        th = jnp.tanh(nn(keys, q_t[:, cols]) * (SCALE / SOFT_CAP))
                        e = jnp.exp2(th * (SOFT_CAP * LOG2E))
                        if mask is not None:
                            e = jnp.where(mask[n // 2][:, cols], e, 0.0)
                        eb = e.astype(BF)
                        e_s[rows, cols] = eb
                        w_s[rows, cols] = (e * (1.0 - th * th)).astype(BF)
                        heads.append(eb)
                    parts.append(heads)
                for head in range(2):
                    cols = slice(head * TILE, (head + 1) * TILE)
                    column = jnp.concatenate([p[head] for p in parts], axis=0)
                    o_acc[:, cols] += nn(turned_of(vt_s, turned), column)

            gap = query_iota - key_iota
            key_pos = key_iota + qt * TILE
            oldest_there = first_shard + r >= 0
            edge_mask = (
                gap + 8 * TOK < WINDOW,
                (gap >= 0) & ((key_pos < q_valid) | (gap == 0)),
            )
            old = jnp.where(oldest_there, 4 * r + 2 * qt, EMPTY)
            own = 4 * (8 + r) + 2 * qt
            edge = (old, old + 1, own, own + 1)
            edge_turned = (old, old + 1, OWN + 4 * r + 2 * qt, OWN + 4 * r + 2 * qt + 1)
            o_acc[...] = jnp.zeros_like(o_acc)
            forward(edge, edge_turned, 0, edge_mask)

            def forward_step(width, n, carry):
                pieces = tuple(listed[n * width + m] for m in range(width))
                forward(pieces, pieces, (4 + n * width) * HD, None)
                return carry

            lax.fori_loop(0, doubles, functools.partial(forward_step, 2 * STEP), 0)
            lax.fori_loop(2 * doubles, steps, functools.partial(forward_step, STEP), 0)
            inv = 1.0 / o_acc[HD : HD + 1, :]
            g_rows2 = jnp.concatenate([g_two[:, :HD], g_two[:, HD:]], axis=0).astype(F32)
            live = query_iota[:1, :] + qt * TILE < q_valid
            g_t = jnp.where(live, g_rows2.T, 0.0) * inv
            delta = jnp.sum(g_t * o_acc[:HD, :], axis=0, keepdims=True) * inv
            gs_t = g_t.astype(BF)
            gs = g_t.T.astype(BF)
            dq_acc[...] = jnp.zeros_like(dq_acc)

            def backward(pieces, turned, slot):
                rows = pl.ds(pl.multiple_of(slot, TILE), len(pieces) * HD)
                columns = []
                for head in range(2):
                    cols = slice(head * TILE, (head + 1) * TILE)
                    parts = []
                    for n in range(0, len(pieces), 2):
                        part = pl.ds(pl.multiple_of(slot + n * HD, TILE), TILE)
                        dp = nn(keys_of(1, pieces[n : n + 2]), gs_t[:, cols])
                        parts.append((w_s[part, cols].astype(F32) * (dp - delta[:, cols])).astype(BF))
                    columns.append(jnp.concatenate(parts, axis=0))
                ds = jnp.concatenate(columns, axis=1)
                dq_acc[...] += nn(turned_of(kt_s, turned), ds)
                dk = nn(ds, q_rows2)
                dv = nn(e_s[rows, :], gs)
                for n, p in enumerate(pieces):
                    dk_acc[p] += dk[n * HD : (n + 1) * HD]
                    dv_acc[p] += dv[n * HD : (n + 1) * HD]

            backward(edge, edge_turned, 0)

            def backward_step(width, n, carry):
                pieces = tuple(listed[n * width + m] for m in range(width))
                backward(pieces, pieces, (4 + n * width) * HD)
                return carry

            lax.fori_loop(0, doubles, functools.partial(backward_step, 2 * STEP), 0)
            lax.fori_loop(2 * doubles, steps, functools.partial(backward_step, STEP), 0)
            dq = dq_acc[...] * SCALE
            c, s = cos[r, :, lanes], sin[r, :, lanes]
            for head in range(2):
                a = dq[: HD // 2, head * TILE : (head + 1) * TILE]
                z = dq[HD // 2 :, head * TILE : (head + 1) * TILE]
                dq_out[r, head * HD : head * HD + HD // 2, lanes] = (a * c + z * s).astype(BF)
                dq_out[r, head * HD + HD // 2 : (head + 1) * HD, lanes] = (z * c - a * s).astype(BF)

        return carry

    lax.fori_loop(0, 4, query_tile, 0)

    def result(ref, b, k, scale):
        live = lax.broadcasted_iota(jnp.int32, (HD, HD), 0) + k * HD < valid_of(b)
        return jnp.where(live, ref[4 * b + k] * scale, 0.0)

    def give(b, carry):
        for k in range(4):
            rows = slice(k * HD, (k + 1) * HD)
            dkv_out[b, 0, rows, :] = result(dk_acc, b, k, SCALE).astype(BF)
            dkv_out[b, 1, rows, :] = result(dv_acc, b, k, 1.0).astype(BF)
        return carry

    lax.fori_loop(0, 8, give, 0)
    for r in range(2):
        for k in range(4):
            rows = slice(k * HD, (k + 1) * HD)
            own_out[r, 0, rows, :] = result(dk_acc, 8 + r, k, SCALE)
            own_out[r, 1, rows, :] = result(dv_acc, 8 + r, k, 1.0)


def attend(valid_len, base, qx, gx, kv, cos, sin):
    vmem = pl.BlockSpec(memory_space=pltpu.VMEM)
    smem = pl.BlockSpec(memory_space=pltpu.SMEM)
    return pl.pallas_call(
        attend_kernel,
        out_shape=(
            jax.ShapeDtypeStruct((2, 2 * HD, TOK), BF),
            jax.ShapeDtypeStruct((8, 2, TOK, HD), BF),
            jax.ShapeDtypeStruct((2, 2, TOK, HD), F32),
        ),
        in_specs=[smem, smem, vmem, vmem, pl.BlockSpec(memory_space=pltpu.HBM), vmem, vmem],
        out_specs=(vmem,) * 3,
        scratch_shapes=[
            pltpu.VMEM((NB + STEP // 4, 2, 4, HD, HD), BF),
            pltpu.VMEM((44 * HD, 2 * TILE), BF),
            pltpu.VMEM((44 * HD, 2 * TILE), BF),
            pltpu.VMEM((OWN + 8, HD, HD), BF),
            pltpu.VMEM((OWN + 8, HD + 16, HD), BF),
            pltpu.VMEM((HD + 16, 2 * TILE), F32),
            pltpu.VMEM((HD, 2 * TILE), F32),
            pltpu.VMEM((PIECES + STEP, HD, HD), F32),
            pltpu.VMEM((PIECES + STEP, HD, HD), F32),
            pltpu.SMEM((48,), jnp.int32),
            pltpu.SemaphoreType.DMA,
        ],
        compiler_params=pltpu.CompilerParams(vmem_limit_bytes=58 << 20),
        name="attend",
    )(valid_len, base, qx, gx, kv.reshape(NB, 2, 4, HD, HD), cos, sin)


PIECE = 256


def finish_kernel(
    dq, dkv, own_hbm, turned_hbm, wq, wk, wv, cos, sin, gx_out, gw_out,
    own, n_buf, w_buf, t_buf, d_buf, y_buf, x_buf, near, far,
    xs, xr, zs, zr, xy, zy, half_buf,
    load_sem, dq_sems, dk_sems, y_sems, x_sems, ring_send, ring_recv, pair_sems, core_sems,
):
    x, yh, core, z, yl = here()
    other = 1 - core
    partner = at_seq(x, yh, other)
    across = at_seq(x, 1 - yh, core)
    beside = at_head(z, 1 - yl)
    x_next, x_prev, x_far = at_seq(x + 1, yh, core), at_seq(x - 1, yh, core), at_seq(x + 2, yh, core)
    z_next, z_prev = at_head(z + 1, yl), at_head(z - 1, yl)
    greet([partner, across, beside, x_next, x_prev, x_far, z_next, z_prev])

    y_copies = [
        remote(dkv.at[pl.ds(6 - 4 * i, 2)], y_buf.at[i], y_sems.at[0, i], y_sems.at[1, i], across)
        for i in range(2)
    ]
    for copy in y_copies:
        copy.start()
    pairs = [
        (dkv.at[pl.ds(0, 2)], far),
        (dkv.at[pl.ds(4, 2)], near),
        (dq.at[0], t_buf.at[: 2 * HD, :TOK]),
        (dq.at[1], t_buf.at[: 2 * HD, TOK:]),
        (turned_hbm.at[0], n_buf.at[:, :TOK]),
        (turned_hbm.at[1], n_buf.at[:, TOK:]),
        (own_hbm, own),
        (wq, w_buf.at[:, : 4 * HD]),
        (wk, w_buf.at[:, 4 * HD : 6 * HD]),
        (wv, w_buf.at[:, 6 * HD :]),
    ]
    loads = [pltpu.make_async_copy(src, dst, load_sem.at[i]) for i, (src, dst) in enumerate(pairs)]
    for copy in loads:
        copy.start()
    head_rows = pl.ds(pl.multiple_of(core * 2 * HD, 2 * HD), 2 * HD)
    dq_swap = remote(dq.at[other], d_buf.at[head_rows], dq_sems.at[0], dq_sems.at[1], partner)
    dq_keep = pltpu.make_async_copy(dq.at[core], d_buf.at[head_rows], dq_sems.at[2])
    back_near = remote(near, x_buf.at[0], x_sems.at[0, 0], x_sems.at[1, 0], x_prev)
    back_far = remote(far, x_buf.at[1], x_sems.at[0, 1], x_sems.at[1, 1], x_far)
    loads[0].wait()

    @pl.when(yh == 0)
    def _():
        back_far.start()

    dq_swap.start()
    dq_keep.start()
    for copy in loads[1:6]:
        copy.wait()

    send, recv = (xs, zs), (xr, zr)
    ahead, behind = (x_next, z_next), (x_prev, z_prev)
    place = (x, z)

    def term(axis, piece, rows):
        part = slice(piece * PIECE, (piece + 1) * PIECE)
        if axis == 0:
            return nt(n_buf[rows, :], t_buf[part, :])
        return nn(w_buf[rows, :], d_buf[:, part])

    def compute(job, slot, step):
        axis, piece = job
        first_row = lax.rem(place[axis] + step, 4) * CHUNK

        def one(half, carry):
            to = pl.ds(pl.multiple_of(half * HALF, HALF), HALF)
            rows = pl.ds(pl.multiple_of(first_row + half * HALF, HALF), HALF)
            send[axis][piece, slot, to, :] = term(axis, piece, rows).astype(BF)
            return carry

        lax.fori_loop(0, 2, one, 0)

    def ring(job):
        axis, piece = job
        out, come = send[axis].at[piece], recv[axis].at[piece]
        top, low = pl.ds(0, HALF), pl.ds(HALF, HALF)
        spans = (
            (out.at[0, top], come.at[0, top], ahead[axis]),
            (out.at[0, low], come.at[0, low], behind[axis]),
            (out.at[1], come.at[1], ahead[axis]),
            (out.at[2], come.at[2], behind[axis]),
        )
        return [
            remote(src, dst, ring_send.at[axis, piece, i], ring_recv.at[axis, piece, i], device)
            for i, (src, dst, device) in enumerate(spans)
        ]

    x0, x1, z0, z1 = jobs = ((0, 0), (0, 1), (1, 0), (1, 1))
    rings = {job: ring(job) for job in jobs}

    def launch(job):
        compute(job, 0, 2)
        rings[job][0].start()
        rings[job][1].start()

    def prepare(job):
        compute(job, 1, 1)
        compute(job, 2, 3)

    def relay(job):
        axis, piece = job
        for way, rows in ((0, slice(0, HALF)), (1, slice(HALF, CHUNK))):
            rings[job][way].wait()
            mine = send[axis][piece, 1 + way, rows, :].astype(F32)
            send[axis][piece, 1 + way, rows, :] = (
                mine + recv[axis][piece, 0, rows, :].astype(F32)
            ).astype(BF)
            rings[job][2 + way].start()

    side, side_device, pair_buf = (yh, yl), (across, beside), (xy, zy)

    def pair(job):
        axis, piece = job
        buf = pair_buf[axis].at[piece]
        return remote(
            buf.at[0], buf.at[1], pair_sems.at[0, axis, piece], pair_sems.at[1, axis, piece], side_device[axis]
        )

    pairs_of = {job: pair(job) for job in jobs}

    def cross(job):
        axis, piece = job
        rings[job][2].wait()
        rings[job][3].wait()

        def summed(half):
            rows = pl.ds(pl.multiple_of(half * HALF, HALF), HALF)
            return (
                send[axis][piece, 3, rows, :].astype(F32)
                + recv[axis][piece, 1, rows, :].astype(F32)
                + recv[axis][piece, 2, rows, :].astype(F32)
            ).astype(BF)

        pair_buf[axis][piece, 0] = summed(1 - side[axis])
        pairs_of[job].start()
        pair_buf[axis][piece, 2] = summed(side[axis])

    def total_of(job):
        axis, piece = job
        pairs_of[job].wait()
        return (pair_buf[axis][piece, 1].astype(F32) + pair_buf[axis][piece, 2].astype(F32)).astype(BF)

    my_rows = pl.ds(pl.multiple_of(core * QTR, QTR), QTR)
    its_rows = pl.ds(pl.multiple_of(other * QTR, QTR), QTR)
    lasts = [
        remote(half_buf.at[piece, its_rows], gw_out.at[piece, core], core_sems.at[0, piece], core_sems.at[1, piece], partner)
        for piece in range(2)
    ]

    def swap(piece):
        half_buf[piece] = total_of((0, piece))
        lasts[piece].start()
        gw_out[piece, core] = half_buf[piece, my_rows, :]

    launch(x0)
    prepare(x0)
    relay(x0)
    compute(x0, 3, 0)

    def add_to(ref, index):
        ref[...] = (ref[...].astype(F32) + y_buf[index].astype(F32)).astype(BF)

    y_copies[0].wait()

    @pl.when(yh == 1)
    def _():
        add_to(near, 0)
        back_near.start()

    y_copies[1].wait()

    @pl.when(yh == 0)
    def _():
        add_to(near, 1)
        back_near.start()

    @pl.when(yh == 1)
    def _():
        add_to(far, 1)
        back_far.start()

    keep = (yh == 0).astype(F32)
    for copy in loads[6:]:
        copy.wait()
    dq_keep.wait()
    dq_swap.wait()
    back_near.wait()
    back_far.wait()
    for r in range(2):
        for kind in range(2):
            total = (
                own[r, kind]
                + y_buf[0, r, kind].astype(F32) * keep
                + x_buf[0, r, kind].astype(F32)
                + x_buf[1, r, kind].astype(F32)
            ).T
            if kind == 0:
                a, b = total[: HD // 2, :], total[HD // 2 :, :]
                c, s = cos[r], sin[r]
                total = jnp.concatenate([a * c + b * s, b * c - a * s], axis=0)
            t_buf[(2 + kind) * HD : (3 + kind) * HD, r * TOK : (r + 1) * TOK] = total.astype(BF)
    dk_swaps = []
    its_cols = pl.ds(pl.multiple_of(other * TOK, TOK), TOK)
    my_cols = pl.ds(pl.multiple_of(core * TOK, TOK), TOK)
    for kind in range(2):
        rows = pl.ds(pl.multiple_of((4 + 2 * kind) * HD + core * HD, HD), HD)
        mine = pl.ds((2 + kind) * HD, HD)
        copy = remote(
            t_buf.at[mine, its_cols], d_buf.at[rows], dk_sems.at[0, kind], dk_sems.at[1, kind], partner
        )
        copy.start()
        dk_swaps.append(copy)
        d_buf[rows, :] = t_buf[mine, my_cols]
    for copy in dk_swaps:
        copy.wait()

    launch(z0)
    launch(z1)
    launch(x1)
    cross(x0)
    for job in (z0, z1, x1):
        prepare(job)
        relay(job)
    for job in (z0, z1, x1):
        compute(job, 3, 0)
    swap(0)
    for job in (z0, x1, z1):
        cross(job)
    gx_out[:, :PIECE] = total_of(z0)
    swap(1)
    gx_out[:, PIECE:] = total_of(z1)
    for copy in lasts:
        copy.wait()


def finish(dq, dkv, own, turned, wq, wk, wv, cos, sin):
    vmem = pl.BlockSpec(memory_space=pltpu.VMEM)
    hbm = pl.BlockSpec(memory_space=pltpu.HBM)
    any_space = pl.BlockSpec(memory_space=pl.ANY)
    dma = pltpu.SemaphoreType.DMA
    return pl.pallas_call(
        finish_kernel,
        out_shape=(
            jax.ShapeDtypeStruct((HALF, TOK), BF),
            jax.ShapeDtypeStruct((2, 2, QTR, PIECE), BF),
        ),
        in_specs=[any_space] * 3 + [hbm] * 4 + [vmem, vmem],
        out_specs=(vmem,) * 2,
        scratch_shapes=[
            pltpu.VMEM((2, 2, TOK, HD), F32),
            pltpu.VMEM((D, 2 * TOK), BF),
            pltpu.VMEM((D, 8 * HD), BF),
            pltpu.VMEM((4 * HD, 2 * TOK), BF),
            pltpu.VMEM((8 * HD, TOK), BF),
            pltpu.VMEM((2, 2, 2, TOK, HD), BF),
            pltpu.VMEM((2, 2, 2, TOK, HD), BF),
            pltpu.VMEM((2, 2, TOK, HD), BF),
            pltpu.VMEM((2, 2, TOK, HD), BF),
            pltpu.VMEM((2, 4, CHUNK, PIECE), BF),
            pltpu.VMEM((2, 3, CHUNK, PIECE), BF),
            pltpu.VMEM((2, 4, CHUNK, PIECE), BF),
            pltpu.VMEM((2, 3, CHUNK, PIECE), BF),
            pltpu.VMEM((2, 3, HALF, PIECE), BF),
            pltpu.VMEM((2, 3, HALF, PIECE), BF),
            pltpu.VMEM((2, HALF, PIECE), BF),
            dma((10,)), dma((3,)), dma((2, 2)), dma((2, 2)), dma((2, 2)),
            dma((2, 2, 4)), dma((2, 2, 4)), dma((2, 2, 2)), dma((2, 2)),
        ],
        compiler_params=pltpu.CompilerParams(
            collective_id=1, has_side_effects=True, vmem_limit_bytes=58 << 20
        ),
        name="finish",
    )(dq, dkv, own, turned, wq, wk, wv, cos, sin)


def emit_kernel(gx, gw, gx_out, gq_out, gk_out, gv_out):
    gx_out[...] = gx[...]
    for head in range(2):
        gq_out[:, head * 2 * HD : (head + 1) * 2 * HD] = gw[0, head]
        gk_out[:, head * HD : (head + 1) * HD] = gw[1, head, :, :HD]
        gv_out[:, head * HD : (head + 1) * HD] = gw[1, head, :, HD:]


def emit(gx, gw):
    vmem = pl.BlockSpec(memory_space=pltpu.VMEM)
    return pl.pallas_call(
        emit_kernel,
        out_shape=(
            jax.ShapeDtypeStruct((HALF, TOK), BF),
            jax.ShapeDtypeStruct((QTR, 4 * HD), BF),
            jax.ShapeDtypeStruct((QTR, 2 * HD), BF),
            jax.ShapeDtypeStruct((QTR, 2 * HD), BF),
        ),
        in_specs=[vmem] * 2,
        out_specs=(vmem,) * 4,
        name="emit",
    )(gx, gw)


def body(queries, keys, values, out_grad, normed, w_query, w_key, w_value, valid_len):
    chip = lax.axis_index("seq") // 2
    inverse_freq = ROPE_BASE ** (-(jnp.arange(HD // 2, dtype=F32) * (2.0 / HD)))
    slots = (chip * 2 * TOK + jnp.arange(2 * TOK, dtype=jnp.int32)).astype(F32).reshape(2, 1, TOK)
    angles = slots * inverse_freq[None, :, None]
    cos, sin = jnp.cos(angles), jnp.sin(angles)
    base = (2 * chip - 8).astype(jnp.int32).reshape(1)
    qx, gx, kv, turned = gather(queries, keys, values, out_grad, normed)
    dq, dkv, own = attend(valid_len, base, qx, gx, kv, cos, sin)
    gx, gq, gk, gv = emit(*finish(dq, dkv, own, turned, w_query, w_key, w_value, cos, sin))
    return gx.T, gq, gk, gv


def solution(mesh):
    both = P("seq", "head")
    placed = (both, both, both, both, P("seq", None), P(None, "head"), P(None, "head"), P(None, "head"), P())
    return jax.shard_map(
        body, mesh=mesh, in_specs=placed, out_specs=(both,) * 4, check_vma=False
    )
```

```python
import functools

import jax
import jax.numpy as jnp
from jax import lax
from jax.experimental import pallas as pl
from jax.experimental.pallas import tpu as pltpu
from jax.sharding import PartitionSpec as P

D = 4608
H = 32
HD = 128
WINDOW = 4096
SOFT_CAP = 50.0
ROPE_BASE = 10000.0
SCALE = (D // H) ** (-0.5)

TOK = 512
NB = 10
TILE = 256
CHUNK = D // 4
HALF = CHUNK // 2
QTR = HALF // 2

BF = jnp.bfloat16
F32 = jnp.float32
MESH = pl.DeviceIdType.MESH
LOG2E = 1.4426950408889634


def nt(left, right):
    return lax.dot_general(left, right, (((1,), (1,)), ((), ())), preferred_element_type=F32)


def nn(left, right):
    return lax.dot_general(left, right, (((1,), (0,)), ((), ())), preferred_element_type=F32)


def here():
    s, h = lax.axis_index("seq"), lax.axis_index("head")
    return s // 4, (s // 2) % 2, s % 2, h // 2, h % 2


def at_seq(x, yh, core):
    return {"seq": (lax.rem(x + 4, 4) * 2 + yh) * 2 + core, "head": lax.axis_index("head")}


def at_head(z, yl):
    return {"seq": lax.axis_index("seq"), "head": lax.rem(z + 4, 4) * 2 + yl}


def remote(src, dst, send, recv, device):
    return pltpu.make_async_remote_copy(
        src_ref=src, dst_ref=dst, send_sem=send, recv_sem=recv, device_id=device, device_id_type=MESH
    )


def greet(devices):
    barrier = pltpu.get_barrier_semaphore()
    for device in devices:
        pl.semaphore_signal(barrier, inc=1, device_id=device, device_id_type=MESH)
    pl.semaphore_wait(barrier, len(devices))


def gather_kernel(
    q, g, k, v, n_hbm, qg, kv, nt_out, kv_own, qg_own, n_ref, turned,
    n_load_sem, kv_load, qg_load, kv_loc, qg_loc, swap_send, swap_recv,
    x_send, x_recv, y_send, y_recv, n_sem, n_send, n_recv,
):
    x, yh, core, _, _ = here()
    other = 1 - core
    partner = at_seq(x, yh, other)
    across = at_seq(x, 1 - yh, core)

    def stage(pair, to, width, sems):
        return [
            pltpu.make_async_copy(
                ref.at[:, head * width : (head + 1) * width], to.at[head, kind], sems.at[head, kind]
            )
            for head in range(2)
            for kind, ref in enumerate(pair)
        ]

    kv_stage = stage((k, v), kv_own, HD, kv_load)
    qg_stage = stage((q, g), qg_own, 2 * HD, qg_load)
    n_load = pltpu.make_async_copy(n_hbm, n_ref, n_load_sem)
    for copy in kv_stage + qg_stage + [n_load]:
        copy.start()
    greet(
        [partner, across]
        + [at_seq(x + step, yh, c) for step in (1, -1, 2) for c in range(2)]
    )
    for copy in kv_stage:
        copy.wait()
    along = [
        [
            remote(
                kv_own.at[head],
                kv.at[8 - 4 * step + core],
                x_send.at[step - 1, head],
                x_recv.at[step - 1, core],
                at_seq(x + step, yh, head),
            )
            for head in range(2)
        ]
        for step in (1, 2)
    ]
    kv_swap = remote(kv_own.at[other], kv.at[8 + core], swap_send.at[0], swap_recv.at[0], partner)
    kv_keep = pltpu.make_async_copy(kv_own.at[core], kv.at[8 + core], kv_loc)
    qg_swap = remote(qg_own.at[other], qg.at[core], swap_send.at[1], swap_recv.at[1], partner)
    qg_keep = pltpu.make_async_copy(qg_own.at[core], qg.at[core], qg_loc)
    kv_swap.start()
    kv_keep.start()
    for copy in along[0] + along[1]:
        copy.start()

    def arrived(step, c):
        dst = kv.at[8 - 4 * step + c]
        remote(dst, dst, x_send.at[step - 1, c], x_recv.at[step - 1, c], partner).wait_recv()

    def turn(i, carry):
        cols = pl.ds(pl.multiple_of(i * HD, HD), HD)
        turned[cols, :] = n_ref[:, cols].T
        return carry

    first_src = jnp.where(yh == 0, 8, 4)
    second_src = jnp.where(yh == 0, 4, 0)
    first = [
        remote(kv.at[first_src + c], kv.at[6 + c], y_send.at[0, c], y_recv.at[0, c], across)
        for c in range(2)
    ]
    second = [
        remote(kv.at[second_src + c], kv.at[2 + c], y_send.at[1, c], y_recv.at[1, c], across)
        for c in range(2)
    ]
    kv_keep.wait()
    kv_swap.wait_recv()

    @pl.when(yh == 0)
    def _():
        for copy in first:
            copy.start()

    for copy in qg_stage:
        copy.wait()
    qg_swap.start()
    qg_keep.start()
    n_load.wait()
    lax.fori_loop(0, D // HD // 2, turn, 0)
    for c in range(2):
        arrived(1, c)

        @pl.when(yh == 0)
        def _():
            second[c].start()

        @pl.when(yh == 1)
        def _():
            first[c].start()

    lax.fori_loop(D // HD // 2, D // HD, turn, 0)
    n_local = pltpu.make_async_copy(turned, nt_out.at[core], n_sem)
    n_swap = remote(turned, nt_out.at[core], n_send, n_recv, partner)
    n_local.start()
    n_swap.start()
    for c in range(2):
        arrived(2, c)

        @pl.when(yh == 1)
        def _():
            second[c].start()

    n_local.wait()
    n_swap.wait()
    qg_keep.wait()
    qg_swap.wait()
    for copy in first + second:
        copy.wait()
    kv_swap.wait_send()
    for copy in along[0] + along[1]:
        copy.wait_send()


def gather(queries, keys, values, grads, normed):
    hbm = pl.BlockSpec(memory_space=pltpu.HBM)
    dma = pltpu.SemaphoreType.DMA
    return pl.pallas_call(
        gather_kernel,
        out_shape=(
            jax.ShapeDtypeStruct((2, 2, TOK, 2 * HD), BF),
            jax.ShapeDtypeStruct((NB, 2, TOK, HD), BF),
            jax.ShapeDtypeStruct((2, D, TOK), BF),
        ),
        in_specs=[hbm] * 5,
        out_specs=(hbm,) * 3,
        scratch_shapes=[
            pltpu.VMEM((2, 2, TOK, HD), BF),
            pltpu.VMEM((2, 2, TOK, 2 * HD), BF),
            pltpu.VMEM((TOK, D), BF),
            pltpu.VMEM((D, TOK), BF),
            dma, dma((2, 2)), dma((2, 2)), dma, dma, dma((2,)), dma((2,)),
            dma((2, 2)), dma((2, 2)), dma((2, 2)), dma((2, 2)), dma, dma, dma,
        ],
        compiler_params=pltpu.CompilerParams(
            collective_id=0, has_side_effects=True, vmem_limit_bytes=60 << 20
        ),
        name="gather",
    )(queries, grads, keys, values, normed)


STEP = 8
PIECES = 4 * NB
EMPTY = PIECES
OWN = PIECES + STEP


def attend_kernel(
    valid, base, qg, kv_hbm, cos, sin, dq_out, dkv_out, own_out,
    kv, e_s, w_s, kt_s, vt_s, o_acc, dq_acc, dk_acc, dv_acc, listed, sem,
):
    first_shard = base[0]
    load = pltpu.make_async_copy(kv_hbm, kv.at[pl.ds(0, NB)], sem)
    load.start()
    dk_acc[...] = jnp.zeros_like(dk_acc)
    dv_acc[...] = jnp.zeros_like(dv_acc)
    for k in range(STEP):
        kv[NB + k // 4, 0, k % 4] = jnp.zeros((HD, HD), BF)
        kv[NB + k // 4, 1, k % 4] = jnp.zeros((HD, HD), BF)
        kt_s[EMPTY + k] = jnp.zeros((HD, HD), BF)
        vt_s[EMPTY + k] = jnp.zeros((HD + 16, HD), BF)
    load.wait()

    def valid_of(b):
        return valid[jnp.maximum(first_shard + b, 0)]

    def turn(b, carry):
        for k in range(4):
            live = lax.broadcasted_iota(jnp.int32, (HD + 16, HD), 1) + k * HD < valid_of(b)
            k_t = kv[b, 0, k].T
            v_t = jnp.concatenate([kv[b, 1, k].T, jnp.ones((16, HD), BF)], axis=0)
            kt_s[4 * b + k] = jnp.where(live[:HD], k_t.astype(F32), 0.0).astype(BF)
            vt_s[4 * b + k] = jnp.where(live, v_t.astype(F32), 0.0).astype(BF)

            @pl.when(b >= 8)
            def _():
                kt_s[OWN + 4 * (b - 8) + k] = k_t
                vt_s[OWN + 4 * (b - 8) + k] = v_t

        return carry

    lax.fori_loop(0, NB, turn, 0)
    key_iota = lax.broadcasted_iota(jnp.int32, (TILE, 2 * TILE), 0)
    query_iota = lax.rem(lax.broadcasted_iota(jnp.int32, (TILE, 2 * TILE), 1), TILE)

    def query_tile(i, carry):
        r, qt = i // 2, lax.rem(i, 2)
        q_valid = valid_of(8 + r)
        q_rows = pl.ds(pl.multiple_of(qt * TILE, TILE), TILE)
        lanes = q_rows

        @pl.when(qt * TILE >= q_valid)
        def _():
            dq_out[r, :, lanes] = jnp.zeros((2 * HD, TILE), BF)

        @pl.when(qt * TILE < q_valid)
        def _():
            def note(t, count):
                j, k = t // 4, lax.rem(t, 4)
                b = r + j
                wanted = (
                    (first_shard + b >= 0)
                    & (k * HD < valid_of(b))
                    & jnp.logical_not((j == 0) & (k < 2 * qt + 2))
                    & jnp.logical_not((j == 8) & (k >= 2 * qt))
                )
                listed[count] = jnp.where(wanted, 4 * b + k, EMPTY)
                return count + wanted.astype(jnp.int32)

            count = lax.fori_loop(0, 36, note, 0)
            for extra in range(STEP - 1):
                listed[count + extra] = EMPTY + extra
            steps = (count + STEP - 1) // STEP
            doubles = steps // 2

            q_two = qg[r, 0, q_rows, :]
            g_two = qg[r, 1, q_rows, :]
            q_rows2 = jnp.concatenate([q_two[:, :HD], q_two[:, HD:]], axis=0)
            q_t = q_rows2.T

            def keys_of(kind, pieces):
                return jnp.concatenate([kv[p // 4, kind, lax.rem(p, 4)] for p in pieces], axis=0)

            def turned_of(ref, pieces):
                return jnp.concatenate([ref[p] for p in pieces], axis=1)

            def forward(pieces, turned, slot, mask):
                parts = []
                for n in range(0, len(pieces), 2):
                    keys = keys_of(0, pieces[n : n + 2])
                    rows = pl.ds(pl.multiple_of(slot + n * HD, TILE), TILE)
                    heads = []
                    for head in range(2):
                        cols = slice(head * TILE, (head + 1) * TILE)
                        th = jnp.tanh(nn(keys, q_t[:, cols]) * (SCALE / SOFT_CAP))
                        e = jnp.exp2(th * (SOFT_CAP * LOG2E))
                        if mask is not None:
                            e = jnp.where(mask[n // 2][:, cols], e, 0.0)
                        eb = e.astype(BF)
                        e_s[rows, cols] = eb
                        w_s[rows, cols] = (e * (1.0 - th * th)).astype(BF)
                        heads.append(eb)
                    parts.append(heads)
                for head in range(2):
                    cols = slice(head * TILE, (head + 1) * TILE)
                    column = jnp.concatenate([p[head] for p in parts], axis=0)
                    o_acc[:, cols] += nn(turned_of(vt_s, turned), column)

            gap = query_iota - key_iota
            key_pos = key_iota + qt * TILE
            oldest_there = first_shard + r >= 0
            edge_mask = (
                gap + 8 * TOK < WINDOW,
                (gap >= 0) & ((key_pos < q_valid) | (gap == 0)),
            )
            old = jnp.where(oldest_there, 4 * r + 2 * qt, EMPTY)
            own = 4 * (8 + r) + 2 * qt
            edge = (old, old + 1, own, own + 1)
            edge_turned = (old, old + 1, OWN + 4 * r + 2 * qt, OWN + 4 * r + 2 * qt + 1)
            o_acc[...] = jnp.zeros_like(o_acc)
            forward(edge, edge_turned, 0, edge_mask)

            def forward_step(width, n, carry):
                pieces = tuple(listed[n * width + m] for m in range(width))
                forward(pieces, pieces, (4 + n * width) * HD, None)
                return carry

            lax.fori_loop(0, doubles, functools.partial(forward_step, 2 * STEP), 0)
            lax.fori_loop(2 * doubles, steps, functools.partial(forward_step, STEP), 0)
            inv = 1.0 / o_acc[HD : HD + 1, :]
            g_rows2 = jnp.concatenate([g_two[:, :HD], g_two[:, HD:]], axis=0).astype(F32)
            live = query_iota[:1, :] + qt * TILE < q_valid
            g_t = jnp.where(live, g_rows2.T, 0.0) * inv
            delta = jnp.sum(g_t * o_acc[:HD, :], axis=0, keepdims=True) * inv
            gs_t = g_t.astype(BF)
            gs = g_t.T.astype(BF)
            dq_acc[...] = jnp.zeros_like(dq_acc)

            def backward(pieces, turned, slot):
                rows = pl.ds(pl.multiple_of(slot, TILE), len(pieces) * HD)
                columns = []
                for head in range(2):
                    cols = slice(head * TILE, (head + 1) * TILE)
                    parts = []
                    for n in range(0, len(pieces), 2):
                        part = pl.ds(pl.multiple_of(slot + n * HD, TILE), TILE)
                        dp = nn(keys_of(1, pieces[n : n + 2]), gs_t[:, cols])
                        parts.append((w_s[part, cols].astype(F32) * (dp - delta[:, cols])).astype(BF))
                    columns.append(jnp.concatenate(parts, axis=0))
                ds = jnp.concatenate(columns, axis=1)
                dq_acc[...] += nn(turned_of(kt_s, turned), ds)
                dk = nn(ds, q_rows2)
                dv = nn(e_s[rows, :], gs)
                for n, p in enumerate(pieces):
                    dk_acc[p] += dk[n * HD : (n + 1) * HD]
                    dv_acc[p] += dv[n * HD : (n + 1) * HD]

            backward(edge, edge_turned, 0)

            def backward_step(width, n, carry):
                pieces = tuple(listed[n * width + m] for m in range(width))
                backward(pieces, pieces, (4 + n * width) * HD)
                return carry

            lax.fori_loop(0, doubles, functools.partial(backward_step, 2 * STEP), 0)
            lax.fori_loop(2 * doubles, steps, functools.partial(backward_step, STEP), 0)
            dq = dq_acc[...] * SCALE
            c, s = cos[r, :, lanes], sin[r, :, lanes]
            for head in range(2):
                a = dq[: HD // 2, head * TILE : (head + 1) * TILE]
                z = dq[HD // 2 :, head * TILE : (head + 1) * TILE]
                dq_out[r, head * HD : head * HD + HD // 2, lanes] = (a * c + z * s).astype(BF)
                dq_out[r, head * HD + HD // 2 : (head + 1) * HD, lanes] = (z * c - a * s).astype(BF)

        return carry

    lax.fori_loop(0, 4, query_tile, 0)

    def result(ref, b, k, scale):
        live = lax.broadcasted_iota(jnp.int32, (HD, HD), 0) + k * HD < valid_of(b)
        return jnp.where(live, ref[4 * b + k] * scale, 0.0)

    def give(b, carry):
        for k in range(4):
            rows = slice(k * HD, (k + 1) * HD)
            dkv_out[b, 0, rows, :] = result(dk_acc, b, k, SCALE).astype(BF)
            dkv_out[b, 1, rows, :] = result(dv_acc, b, k, 1.0).astype(BF)
        return carry

    lax.fori_loop(0, 8, give, 0)
    for r in range(2):
        for k in range(4):
            rows = slice(k * HD, (k + 1) * HD)
            own_out[r, 0, rows, :] = result(dk_acc, 8 + r, k, SCALE)
            own_out[r, 1, rows, :] = result(dv_acc, 8 + r, k, 1.0)


def attend(valid_len, base, qg, kv, cos, sin):
    vmem = pl.BlockSpec(memory_space=pltpu.VMEM)
    smem = pl.BlockSpec(memory_space=pltpu.SMEM)
    return pl.pallas_call(
        attend_kernel,
        out_shape=(
            jax.ShapeDtypeStruct((2, 2 * HD, TOK), BF),
            jax.ShapeDtypeStruct((8, 2, TOK, HD), BF),
            jax.ShapeDtypeStruct((2, 2, TOK, HD), F32),
        ),
        in_specs=[smem, smem, vmem, pl.BlockSpec(memory_space=pltpu.HBM), vmem, vmem],
        out_specs=(vmem,) * 3,
        scratch_shapes=[
            pltpu.VMEM((NB + STEP // 4, 2, 4, HD, HD), BF),
            pltpu.VMEM((44 * HD, 2 * TILE), BF),
            pltpu.VMEM((44 * HD, 2 * TILE), BF),
            pltpu.VMEM((OWN + 8, HD, HD), BF),
            pltpu.VMEM((OWN + 8, HD + 16, HD), BF),
            pltpu.VMEM((HD + 16, 2 * TILE), F32),
            pltpu.VMEM((HD, 2 * TILE), F32),
            pltpu.VMEM((PIECES + STEP, HD, HD), F32),
            pltpu.VMEM((PIECES + STEP, HD, HD), F32),
            pltpu.SMEM((48,), jnp.int32),
            pltpu.SemaphoreType.DMA,
        ],
        compiler_params=pltpu.CompilerParams(vmem_limit_bytes=58 << 20),
        name="attend",
    )(valid_len, base, qg, kv.reshape(NB, 2, 4, HD, HD), cos, sin)


PIECE = 256


def finish_kernel(
    dq, dkv, own_hbm, turned_hbm, wq, wk, wv, cos, sin, gx_out, gw_out,
    own, n_buf, w_buf, t_buf, d_buf, y_buf, x_buf, near, far,
    xs, xr, zs, zr, xy, zy, half_buf,
    load_sem, dq_sems, dk_sems, y_sems, x_sems, ring_send, ring_recv, pair_sems, core_sems,
):
    x, yh, core, z, yl = here()
    other = 1 - core
    partner = at_seq(x, yh, other)
    across = at_seq(x, 1 - yh, core)
    beside = at_head(z, 1 - yl)
    x_next, x_prev, x_far = at_seq(x + 1, yh, core), at_seq(x - 1, yh, core), at_seq(x + 2, yh, core)
    z_next, z_prev = at_head(z + 1, yl), at_head(z - 1, yl)
    greet([partner, across, beside, x_next, x_prev, x_far, z_next, z_prev])

    y_copies = [
        [
            remote(dkv.at[6 - 4 * i + r], y_buf.at[i, r], y_sems.at[0, i, r], y_sems.at[1, i, r], across)
            for r in range(2)
        ]
        for i in range(2)
    ]
    for copy in y_copies[1] + y_copies[0]:
        copy.start()
    pairs = [
        (dkv.at[pl.ds(0, 2)], far),
        (dkv.at[pl.ds(4, 2)], near),
        (dq.at[0], t_buf.at[: 2 * HD, :TOK]),
        (dq.at[1], t_buf.at[: 2 * HD, TOK:]),
        (turned_hbm.at[0], n_buf.at[:, :TOK]),
        (turned_hbm.at[1], n_buf.at[:, TOK:]),
        (own_hbm, own),
        (wq, w_buf.at[:, : 4 * HD]),
        (wk, w_buf.at[:, 4 * HD : 6 * HD]),
        (wv, w_buf.at[:, 6 * HD :]),
    ]
    loads = [pltpu.make_async_copy(src, dst, load_sem.at[i]) for i, (src, dst) in enumerate(pairs)]
    for copy in loads:
        copy.start()
    head_rows = pl.ds(pl.multiple_of(core * 2 * HD, 2 * HD), 2 * HD)
    dq_swap = remote(dq.at[other], d_buf.at[head_rows], dq_sems.at[0], dq_sems.at[1], partner)
    dq_keep = pltpu.make_async_copy(dq.at[core], d_buf.at[head_rows], dq_sems.at[2])
    back_near, back_far = (
        [
            remote(src.at[r], x_buf.at[i, r], x_sems.at[0, i, r], x_sems.at[1, i, r], device)
            for r in range(2)
        ]
        for i, (src, device) in enumerate(((near, x_prev), (far, x_far)))
    )
    loads[0].wait()

    @pl.when(yh == 0)
    def _():
        for copy in back_far:
            copy.start()

    dq_swap.start()
    dq_keep.start()
    for copy in loads[1:6]:
        copy.wait()

    send, recv = (xs, zs), (xr, zr)
    ahead, behind = (x_next, z_next), (x_prev, z_prev)
    place = (x, z)

    def term(axis, piece, rows):
        part = slice(piece * PIECE, (piece + 1) * PIECE)
        if axis == 0:
            return nt(n_buf[rows, :], t_buf[part, :])
        return nn(w_buf[rows, :], d_buf[:, part])

    def compute(job, slot, step):
        axis, piece = job
        first_row = lax.rem(place[axis] + step, 4) * CHUNK

        def one(half, carry):
            to = pl.ds(pl.multiple_of(half * HALF, HALF), HALF)
            rows = pl.ds(pl.multiple_of(first_row + half * HALF, HALF), HALF)
            send[axis][piece, slot, to, :] = term(axis, piece, rows).astype(BF)
            return carry

        lax.fori_loop(0, 2, one, 0)

    def ring(job):
        axis, piece = job
        out, come = send[axis].at[piece], recv[axis].at[piece]
        top, low = pl.ds(0, HALF), pl.ds(HALF, HALF)
        spans = (
            (out.at[0, top], come.at[0, top], ahead[axis]),
            (out.at[0, low], come.at[0, low], behind[axis]),
            (out.at[1], come.at[1], ahead[axis]),
            (out.at[2], come.at[2], behind[axis]),
        )
        return [
            remote(src, dst, ring_send.at[axis, piece, i], ring_recv.at[axis, piece, i], device)
            for i, (src, dst, device) in enumerate(spans)
        ]

    x0, x1, z0, z1 = jobs = ((0, 0), (0, 1), (1, 0), (1, 1))
    rings = {job: ring(job) for job in jobs}

    def launch(job):
        compute(job, 0, 2)
        rings[job][0].start()
        rings[job][1].start()

    def prepare(job):
        compute(job, 1, 1)
        compute(job, 2, 3)

    def relay(job):
        axis, piece = job
        for way, rows in ((0, slice(0, HALF)), (1, slice(HALF, CHUNK))):
            rings[job][way].wait()
            mine = send[axis][piece, 1 + way, rows, :].astype(F32)
            send[axis][piece, 1 + way, rows, :] = (
                mine + recv[axis][piece, 0, rows, :].astype(F32)
            ).astype(BF)
            rings[job][2 + way].start()

    side, side_device, pair_buf = (yh, yl), (across, beside), (xy, zy)

    def pair(job):
        axis, piece = job
        buf = pair_buf[axis].at[piece]
        return remote(
            buf.at[0], buf.at[1], pair_sems.at[0, axis, piece], pair_sems.at[1, axis, piece], side_device[axis]
        )

    pairs_of = {job: pair(job) for job in jobs}

    def cross(job):
        axis, piece = job
        rings[job][2].wait()
        rings[job][3].wait()

        def summed(half):
            rows = pl.ds(pl.multiple_of(half * HALF, HALF), HALF)
            return (
                send[axis][piece, 3, rows, :].astype(F32)
                + recv[axis][piece, 1, rows, :].astype(F32)
                + recv[axis][piece, 2, rows, :].astype(F32)
            ).astype(BF)

        pair_buf[axis][piece, 0] = summed(1 - side[axis])
        pairs_of[job].start()
        pair_buf[axis][piece, 2] = summed(side[axis])

    def total_of(job):
        axis, piece = job
        pairs_of[job].wait()
        return (pair_buf[axis][piece, 1].astype(F32) + pair_buf[axis][piece, 2].astype(F32)).astype(BF)

    my_rows = pl.ds(pl.multiple_of(core * QTR, QTR), QTR)
    its_rows = pl.ds(pl.multiple_of(other * QTR, QTR), QTR)
    lasts = [
        remote(half_buf.at[piece, its_rows], gw_out.at[piece, core], core_sems.at[0, piece], core_sems.at[1, piece], partner)
        for piece in range(2)
    ]

    def swap(piece):
        half_buf[piece] = total_of((0, piece))
        lasts[piece].start()
        gw_out[piece, core] = half_buf[piece, my_rows, :]


    def add_to(ref, index, r):
        ref[r] = (ref[r].astype(F32) + y_buf[index, r].astype(F32)).astype(BF)

    def further(r):
        y_copies[1][r].wait()

        @pl.when(yh == 0)
        def _():
            add_to(near, 1, r)
            back_near[r].start()

        @pl.when(yh == 1)
        def _():
            add_to(far, 1, r)
            back_far[r].start()

    def nearer(r):
        y_copies[0][r].wait()

        @pl.when(yh == 1)
        def _():
            add_to(near, 0, r)
            back_near[r].start()

    launch(x0)
    prepare(x0)
    compute(x0, 3, 0)
    for r in range(2):
        further(r)
    for r in range(2):
        nearer(r)
    keep = (yh == 0).astype(F32)
    for copy in loads[6:]:
        copy.wait()
    dq_keep.wait()
    dq_swap.wait()
    for copy in back_far + back_near:
        copy.wait()
    for r in range(2):
        for kind in range(2):
            total = (
                own[r, kind]
                + y_buf[0, r, kind].astype(F32) * keep
                + x_buf[0, r, kind].astype(F32)
                + x_buf[1, r, kind].astype(F32)
            ).T
            if kind == 0:
                a, b = total[: HD // 2, :], total[HD // 2 :, :]
                c, s = cos[r], sin[r]
                total = jnp.concatenate([a * c + b * s, b * c - a * s], axis=0)
            t_buf[(2 + kind) * HD : (3 + kind) * HD, r * TOK : (r + 1) * TOK] = total.astype(BF)
    dk_swaps = []
    its_cols = pl.ds(pl.multiple_of(other * TOK, TOK), TOK)
    my_cols = pl.ds(pl.multiple_of(core * TOK, TOK), TOK)
    for kind in range(2):
        rows = pl.ds(pl.multiple_of((4 + 2 * kind) * HD + core * HD, HD), HD)
        mine = pl.ds((2 + kind) * HD, HD)
        copy = remote(
            t_buf.at[mine, its_cols], d_buf.at[rows], dk_sems.at[0, kind], dk_sems.at[1, kind], partner
        )
        copy.start()
        dk_swaps.append(copy)
        d_buf[rows, :] = t_buf[mine, my_cols]
    for copy in dk_swaps:
        copy.wait()

    launch(z0)
    launch(z1)
    relay(x0)
    launch(x1)
    cross(x0)
    for job in (z0, z1, x1):
        prepare(job)
        relay(job)
    for job in (z0, z1, x1):
        compute(job, 3, 0)
    swap(0)
    for job in (z0, x1, z1):
        cross(job)
    gx_out[:, :PIECE] = total_of(z0)
    swap(1)
    gx_out[:, PIECE:] = total_of(z1)
    for copy in lasts:
        copy.wait()


def finish(dq, dkv, own, turned, wq, wk, wv, cos, sin):
    vmem = pl.BlockSpec(memory_space=pltpu.VMEM)
    hbm = pl.BlockSpec(memory_space=pltpu.HBM)
    any_space = pl.BlockSpec(memory_space=pl.ANY)
    dma = pltpu.SemaphoreType.DMA
    return pl.pallas_call(
        finish_kernel,
        out_shape=(
            jax.ShapeDtypeStruct((HALF, TOK), BF),
            jax.ShapeDtypeStruct((2, 2, QTR, PIECE), BF),
        ),
        in_specs=[any_space] * 3 + [hbm] * 4 + [vmem, vmem],
        out_specs=(vmem,) * 2,
        scratch_shapes=[
            pltpu.VMEM((2, 2, TOK, HD), F32),
            pltpu.VMEM((D, 2 * TOK), BF),
            pltpu.VMEM((D, 8 * HD), BF),
            pltpu.VMEM((4 * HD, 2 * TOK), BF),
            pltpu.VMEM((8 * HD, TOK), BF),
            pltpu.VMEM((2, 2, 2, TOK, HD), BF),
            pltpu.VMEM((2, 2, 2, TOK, HD), BF),
            pltpu.VMEM((2, 2, TOK, HD), BF),
            pltpu.VMEM((2, 2, TOK, HD), BF),
            pltpu.VMEM((2, 4, CHUNK, PIECE), BF),
            pltpu.VMEM((2, 3, CHUNK, PIECE), BF),
            pltpu.VMEM((2, 4, CHUNK, PIECE), BF),
            pltpu.VMEM((2, 3, CHUNK, PIECE), BF),
            pltpu.VMEM((2, 3, HALF, PIECE), BF),
            pltpu.VMEM((2, 3, HALF, PIECE), BF),
            pltpu.VMEM((2, HALF, PIECE), BF),
            dma((10,)), dma((3,)), dma((2, 2)), dma((2, 2, 2)), dma((2, 2, 2)),
            dma((2, 2, 4)), dma((2, 2, 4)), dma((2, 2, 2)), dma((2, 2)),
        ],
        compiler_params=pltpu.CompilerParams(
            collective_id=1, has_side_effects=True, vmem_limit_bytes=58 << 20
        ),
        name="finish",
    )(dq, dkv, own, turned, wq, wk, wv, cos, sin)


def emit_kernel(gx, gw, gx_out, gq_out, gk_out, gv_out):
    gx_out[...] = gx[...]
    for head in range(2):
        gq_out[:, head * 2 * HD : (head + 1) * 2 * HD] = gw[0, head]
        gk_out[:, head * HD : (head + 1) * HD] = gw[1, head, :, :HD]
        gv_out[:, head * HD : (head + 1) * HD] = gw[1, head, :, HD:]


def emit(gx, gw):
    vmem = pl.BlockSpec(memory_space=pltpu.VMEM)
    return pl.pallas_call(
        emit_kernel,
        out_shape=(
            jax.ShapeDtypeStruct((HALF, TOK), BF),
            jax.ShapeDtypeStruct((QTR, 4 * HD), BF),
            jax.ShapeDtypeStruct((QTR, 2 * HD), BF),
            jax.ShapeDtypeStruct((QTR, 2 * HD), BF),
        ),
        in_specs=[vmem] * 2,
        out_specs=(vmem,) * 4,
        name="emit",
    )(gx, gw)


def body(queries, keys, values, out_grad, normed, w_query, w_key, w_value, valid_len):
    chip = lax.axis_index("seq") // 2
    inverse_freq = ROPE_BASE ** (-(jnp.arange(HD // 2, dtype=F32) * (2.0 / HD)))
    slots = (chip * 2 * TOK + jnp.arange(2 * TOK, dtype=jnp.int32)).astype(F32).reshape(2, 1, TOK)
    angles = slots * inverse_freq[None, :, None]
    cos, sin = jnp.cos(angles), jnp.sin(angles)
    base = (2 * chip - 8).astype(jnp.int32).reshape(1)
    qg, kv, turned = gather(queries, keys, values, out_grad, normed)
    dq, dkv, own = attend(valid_len, base, qg, kv, cos, sin)
    gx, gq, gk, gv = emit(*finish(dq, dkv, own, turned, w_query, w_key, w_value, cos, sin))
    return gx.T, gq, gk, gv


def solution(mesh):
    both = P("seq", "head")
    placed = (both, both, both, both, P("seq", None), P(None, "head"), P(None, "head"), P(None, "head"), P())
    return jax.shard_map(
        body, mesh=mesh, in_specs=placed, out_specs=(both,) * 4, check_vma=False
    )
```

```python
import functools

import jax
import jax.numpy as jnp
from jax import lax
from jax.experimental import pallas as pl
from jax.experimental.pallas import tpu as pltpu
from jax.sharding import PartitionSpec as P

D = 4608
H = 32
HD = 128
WINDOW = 4096
SOFT_CAP = 50.0
ROPE_BASE = 10000.0
SCALE = (D // H) ** (-0.5)

TOK = 512
NB = 10
TILE = 256
CHUNK = D // 4
HALF = CHUNK // 2
QTR = HALF // 2

BF = jnp.bfloat16
F32 = jnp.float32
MESH = pl.DeviceIdType.MESH
STEPS = (1, -1, 2)
LOG2E = 1.4426950408889634


def nt(left, right):
    return lax.dot_general(left, right, (((1,), (1,)), ((), ())), preferred_element_type=F32)


def nn(left, right):
    return lax.dot_general(left, right, (((1,), (0,)), ((), ())), preferred_element_type=F32)


def here():
    s, h = lax.axis_index("seq"), lax.axis_index("head")
    return s // 4, (s // 2) % 2, s % 2, h // 2, h % 2


def at_seq(x, yh, core):
    return {"seq": (lax.rem(x + 4, 4) * 2 + yh) * 2 + core, "head": lax.axis_index("head")}


def at_head(z, yl):
    return {"seq": lax.axis_index("seq"), "head": lax.rem(z + 4, 4) * 2 + yl}


def at_core(z, yl, core):
    s = lax.axis_index("seq")
    return {"seq": s - s % 2 + core, "head": lax.rem(z + 4, 4) * 2 + yl}


def remote(src, dst, send, recv, device):
    return pltpu.make_async_remote_copy(
        src_ref=src, dst_ref=dst, send_sem=send, recv_sem=recv, device_id=device, device_id_type=MESH
    )


def greet(devices):
    barrier = pltpu.get_barrier_semaphore()
    for device in devices:
        pl.semaphore_signal(barrier, inc=1, device_id=device, device_id_type=MESH)
    pl.semaphore_wait(barrier, len(devices))


def gather_kernel(
    q, g, k, v, n_hbm, wk, wv, qg, kv, nt_out, w_all, kv_own, qg_own, n_ref, turned,
    n_load_sem, kv_load, qg_load, kv_loc, qg_loc, swap_send, swap_recv,
    x_send, x_recv, y_send, y_recv, n_sem, n_send, n_recv, w_loc, w_send, w_recv, w_pass, w_get,
):
    x, yh, core, z, yl = here()
    other = 1 - core
    partner = at_seq(x, yh, other)
    across = at_seq(x, 1 - yh, core)

    def stage(pair, to, width, sems):
        return [
            pltpu.make_async_copy(
                ref.at[:, head * width : (head + 1) * width], to.at[head, kind], sems.at[head, kind]
            )
            for head in range(2)
            for kind, ref in enumerate(pair)
        ]

    kv_stage = stage((k, v), kv_own, HD, kv_load)
    qg_stage = stage((q, g), qg_own, 2 * HD, qg_load)
    n_load = pltpu.make_async_copy(n_hbm, n_ref, n_load_sem)
    for copy in kv_stage + qg_stage + [n_load]:
        copy.start()
    greet(
        [partner, across]
        + [at_seq(x + step, yh, c) for step in (1, -1, 2) for c in range(2)]
        + [at_head(z + step, yl) for step in STEPS]
    )
    for copy in kv_stage:
        copy.wait()
    along = [
        [
            remote(
                kv_own.at[head],
                kv.at[8 - 4 * step + core],
                x_send.at[step - 1, head],
                x_recv.at[step - 1, core],
                at_seq(x + step, yh, head),
            )
            for head in range(2)
        ]
        for step in (1, 2)
    ]
    kv_swap = remote(kv_own.at[other], kv.at[8 + core], swap_send.at[0], swap_recv.at[0], partner)
    kv_keep = pltpu.make_async_copy(kv_own.at[core], kv.at[8 + core], kv_loc)
    qg_swap = remote(qg_own.at[other], qg.at[core], swap_send.at[1], swap_recv.at[1], partner)
    qg_keep = pltpu.make_async_copy(qg_own.at[core], qg.at[core], qg_loc)
    kv_swap.start()
    kv_keep.start()
    for copy in along[0] + along[1]:
        copy.start()

    def arrived(step, c):
        dst = kv.at[8 - 4 * step + c]
        remote(dst, dst, x_send.at[step - 1, c], x_recv.at[step - 1, c], partner).wait_recv()

    def turn(i, carry):
        cols = pl.ds(pl.multiple_of(i * HD, HD), HD)
        turned[cols, :] = n_ref[:, cols].T
        return carry

    first_src = jnp.where(yh == 0, 8, 4)
    second_src = jnp.where(yh == 0, 4, 0)
    first = [
        remote(kv.at[first_src + c], kv.at[6 + c], y_send.at[0, c], y_recv.at[0, c], across)
        for c in range(2)
    ]
    second = [
        remote(kv.at[second_src + c], kv.at[2 + c], y_send.at[1, c], y_recv.at[1, c], across)
        for c in range(2)
    ]
    kv_keep.wait()
    kv_swap.wait_recv()

    @pl.when(yh == 0)
    def _():
        for copy in first:
            copy.start()

    part = pl.ds(pl.multiple_of(core * HALF, HALF), HALF)
    w_keep, w_out, w_on = [], [], []
    for kind, ref in enumerate((wk, wv)):
        own_rows = pl.ds(pl.multiple_of(z * CHUNK, CHUNK), CHUNK)
        w_keep.append(pltpu.make_async_copy(ref.at[own_rows], w_all.at[z, kind], w_loc.at[kind]))
        for i, step in enumerate(STEPS):
            rows = pl.ds(pl.multiple_of(lax.rem(z + 4 + step, 4) * CHUNK + core * HALF, HALF), HALF)
            w_out.append(
                remote(ref.at[rows], w_all.at[z, kind, part], w_send.at[kind, i], w_recv.at[kind, i], at_head(z + step, yl))
            )
            come = w_all.at[lax.rem(z + 4 - step, 4), kind, part]
            w_on.append(remote(come, come, w_pass.at[kind, i], w_get.at[kind, i], partner))
    for copy in w_out + w_keep:
        copy.start()
    for copy in qg_stage:
        copy.wait()
    qg_swap.start()
    qg_keep.start()
    n_load.wait()
    lax.fori_loop(0, D // HD // 2, turn, 0)
    for c in range(2):
        arrived(1, c)

        @pl.when(yh == 0)
        def _():
            second[c].start()

        @pl.when(yh == 1)
        def _():
            first[c].start()

    lax.fori_loop(D // HD // 2, D // HD, turn, 0)
    n_local = pltpu.make_async_copy(turned, nt_out.at[core], n_sem)
    n_swap = remote(turned, nt_out.at[core], n_send, n_recv, partner)
    n_local.start()
    n_swap.start()
    for c in range(2):
        arrived(2, c)

        @pl.when(yh == 1)
        def _():
            second[c].start()

    for out, on in zip(w_out, w_on):
        out.wait()
        on.start()
    n_local.wait()
    n_swap.wait()
    qg_keep.wait()
    qg_swap.wait()
    for copy in first + second:
        copy.wait()
    for copy in w_on + w_keep:
        copy.wait()
    kv_swap.wait_send()
    for copy in along[0] + along[1]:
        copy.wait_send()


def gather(queries, keys, values, grads, normed, wk, wv):
    hbm = pl.BlockSpec(memory_space=pltpu.HBM)
    dma = pltpu.SemaphoreType.DMA
    return pl.pallas_call(
        gather_kernel,
        out_shape=(
            jax.ShapeDtypeStruct((2, 2, TOK, 2 * HD), BF),
            jax.ShapeDtypeStruct((NB, 2, TOK, HD), BF),
            jax.ShapeDtypeStruct((2, D, TOK), BF),
            jax.ShapeDtypeStruct((4, 2, CHUNK, 2 * HD), BF),
        ),
        in_specs=[hbm] * 7,
        out_specs=(hbm,) * 4,
        scratch_shapes=[
            pltpu.VMEM((2, 2, TOK, HD), BF),
            pltpu.VMEM((2, 2, TOK, 2 * HD), BF),
            pltpu.VMEM((TOK, D), BF),
            pltpu.VMEM((D, TOK), BF),
            dma, dma((2, 2)), dma((2, 2)), dma, dma, dma((2,)), dma((2,)),
            dma((2, 2)), dma((2, 2)), dma((2, 2)), dma((2, 2)), dma, dma, dma,
            dma((2,)), dma((2, 3)), dma((2, 3)), dma((2, 3)), dma((2, 3)),
        ],
        compiler_params=pltpu.CompilerParams(
            collective_id=0, has_side_effects=True, vmem_limit_bytes=60 << 20
        ),
        name="gather",
    )(queries, grads, keys, values, normed, wk, wv)


STEP = 8
PIECES = 4 * NB
EMPTY = PIECES
OWN = PIECES + STEP


def attend_kernel(
    valid, base, qg, kv_hbm, cos, sin, dq_out, dkv_out, own_out,
    kv, e_s, w_s, kt_s, vt_s, o_acc, dq_acc, dk_acc, dv_acc, listed, sem,
):
    first_shard = base[0]
    load = pltpu.make_async_copy(kv_hbm, kv.at[pl.ds(0, NB)], sem)
    load.start()
    dk_acc[...] = jnp.zeros_like(dk_acc)
    dv_acc[...] = jnp.zeros_like(dv_acc)
    for k in range(STEP):
        kv[NB + k // 4, 0, k % 4] = jnp.zeros((HD, HD), BF)
        kv[NB + k // 4, 1, k % 4] = jnp.zeros((HD, HD), BF)
        kt_s[EMPTY + k] = jnp.zeros((HD, HD), BF)
        vt_s[EMPTY + k] = jnp.zeros((HD + 16, HD), BF)
    load.wait()

    def valid_of(b):
        return valid[jnp.maximum(first_shard + b, 0)]

    def turn(b, carry):
        for k in range(4):
            live = lax.broadcasted_iota(jnp.int32, (HD + 16, HD), 1) + k * HD < valid_of(b)
            k_t = kv[b, 0, k].T
            v_t = jnp.concatenate([kv[b, 1, k].T, jnp.ones((16, HD), BF)], axis=0)
            kt_s[4 * b + k] = jnp.where(live[:HD], k_t.astype(F32), 0.0).astype(BF)
            vt_s[4 * b + k] = jnp.where(live, v_t.astype(F32), 0.0).astype(BF)

            @pl.when(b >= 8)
            def _():
                kt_s[OWN + 4 * (b - 8) + k] = k_t
                vt_s[OWN + 4 * (b - 8) + k] = v_t

        return carry

    lax.fori_loop(0, NB, turn, 0)
    key_iota = lax.broadcasted_iota(jnp.int32, (TILE, 2 * TILE), 0)
    query_iota = lax.rem(lax.broadcasted_iota(jnp.int32, (TILE, 2 * TILE), 1), TILE)

    def query_tile(i, carry):
        r, qt = i // 2, lax.rem(i, 2)
        q_valid = valid_of(8 + r)
        q_rows = pl.ds(pl.multiple_of(qt * TILE, TILE), TILE)
        lanes = q_rows

        @pl.when(qt * TILE >= q_valid)
        def _():
            dq_out[r, :, lanes] = jnp.zeros((2 * HD, TILE), BF)

        @pl.when(qt * TILE < q_valid)
        def _():
            def note(t, count):
                j, k = t // 4, lax.rem(t, 4)
                b = r + j
                wanted = (
                    (first_shard + b >= 0)
                    & (k * HD < valid_of(b))
                    & jnp.logical_not((j == 0) & (k < 2 * qt + 2))
                    & jnp.logical_not((j == 8) & (k >= 2 * qt))
                )
                listed[count] = jnp.where(wanted, 4 * b + k, EMPTY)
                return count + wanted.astype(jnp.int32)

            count = lax.fori_loop(0, 36, note, 0)
            for extra in range(STEP - 1):
                listed[count + extra] = EMPTY + extra
            steps = (count + STEP - 1) // STEP
            doubles = steps // 2

            q_two = qg[r, 0, q_rows, :]
            g_two = qg[r, 1, q_rows, :]
            q_rows2 = jnp.concatenate([q_two[:, :HD], q_two[:, HD:]], axis=0)
            q_t = q_rows2.T

            def keys_of(kind, pieces):
                return jnp.concatenate([kv[p // 4, kind, lax.rem(p, 4)] for p in pieces], axis=0)

            def turned_of(ref, pieces):
                return jnp.concatenate([ref[p] for p in pieces], axis=1)

            def forward(pieces, turned, slot, mask):
                parts = []
                for n in range(0, len(pieces), 2):
                    keys = keys_of(0, pieces[n : n + 2])
                    rows = pl.ds(pl.multiple_of(slot + n * HD, TILE), TILE)
                    heads = []
                    for head in range(2):
                        cols = slice(head * TILE, (head + 1) * TILE)
                        th = jnp.tanh(nn(keys, q_t[:, cols]) * (SCALE / SOFT_CAP))
                        e = jnp.exp2(th * (SOFT_CAP * LOG2E))
                        if mask is not None:
                            e = jnp.where(mask[n // 2][:, cols], e, 0.0)
                        eb = e.astype(BF)
                        e_s[rows, cols] = eb
                        w_s[rows, cols] = (e * (1.0 - th * th)).astype(BF)
                        heads.append(eb)
                    parts.append(heads)
                for head in range(2):
                    cols = slice(head * TILE, (head + 1) * TILE)
                    column = jnp.concatenate([p[head] for p in parts], axis=0)
                    o_acc[:, cols] += nn(turned_of(vt_s, turned), column)

            gap = query_iota - key_iota
            key_pos = key_iota + qt * TILE
            oldest_there = first_shard + r >= 0
            edge_mask = (
                gap + 8 * TOK < WINDOW,
                (gap >= 0) & ((key_pos < q_valid) | (gap == 0)),
            )
            old = jnp.where(oldest_there, 4 * r + 2 * qt, EMPTY)
            own = 4 * (8 + r) + 2 * qt
            edge = (old, old + 1, own, own + 1)
            edge_turned = (old, old + 1, OWN + 4 * r + 2 * qt, OWN + 4 * r + 2 * qt + 1)
            o_acc[...] = jnp.zeros_like(o_acc)
            forward(edge, edge_turned, 0, edge_mask)

            def forward_step(width, n, carry):
                pieces = tuple(listed[n * width + m] for m in range(width))
                forward(pieces, pieces, (4 + n * width) * HD, None)
                return carry

            lax.fori_loop(0, doubles, functools.partial(forward_step, 2 * STEP), 0)
            lax.fori_loop(2 * doubles, steps, functools.partial(forward_step, STEP), 0)
            inv = 1.0 / o_acc[HD : HD + 1, :]
            g_rows2 = jnp.concatenate([g_two[:, :HD], g_two[:, HD:]], axis=0).astype(F32)
            live = query_iota[:1, :] + qt * TILE < q_valid
            g_t = jnp.where(live, g_rows2.T, 0.0) * inv
            delta = jnp.sum(g_t * o_acc[:HD, :], axis=0, keepdims=True) * inv
            gs_t = g_t.astype(BF)
            gs = g_t.T.astype(BF)
            dq_acc[...] = jnp.zeros_like(dq_acc)

            def backward(pieces, turned, slot):
                rows = pl.ds(pl.multiple_of(slot, TILE), len(pieces) * HD)
                columns = []
                for head in range(2):
                    cols = slice(head * TILE, (head + 1) * TILE)
                    parts = []
                    for n in range(0, len(pieces), 2):
                        part = pl.ds(pl.multiple_of(slot + n * HD, TILE), TILE)
                        dp = nn(keys_of(1, pieces[n : n + 2]), gs_t[:, cols])
                        parts.append((w_s[part, cols].astype(F32) * (dp - delta[:, cols])).astype(BF))
                    columns.append(jnp.concatenate(parts, axis=0))
                ds = jnp.concatenate(columns, axis=1)
                dq_acc[...] += nn(turned_of(kt_s, turned), ds)
                dk = nn(ds, q_rows2)
                dv = nn(e_s[rows, :], gs)
                for n, p in enumerate(pieces):
                    dk_acc[p] += dk[n * HD : (n + 1) * HD]
                    dv_acc[p] += dv[n * HD : (n + 1) * HD]

            backward(edge, edge_turned, 0)

            def backward_step(width, n, carry):
                pieces = tuple(listed[n * width + m] for m in range(width))
                backward(pieces, pieces, (4 + n * width) * HD)
                return carry

            lax.fori_loop(0, doubles, functools.partial(backward_step, 2 * STEP), 0)
            lax.fori_loop(2 * doubles, steps, functools.partial(backward_step, STEP), 0)
            dq = dq_acc[...] * SCALE
            c, s = cos[r, :, lanes], sin[r, :, lanes]
            for head in range(2):
                a = dq[: HD // 2, head * TILE : (head + 1) * TILE]
                z = dq[HD // 2 :, head * TILE : (head + 1) * TILE]
                dq_out[r, head * HD : head * HD + HD // 2, lanes] = (a * c + z * s).astype(BF)
                dq_out[r, head * HD + HD // 2 : (head + 1) * HD, lanes] = (z * c - a * s).astype(BF)

        return carry

    lax.fori_loop(0, 4, query_tile, 0)

    def result(ref, b, k, scale):
        live = lax.broadcasted_iota(jnp.int32, (HD, HD), 0) + k * HD < valid_of(b)
        return jnp.where(live, ref[4 * b + k] * scale, 0.0)

    def give(b, carry):
        for k in range(4):
            rows = slice(k * HD, (k + 1) * HD)
            dkv_out[b, 0, rows, :] = result(dk_acc, b, k, SCALE).astype(BF)
            dkv_out[b, 1, rows, :] = result(dv_acc, b, k, 1.0).astype(BF)
        return carry

    lax.fori_loop(0, 8, give, 0)
    for r in range(2):
        for k in range(4):
            rows = slice(k * HD, (k + 1) * HD)
            own_out[r, 0, rows, :] = result(dk_acc, 8 + r, k, SCALE)
            own_out[r, 1, rows, :] = result(dv_acc, 8 + r, k, 1.0)


def attend(valid_len, base, qg, kv, cos, sin):
    vmem = pl.BlockSpec(memory_space=pltpu.VMEM)
    smem = pl.BlockSpec(memory_space=pltpu.SMEM)
    return pl.pallas_call(
        attend_kernel,
        out_shape=(
            jax.ShapeDtypeStruct((2, 2 * HD, TOK), BF),
            jax.ShapeDtypeStruct((8, 2, TOK, HD), BF),
            jax.ShapeDtypeStruct((2, 2, TOK, HD), F32),
        ),
        in_specs=[smem, smem, vmem, pl.BlockSpec(memory_space=pltpu.HBM), vmem, vmem],
        out_specs=(vmem,) * 3,
        scratch_shapes=[
            pltpu.VMEM((NB + STEP // 4, 2, 4, HD, HD), BF),
            pltpu.VMEM((44 * HD, 2 * TILE), BF),
            pltpu.VMEM((44 * HD, 2 * TILE), BF),
            pltpu.VMEM((OWN + 8, HD, HD), BF),
            pltpu.VMEM((OWN + 8, HD + 16, HD), BF),
            pltpu.VMEM((HD + 16, 2 * TILE), F32),
            pltpu.VMEM((HD, 2 * TILE), F32),
            pltpu.VMEM((PIECES + STEP, HD, HD), F32),
            pltpu.VMEM((PIECES + STEP, HD, HD), F32),
            pltpu.SMEM((48,), jnp.int32),
            pltpu.SemaphoreType.DMA,
        ],
        compiler_params=pltpu.CompilerParams(vmem_limit_bytes=58 << 20),
        name="attend",
    )(valid_len, base, qg, kv.reshape(NB, 2, 4, HD, HD), cos, sin)


PIECE = 256


def finish_kernel(
    dq, dkv, own_hbm, turned_hbm, wq, w_all, cos, sin, gx_out, gw_out,
    own, n_buf, w_buf, wkv_buf, t_buf, d_buf, dkv_t, g_buf, y_buf, x_buf, near, far,
    xs, xr, zs, zr, xy, zy, half_buf,
    load_sem, dq_sems, dk_sems, y_sems, x_sems, ring_send, ring_recv, pair_sems, core_sems, g_send, g_recv,
):
    x, yh, core, z, yl = here()
    other = 1 - core
    partner = at_seq(x, yh, other)
    across = at_seq(x, 1 - yh, core)
    beside = at_head(z, 1 - yl)
    x_next, x_prev, x_far = at_seq(x + 1, yh, core), at_seq(x - 1, yh, core), at_seq(x + 2, yh, core)
    z_next, z_prev = at_head(z + 1, yl), at_head(z - 1, yl)
    round_z = [[at_core(z + step, yl, c) for c in range(2)] for step in STEPS]
    greet([partner, across, beside, x_next, x_prev, x_far] + sum(round_z, []))

    y_copies = [
        [
            remote(dkv.at[6 - 4 * i + r], y_buf.at[i, r], y_sems.at[0, i, r], y_sems.at[1, i, r], across)
            for r in range(2)
        ]
        for i in range(2)
    ]
    for copy in y_copies[1] + y_copies[0]:
        copy.start()
    pairs = [
        (dkv.at[pl.ds(0, 2)], far),
        (dkv.at[pl.ds(4, 2)], near),
        (wq, w_buf),
        (dq.at[0], t_buf.at[: 2 * HD, :TOK]),
        (dq.at[1], t_buf.at[: 2 * HD, TOK:]),
        (turned_hbm.at[0], n_buf.at[:, :TOK]),
        (turned_hbm.at[1], n_buf.at[:, TOK:]),
        (own_hbm, own),
    ] + [
        (w_all.at[i, kind], wkv_buf.at[i, :, kind * 2 * HD : (kind + 1) * 2 * HD])
        for i in range(4)
        for kind in range(2)
    ]
    loads = [pltpu.make_async_copy(src, dst, load_sem.at[i]) for i, (src, dst) in enumerate(pairs)]
    for copy in loads:
        copy.start()
    head_rows = pl.ds(pl.multiple_of(core * 2 * HD, 2 * HD), 2 * HD)
    dq_swap = remote(dq.at[other], d_buf.at[head_rows], dq_sems.at[0], dq_sems.at[1], partner)
    dq_keep = pltpu.make_async_copy(dq.at[core], d_buf.at[head_rows], dq_sems.at[2])
    back_near, back_far = (
        [
            remote(src.at[r], x_buf.at[i, r], x_sems.at[0, i, r], x_sems.at[1, i, r], device)
            for r in range(2)
        ]
        for i, (src, device) in enumerate(((near, x_prev), (far, x_far)))
    )
    loads[0].wait()

    @pl.when(yh == 0)
    def _():
        for copy in back_far:
            copy.start()

    dq_swap.start()
    dq_keep.start()
    for copy in loads[1:3]:
        copy.wait()
    dq_keep.wait()
    dq_swap.wait()

    send, recv = (xs, zs), (xr, zr)
    ahead, behind = (x_next, z_next), (x_prev, z_prev)
    place = (x, z)

    def term(axis, piece, rows):
        part = slice(piece * PIECE, (piece + 1) * PIECE)
        if axis == 0:
            return nt(n_buf[rows, :], t_buf[part, :])
        return nn(w_buf[rows, :], d_buf[:, part])

    def compute(job, slot, step):
        axis, piece = job
        first_row = lax.rem(place[axis] + step, 4) * CHUNK

        def one(half, carry):
            to = pl.ds(pl.multiple_of(half * HALF, HALF), HALF)
            rows = pl.ds(pl.multiple_of(first_row + half * HALF, HALF), HALF)
            send[axis][piece, slot, to, :] = term(axis, piece, rows).astype(BF)
            return carry

        lax.fori_loop(0, 2, one, 0)

    def ring(job):
        axis, piece = job
        out, come = send[axis].at[piece], recv[axis].at[piece]
        top, low = pl.ds(0, HALF), pl.ds(HALF, HALF)
        spans = (
            (out.at[0, top], come.at[0, top], ahead[axis]),
            (out.at[0, low], come.at[0, low], behind[axis]),
            (out.at[1], come.at[1], ahead[axis]),
            (out.at[2], come.at[2], behind[axis]),
        )
        return [
            remote(src, dst, ring_send.at[axis, piece, i], ring_recv.at[axis, piece, i], device)
            for i, (src, dst, device) in enumerate(spans)
        ]

    x0, x1, z0, z1 = jobs = ((0, 0), (0, 1), (1, 0), (1, 1))
    rings = {job: ring(job) for job in jobs}

    def launch(job):
        compute(job, 0, 2)
        rings[job][0].start()
        rings[job][1].start()

    def prepare(job):
        compute(job, 1, 1)
        compute(job, 2, 3)

    def relay(job):
        axis, piece = job
        for way, rows in ((0, slice(0, HALF)), (1, slice(HALF, CHUNK))):
            rings[job][way].wait()
            mine = send[axis][piece, 1 + way, rows, :].astype(F32)
            send[axis][piece, 1 + way, rows, :] = (
                mine + recv[axis][piece, 0, rows, :].astype(F32)
            ).astype(BF)
            rings[job][2 + way].start()

    side, side_device, pair_buf = (yh, yl), (across, beside), (xy, zy)

    def pair(job):
        axis, piece = job
        buf = pair_buf[axis].at[piece]
        return remote(
            buf.at[0], buf.at[1], pair_sems.at[0, axis, piece], pair_sems.at[1, axis, piece], side_device[axis]
        )

    pairs_of = {job: pair(job) for job in jobs}

    def keys_part(piece, rows):
        total = jnp.zeros((HALF, PIECE), F32)
        for i in range(4):
            found = [
                g_buf[i, head, piece, kind * HD : (kind + 1) * HD, :] for kind in range(2) for head in range(2)
            ]
            total += nn(wkv_buf[i, rows, :], jnp.concatenate(found, axis=0))
        return total

    def cross(job):
        axis, piece = job
        rings[job][2].wait()
        rings[job][3].wait()

        def summed(half):
            rows = pl.ds(pl.multiple_of(half * HALF, HALF), HALF)
            total = (
                send[axis][piece, 3, rows, :].astype(F32)
                + recv[axis][piece, 1, rows, :].astype(F32)
                + recv[axis][piece, 2, rows, :].astype(F32)
            )
            if axis == 1:
                total += keys_part(piece, rows)
            return total.astype(BF)

        pair_buf[axis][piece, 0] = summed(1 - side[axis])
        pairs_of[job].start()
        pair_buf[axis][piece, 2] = summed(side[axis])

    def total_of(job):
        axis, piece = job
        pairs_of[job].wait()
        return (pair_buf[axis][piece, 1].astype(F32) + pair_buf[axis][piece, 2].astype(F32)).astype(BF)

    my_rows = pl.ds(pl.multiple_of(core * QTR, QTR), QTR)
    its_rows = pl.ds(pl.multiple_of(other * QTR, QTR), QTR)
    lasts = [
        remote(half_buf.at[piece, its_rows], gw_out.at[piece, core], core_sems.at[0, piece], core_sems.at[1, piece], partner)
        for piece in range(2)
    ]

    def swap(piece):
        half_buf[piece] = total_of((0, piece))
        lasts[piece].start()
        gw_out[piece, core] = half_buf[piece, my_rows, :]


    def add_to(ref, index, r):
        ref[r] = (ref[r].astype(F32) + y_buf[index, r].astype(F32)).astype(BF)

    def further(r):
        y_copies[1][r].wait()

        @pl.when(yh == 0)
        def _():
            add_to(near, 1, r)
            back_near[r].start()

        @pl.when(yh == 1)
        def _():
            add_to(far, 1, r)
            back_far[r].start()

    def nearer(r):
        y_copies[0][r].wait()

        @pl.when(yh == 1)
        def _():
            add_to(near, 0, r)
            back_near[r].start()

    launch(z0)
    launch(z1)
    prepare(z0)
    prepare(z1)
    for r in range(2):
        further(r)
    relay(z0)
    relay(z1)
    for r in range(2):
        nearer(r)
    for copy in loads[3:]:
        copy.wait()
    launch(x0)
    prepare(x0)
    for job in (z0, z1, x0):
        compute(job, 3, 0)
    keep = (yh == 0).astype(F32)
    for copy in back_far + back_near:
        copy.wait()
    for r in range(2):
        for kind in range(2):
            total = (
                own[r, kind]
                + y_buf[0, r, kind].astype(F32) * keep
                + x_buf[0, r, kind].astype(F32)
                + x_buf[1, r, kind].astype(F32)
            ).T
            if kind == 0:
                a, b = total[: HD // 2, :], total[HD // 2 :, :]
                c, s = cos[r], sin[r]
                total = jnp.concatenate([a * c + b * s, b * c - a * s], axis=0)
            total = total.astype(BF)
            t_buf[(2 + kind) * HD : (3 + kind) * HD, r * TOK : (r + 1) * TOK] = total
            for piece in range(2):
                dkv_t[r, piece, kind * HD : (kind + 1) * HD, :] = total[:, piece * PIECE : (piece + 1) * PIECE]
    spread = [
        [
            remote(dkv_t.at[r, piece], g_buf.at[z, core, piece], g_send.at[i, r, piece], g_recv.at[i, core, piece], round_z[i][r])
            for i in range(3)
            for r in range(2)
        ]
        for piece in range(2)
    ]
    kin = [
        remote(dkv_t.at[other, piece], g_buf.at[z, core, piece], dk_sems.at[0, piece], dk_sems.at[1, piece], partner)
        for piece in range(2)
    ]
    for piece in range(2):
        for copy in spread[piece] + [kin[piece]]:
            copy.start()
        g_buf[z, core, piece] = dkv_t[core, piece]

    def gathered(piece):
        kin[piece].wait()
        for i, step in enumerate(STEPS):
            for head in range(2):
                come = g_buf.at[lax.rem(z + 4 - step, 4), head, piece]
                remote(come, come, g_send.at[i, head, piece], g_recv.at[i, head, piece], partner).wait_recv()

    launch(x1)
    relay(x0)
    prepare(x1)
    compute(x1, 3, 0)
    relay(x1)
    gathered(0)
    cross(z0)
    cross(x0)
    gathered(1)
    cross(z1)
    swap(0)
    cross(x1)
    gx_out[:, :PIECE] = total_of(z0)
    swap(1)
    gx_out[:, PIECE:] = total_of(z1)
    for copy in lasts:
        copy.wait()
    for piece in range(2):
        for copy in spread[piece]:
            copy.wait_send()


def finish(dq, dkv, own, turned, wq, w_all, cos, sin):
    vmem = pl.BlockSpec(memory_space=pltpu.VMEM)
    hbm = pl.BlockSpec(memory_space=pltpu.HBM)
    any_space = pl.BlockSpec(memory_space=pl.ANY)
    dma = pltpu.SemaphoreType.DMA
    return pl.pallas_call(
        finish_kernel,
        out_shape=(
            jax.ShapeDtypeStruct((HALF, TOK), BF),
            jax.ShapeDtypeStruct((2, 2, QTR, PIECE), BF),
        ),
        in_specs=[any_space] * 3 + [hbm] * 3 + [vmem, vmem],
        out_specs=(vmem,) * 2,
        scratch_shapes=[
            pltpu.VMEM((2, 2, TOK, HD), F32),
            pltpu.VMEM((D, 2 * TOK), BF),
            pltpu.VMEM((D, 4 * HD), BF),
            pltpu.VMEM((4, CHUNK, 4 * HD), BF),
            pltpu.VMEM((4 * HD, 2 * TOK), BF),
            pltpu.VMEM((4 * HD, TOK), BF),
            pltpu.VMEM((2, 2, 2 * HD, PIECE), BF),
            pltpu.VMEM((4, 2, 2, 2 * HD, PIECE), BF),
            pltpu.VMEM((2, 2, 2, TOK, HD), BF),
            pltpu.VMEM((2, 2, 2, TOK, HD), BF),
            pltpu.VMEM((2, 2, TOK, HD), BF),
            pltpu.VMEM((2, 2, TOK, HD), BF),
            pltpu.VMEM((2, 4, CHUNK, PIECE), BF),
            pltpu.VMEM((2, 3, CHUNK, PIECE), BF),
            pltpu.VMEM((2, 4, CHUNK, PIECE), BF),
            pltpu.VMEM((2, 3, CHUNK, PIECE), BF),
            pltpu.VMEM((2, 3, HALF, PIECE), BF),
            pltpu.VMEM((2, 3, HALF, PIECE), BF),
            pltpu.VMEM((2, HALF, PIECE), BF),
            dma((16,)), dma((3,)), dma((2, 2)), dma((2, 2, 2)), dma((2, 2, 2)),
            dma((2, 2, 4)), dma((2, 2, 4)), dma((2, 2, 2)), dma((2, 2)), dma((3, 2, 2)), dma((3, 2, 2)),
        ],
        compiler_params=pltpu.CompilerParams(
            collective_id=1, has_side_effects=True, vmem_limit_bytes=58 << 20
        ),
        name="finish",
    )(dq, dkv, own, turned, wq, w_all, cos, sin)


def emit_kernel(gx, gw, gx_out, gq_out, gk_out, gv_out):
    gx_out[...] = gx[...]
    for head in range(2):
        gq_out[:, head * 2 * HD : (head + 1) * 2 * HD] = gw[0, head]
        gk_out[:, head * HD : (head + 1) * HD] = gw[1, head, :, :HD]
        gv_out[:, head * HD : (head + 1) * HD] = gw[1, head, :, HD:]


def emit(gx, gw):
    vmem = pl.BlockSpec(memory_space=pltpu.VMEM)
    return pl.pallas_call(
        emit_kernel,
        out_shape=(
            jax.ShapeDtypeStruct((HALF, TOK), BF),
            jax.ShapeDtypeStruct((QTR, 4 * HD), BF),
            jax.ShapeDtypeStruct((QTR, 2 * HD), BF),
            jax.ShapeDtypeStruct((QTR, 2 * HD), BF),
        ),
        in_specs=[vmem] * 2,
        out_specs=(vmem,) * 4,
        name="emit",
    )(gx, gw)


def body(queries, keys, values, out_grad, normed, w_query, w_key, w_value, valid_len):
    chip = lax.axis_index("seq") // 2
    inverse_freq = ROPE_BASE ** (-(jnp.arange(HD // 2, dtype=F32) * (2.0 / HD)))
    slots = (chip * 2 * TOK + jnp.arange(2 * TOK, dtype=jnp.int32)).astype(F32).reshape(2, 1, TOK)
    angles = slots * inverse_freq[None, :, None]
    cos, sin = jnp.cos(angles), jnp.sin(angles)
    base = (2 * chip - 8).astype(jnp.int32).reshape(1)
    qg, kv, turned, w_all = gather(queries, keys, values, out_grad, normed, w_key, w_value)
    dq, dkv, own = attend(valid_len, base, qg, kv, cos, sin)
    gx, gq, gk, gv = emit(*finish(dq, dkv, own, turned, w_query, w_all, cos, sin))
    return gx.T, gq, gk, gv


def solution(mesh):
    both = P("seq", "head")
    placed = (both, both, both, both, P("seq", None), P(None, "head"), P(None, "head"), P(None, "head"), P())
    return jax.shard_map(
        body, mesh=mesh, in_specs=placed, out_specs=(both,) * 4, check_vma=False
    )
```

```python
import functools

import jax
import jax.numpy as jnp
from jax import lax
from jax.experimental import pallas as pl
from jax.experimental.pallas import tpu as pltpu
from jax.sharding import PartitionSpec as P

D = 4608
H = 32
HD = 128
WINDOW = 4096
SOFT_CAP = 50.0
ROPE_BASE = 10000.0
SCALE = (D // H) ** (-0.5)

TOK = 512
NB = 10
TILE = 256
CHUNK = D // 4
HALF = CHUNK // 2
QTR = HALF // 2

BF = jnp.bfloat16
F32 = jnp.float32
MESH = pl.DeviceIdType.MESH
STEPS = (1, -1, 2)
LOG2E = 1.4426950408889634


def nt(left, right):
    return lax.dot_general(left, right, (((1,), (1,)), ((), ())), preferred_element_type=F32)


def nn(left, right):
    return lax.dot_general(left, right, (((1,), (0,)), ((), ())), preferred_element_type=F32)


def here():
    s, h = lax.axis_index("seq"), lax.axis_index("head")
    return s // 4, (s // 2) % 2, s % 2, h // 2, h % 2


def at_seq(x, yh, core):
    return {"seq": (lax.rem(x + 4, 4) * 2 + yh) * 2 + core, "head": lax.axis_index("head")}


def at_head(z, yl):
    return {"seq": lax.axis_index("seq"), "head": lax.rem(z + 4, 4) * 2 + yl}


def at_core(z, yl, core):
    s = lax.axis_index("seq")
    return {"seq": s - s % 2 + core, "head": lax.rem(z + 4, 4) * 2 + yl}


def remote(src, dst, send, recv, device):
    return pltpu.make_async_remote_copy(
        src_ref=src, dst_ref=dst, send_sem=send, recv_sem=recv, device_id=device, device_id_type=MESH
    )


def greet(devices):
    barrier = pltpu.get_barrier_semaphore()
    for device in devices:
        pl.semaphore_signal(barrier, inc=1, device_id=device, device_id_type=MESH)
    pl.semaphore_wait(barrier, len(devices))


def gather_kernel(
    q, g, k, v, n_hbm, qg, kv, nt_out, kv_own, qg_own, n_ref, turned,
    n_load_sem, kv_load, qg_load, kv_loc, qg_loc, swap_send, swap_recv,
    x_send, x_recv, y_send, y_recv, n_sem, n_send, n_recv,
):
    x, yh, core, _, _ = here()
    other = 1 - core
    partner = at_seq(x, yh, other)
    across = at_seq(x, 1 - yh, core)

    def stage(pair, to, width, sems):
        return [
            pltpu.make_async_copy(
                ref.at[:, head * width : (head + 1) * width], to.at[head, kind], sems.at[head, kind]
            )
            for head in range(2)
            for kind, ref in enumerate(pair)
        ]

    kv_stage = stage((k, v), kv_own, HD, kv_load)
    qg_stage = stage((q, g), qg_own, 2 * HD, qg_load)
    n_load = pltpu.make_async_copy(n_hbm, n_ref, n_load_sem)
    for copy in kv_stage + qg_stage + [n_load]:
        copy.start()
    greet(
        [partner, across]
        + [at_seq(x + step, yh, c) for step in (1, -1, 2) for c in range(2)]
    )
    for copy in kv_stage:
        copy.wait()
    along = [
        [
            remote(
                kv_own.at[head],
                kv.at[8 - 4 * step + core],
                x_send.at[step - 1, head],
                x_recv.at[step - 1, core],
                at_seq(x + step, yh, head),
            )
            for head in range(2)
        ]
        for step in (1, 2)
    ]
    kv_swap = remote(kv_own.at[other], kv.at[8 + core], swap_send.at[0], swap_recv.at[0], partner)
    kv_keep = pltpu.make_async_copy(kv_own.at[core], kv.at[8 + core], kv_loc)
    qg_swap = remote(qg_own.at[other], qg.at[core], swap_send.at[1], swap_recv.at[1], partner)
    qg_keep = pltpu.make_async_copy(qg_own.at[core], qg.at[core], qg_loc)
    kv_swap.start()
    kv_keep.start()
    for copy in along[0] + along[1]:
        copy.start()

    def arrived(step, c):
        dst = kv.at[8 - 4 * step + c]
        remote(dst, dst, x_send.at[step - 1, c], x_recv.at[step - 1, c], partner).wait_recv()

    def turn(i, carry):
        cols = pl.ds(pl.multiple_of(i * HD, HD), HD)
        turned[cols, :] = n_ref[:, cols].T
        return carry

    first_src = jnp.where(yh == 0, 8, 4)
    second_src = jnp.where(yh == 0, 4, 0)
    first = [
        remote(kv.at[first_src + c], kv.at[6 + c], y_send.at[0, c], y_recv.at[0, c], across)
        for c in range(2)
    ]
    second = [
        remote(kv.at[second_src + c], kv.at[2 + c], y_send.at[1, c], y_recv.at[1, c], across)
        for c in range(2)
    ]
    kv_keep.wait()
    kv_swap.wait_recv()

    @pl.when(yh == 0)
    def _():
        for copy in first:
            copy.start()

    for copy in qg_stage:
        copy.wait()
    qg_swap.start()
    qg_keep.start()
    n_load.wait()
    lax.fori_loop(0, D // HD // 2, turn, 0)
    for c in range(2):
        arrived(1, c)

        @pl.when(yh == 0)
        def _():
            second[c].start()

        @pl.when(yh == 1)
        def _():
            first[c].start()

    lax.fori_loop(D // HD // 2, D // HD, turn, 0)
    n_local = pltpu.make_async_copy(turned, nt_out.at[core], n_sem)
    n_swap = remote(turned, nt_out.at[core], n_send, n_recv, partner)
    n_local.start()
    n_swap.start()
    for c in range(2):
        arrived(2, c)

        @pl.when(yh == 1)
        def _():
            second[c].start()

    n_local.wait()
    n_swap.wait()
    qg_keep.wait()
    qg_swap.wait()
    for copy in first + second:
        copy.wait()
    kv_swap.wait_send()
    for copy in along[0] + along[1]:
        copy.wait_send()


def gather(queries, keys, values, grads, normed):
    hbm = pl.BlockSpec(memory_space=pltpu.HBM)
    dma = pltpu.SemaphoreType.DMA
    return pl.pallas_call(
        gather_kernel,
        out_shape=(
            jax.ShapeDtypeStruct((2, 2, TOK, 2 * HD), BF),
            jax.ShapeDtypeStruct((NB, 2, TOK, HD), BF),
            jax.ShapeDtypeStruct((2, D, TOK), BF),
        ),
        in_specs=[hbm] * 5,
        out_specs=(hbm,) * 3,
        scratch_shapes=[
            pltpu.VMEM((2, 2, TOK, HD), BF),
            pltpu.VMEM((2, 2, TOK, 2 * HD), BF),
            pltpu.VMEM((TOK, D), BF),
            pltpu.VMEM((D, TOK), BF),
            dma, dma((2, 2)), dma((2, 2)), dma, dma, dma((2,)), dma((2,)),
            dma((2, 2)), dma((2, 2)), dma((2, 2)), dma((2, 2)), dma, dma, dma,
        ],
        compiler_params=pltpu.CompilerParams(
            collective_id=0, has_side_effects=True, vmem_limit_bytes=60 << 20
        ),
        name="gather",
    )(queries, grads, keys, values, normed)


STEP = 8
PIECES = 4 * NB
EMPTY = PIECES
OWN = PIECES + STEP


def attend_kernel(
    valid, base, qg, kv_hbm, cos, sin, dq_out, dkv_out, own_out,
    kv, e_s, w_s, kt_s, vt_s, o_acc, dq_acc, dk_acc, dv_acc, listed, sem,
):
    first_shard = base[0]
    load = pltpu.make_async_copy(kv_hbm, kv.at[pl.ds(0, NB)], sem)
    load.start()
    dk_acc[...] = jnp.zeros_like(dk_acc)
    dv_acc[...] = jnp.zeros_like(dv_acc)
    for k in range(STEP):
        kv[NB + k // 4, 0, k % 4] = jnp.zeros((HD, HD), BF)
        kv[NB + k // 4, 1, k % 4] = jnp.zeros((HD, HD), BF)
        kt_s[EMPTY + k] = jnp.zeros((HD, HD), BF)
        vt_s[EMPTY + k] = jnp.zeros((HD + 16, HD), BF)
    load.wait()

    def valid_of(b):
        return valid[jnp.maximum(first_shard + b, 0)]

    def turn(b, carry):
        for k in range(4):
            live = lax.broadcasted_iota(jnp.int32, (HD + 16, HD), 1) + k * HD < valid_of(b)
            k_t = kv[b, 0, k].T
            v_t = jnp.concatenate([kv[b, 1, k].T, jnp.ones((16, HD), BF)], axis=0)
            kt_s[4 * b + k] = jnp.where(live[:HD], k_t.astype(F32), 0.0).astype(BF)
            vt_s[4 * b + k] = jnp.where(live, v_t.astype(F32), 0.0).astype(BF)

            @pl.when(b >= 8)
            def _():
                kt_s[OWN + 4 * (b - 8) + k] = k_t
                vt_s[OWN + 4 * (b - 8) + k] = v_t

        return carry

    lax.fori_loop(0, NB, turn, 0)
    key_iota = lax.broadcasted_iota(jnp.int32, (TILE, 2 * TILE), 0)
    query_iota = lax.rem(lax.broadcasted_iota(jnp.int32, (TILE, 2 * TILE), 1), TILE)

    def query_tile(i, carry):
        r, qt = i // 2, lax.rem(i, 2)
        q_valid = valid_of(8 + r)
        q_rows = pl.ds(pl.multiple_of(qt * TILE, TILE), TILE)
        lanes = q_rows

        @pl.when(qt * TILE >= q_valid)
        def _():
            dq_out[r, :, lanes] = jnp.zeros((2 * HD, TILE), BF)

        @pl.when(qt * TILE < q_valid)
        def _():
            def note(t, count):
                j, k = t // 4, lax.rem(t, 4)
                b = r + j
                wanted = (
                    (first_shard + b >= 0)
                    & (k * HD < valid_of(b))
                    & jnp.logical_not((j == 0) & (k < 2 * qt + 2))
                    & jnp.logical_not((j == 8) & (k >= 2 * qt))
                )
                listed[count] = jnp.where(wanted, 4 * b + k, EMPTY)
                return count + wanted.astype(jnp.int32)

            count = lax.fori_loop(0, 36, note, 0)
            for extra in range(STEP - 1):
                listed[count + extra] = EMPTY + extra
            steps = (count + STEP - 1) // STEP
            doubles = steps // 2

            q_two = qg[r, 0, q_rows, :]
            g_two = qg[r, 1, q_rows, :]
            q_rows2 = jnp.concatenate([q_two[:, :HD], q_two[:, HD:]], axis=0)
            q_t = q_rows2.T

            def keys_of(kind, pieces):
                return jnp.concatenate([kv[p // 4, kind, lax.rem(p, 4)] for p in pieces], axis=0)

            def turned_of(ref, pieces):
                return jnp.concatenate([ref[p] for p in pieces], axis=1)

            def forward(pieces, turned, slot, mask):
                parts = []
                for n in range(0, len(pieces), 2):
                    keys = keys_of(0, pieces[n : n + 2])
                    rows = pl.ds(pl.multiple_of(slot + n * HD, TILE), TILE)
                    heads = []
                    for head in range(2):
                        cols = slice(head * TILE, (head + 1) * TILE)
                        th = jnp.tanh(nn(keys, q_t[:, cols]) * (SCALE / SOFT_CAP))
                        e = jnp.exp2(th * (SOFT_CAP * LOG2E))
                        if mask is not None:
                            e = jnp.where(mask[n // 2][:, cols], e, 0.0)
                        eb = e.astype(BF)
                        e_s[rows, cols] = eb
                        w_s[rows, cols] = (e * (1.0 - th * th)).astype(BF)
                        heads.append(eb)
                    parts.append(heads)
                for head in range(2):
                    cols = slice(head * TILE, (head + 1) * TILE)
                    column = jnp.concatenate([p[head] for p in parts], axis=0)
                    o_acc[:, cols] += nn(turned_of(vt_s, turned), column)

            gap = query_iota - key_iota
            key_pos = key_iota + qt * TILE
            oldest_there = first_shard + r >= 0
            edge_mask = (
                gap + 8 * TOK < WINDOW,
                (gap >= 0) & ((key_pos < q_valid) | (gap == 0)),
            )
            old = jnp.where(oldest_there, 4 * r + 2 * qt, EMPTY)
            own = 4 * (8 + r) + 2 * qt
            edge = (old, old + 1, own, own + 1)
            edge_turned = (old, old + 1, OWN + 4 * r + 2 * qt, OWN + 4 * r + 2 * qt + 1)
            o_acc[...] = jnp.zeros_like(o_acc)
            forward(edge, edge_turned, 0, edge_mask)

            def forward_step(width, n, carry):
                pieces = tuple(listed[n * width + m] for m in range(width))
                forward(pieces, pieces, (4 + n * width) * HD, None)
                return carry

            lax.fori_loop(0, doubles, functools.partial(forward_step, 2 * STEP), 0)
            lax.fori_loop(2 * doubles, steps, functools.partial(forward_step, STEP), 0)
            inv = 1.0 / o_acc[HD : HD + 1, :]
            g_rows2 = jnp.concatenate([g_two[:, :HD], g_two[:, HD:]], axis=0).astype(F32)
            live = query_iota[:1, :] + qt * TILE < q_valid
            g_t = jnp.where(live, g_rows2.T, 0.0) * inv
            delta = jnp.sum(g_t * o_acc[:HD, :], axis=0, keepdims=True) * inv
            gs_t = g_t.astype(BF)
            gs = g_t.T.astype(BF)
            dq_acc[...] = jnp.zeros_like(dq_acc)

            def backward(pieces, turned, slot):
                rows = pl.ds(pl.multiple_of(slot, TILE), len(pieces) * HD)
                columns = []
                for head in range(2):
                    cols = slice(head * TILE, (head + 1) * TILE)
                    parts = []
                    for n in range(0, len(pieces), 2):
                        part = pl.ds(pl.multiple_of(slot + n * HD, TILE), TILE)
                        dp = nn(keys_of(1, pieces[n : n + 2]), gs_t[:, cols])
                        parts.append((w_s[part, cols].astype(F32) * (dp - delta[:, cols])).astype(BF))
                    columns.append(jnp.concatenate(parts, axis=0))
                ds = jnp.concatenate(columns, axis=1)
                dq_acc[...] += nn(turned_of(kt_s, turned), ds)
                dk = nn(ds, q_rows2)
                dv = nn(e_s[rows, :], gs)
                for n, p in enumerate(pieces):
                    dk_acc[p] += dk[n * HD : (n + 1) * HD]
                    dv_acc[p] += dv[n * HD : (n + 1) * HD]

            backward(edge, edge_turned, 0)

            def backward_step(width, n, carry):
                pieces = tuple(listed[n * width + m] for m in range(width))
                backward(pieces, pieces, (4 + n * width) * HD)
                return carry

            lax.fori_loop(0, doubles, functools.partial(backward_step, 2 * STEP), 0)
            lax.fori_loop(2 * doubles, steps, functools.partial(backward_step, STEP), 0)
            dq = dq_acc[...] * SCALE
            c, s = cos[r, :, lanes], sin[r, :, lanes]
            for head in range(2):
                a = dq[: HD // 2, head * TILE : (head + 1) * TILE]
                z = dq[HD // 2 :, head * TILE : (head + 1) * TILE]
                dq_out[r, head * HD : head * HD + HD // 2, lanes] = (a * c + z * s).astype(BF)
                dq_out[r, head * HD + HD // 2 : (head + 1) * HD, lanes] = (z * c - a * s).astype(BF)

        return carry

    lax.fori_loop(0, 4, query_tile, 0)

    def result(ref, b, k, scale):
        live = lax.broadcasted_iota(jnp.int32, (HD, HD), 0) + k * HD < valid_of(b)
        return jnp.where(live, ref[4 * b + k] * scale, 0.0)

    def give(b, carry):
        for k in range(4):
            rows = slice(k * HD, (k + 1) * HD)
            dkv_out[b, 0, rows, :] = result(dk_acc, b, k, SCALE).astype(BF)
            dkv_out[b, 1, rows, :] = result(dv_acc, b, k, 1.0).astype(BF)
        return carry

    lax.fori_loop(0, 8, give, 0)
    for r in range(2):
        for k in range(4):
            rows = slice(k * HD, (k + 1) * HD)
            own_out[r, 0, rows, :] = result(dk_acc, 8 + r, k, SCALE)
            own_out[r, 1, rows, :] = result(dv_acc, 8 + r, k, 1.0)


def attend(valid_len, base, qg, kv, cos, sin):
    vmem = pl.BlockSpec(memory_space=pltpu.VMEM)
    smem = pl.BlockSpec(memory_space=pltpu.SMEM)
    return pl.pallas_call(
        attend_kernel,
        out_shape=(
            jax.ShapeDtypeStruct((2, 2 * HD, TOK), BF),
            jax.ShapeDtypeStruct((8, 2, TOK, HD), BF),
            jax.ShapeDtypeStruct((2, 2, TOK, HD), F32),
        ),
        in_specs=[smem, smem, vmem, pl.BlockSpec(memory_space=pltpu.HBM), vmem, vmem],
        out_specs=(vmem,) * 3,
        scratch_shapes=[
            pltpu.VMEM((NB + STEP // 4, 2, 4, HD, HD), BF),
            pltpu.VMEM((44 * HD, 2 * TILE), BF),
            pltpu.VMEM((44 * HD, 2 * TILE), BF),
            pltpu.VMEM((OWN + 8, HD, HD), BF),
            pltpu.VMEM((OWN + 8, HD + 16, HD), BF),
            pltpu.VMEM((HD + 16, 2 * TILE), F32),
            pltpu.VMEM((HD, 2 * TILE), F32),
            pltpu.VMEM((PIECES + STEP, HD, HD), F32),
            pltpu.VMEM((PIECES + STEP, HD, HD), F32),
            pltpu.SMEM((48,), jnp.int32),
            pltpu.SemaphoreType.DMA,
        ],
        compiler_params=pltpu.CompilerParams(vmem_limit_bytes=58 << 20),
        cost_estimate=pl.CostEstimate(flops=26_000_000_000, bytes_accessed=8 << 20, transcendentals=20_000_000),
        name="attend",
    )(valid_len, base, qg, kv.reshape(NB, 2, 4, HD, HD), cos, sin)


PIECE = 256


def finish_kernel(
    dq, dkv, own_hbm, turned_hbm, wq, wk, wv, w_near, w_back, w_far, cos, sin, gx_out, gw_out,
    own, n_buf, w_buf, t_buf, dkv_t, gq_buf, g_buf, zq_buf, y_buf, x_buf, near, far,
    xs, xr, xy, zy, half_buf,
    load_sem, dq_sems, dk_sems, y_sems, x_sems, ring_send, ring_recv, pair_sems, core_sems, g_send, g_recv,
    gq_send, gq_recv, w_load, w_send, w_recv,
):
    x, yh, core, z, yl = here()
    other = 1 - core
    partner = at_seq(x, yh, other)
    across = at_seq(x, 1 - yh, core)
    beside = at_head(z, 1 - yl)
    x_next, x_prev, x_far = at_seq(x + 1, yh, core), at_seq(x - 1, yh, core), at_seq(x + 2, yh, core)
    round_z = [[at_core(z + step, yl, c) for c in range(2)] for step in STEPS]
    greet([partner, across, beside, x_next, x_prev, x_far] + sum(round_z, []))

    y_copies = [
        [
            remote(dkv.at[6 - 4 * i + r], y_buf.at[i, r], y_sems.at[0, i, r], y_sems.at[1, i, r], across)
            for r in range(2)
        ]
        for i in range(2)
    ]
    for copy in y_copies[1] + y_copies[0]:
        copy.start()
    pairs = [
        (dkv.at[pl.ds(0, 2)], far),
        (dkv.at[pl.ds(4, 2)], near),
        (dq.at[0], t_buf.at[: 2 * HD, :TOK]),
        (dq.at[1], t_buf.at[: 2 * HD, TOK:]),
        (turned_hbm.at[0], n_buf.at[:, :TOK]),
        (turned_hbm.at[1], n_buf.at[:, TOK:]),
        (own_hbm, own),
    ]
    loads = [pltpu.make_async_copy(src, dst, load_sem.at[i]) for i, (src, dst) in enumerate(pairs)]
    for copy in loads:
        copy.start()
    q_spread = [
        remote(dq.at[r], gq_buf.at[i, core], gq_send.at[i, r], gq_recv.at[i, core], round_z[i][r])
        for i in range(3)
        for r in range(2)
    ]
    q_kin = remote(dq.at[other], gq_buf.at[3, core], dq_sems.at[0], dq_sems.at[1], partner)
    q_keep = pltpu.make_async_copy(dq.at[core], gq_buf.at[3, core], dq_sems.at[2])
    part = pl.ds(pl.multiple_of(core * HALF, HALF), HALF)
    own_rows = pl.ds(pl.multiple_of(z * CHUNK, CHUNK), CHUNK)
    w_in = [
        pltpu.make_async_copy(src, w_buf.at[i, part], w_load.at[i])
        for i, src in enumerate((w_near, w_back, w_far))
    ] + [
        pltpu.make_async_copy(ref.at[own_rows], w_buf.at[3, :, cols], w_load.at[3 + i])
        for i, (ref, cols) in enumerate(
            ((wq, slice(0, 4 * HD)), (wk, slice(4 * HD, 6 * HD)), (wv, slice(6 * HD, 8 * HD)))
        )
    ]
    w_on = [
        remote(src, w_buf.at[i, part], w_send.at[i], w_recv.at[i], partner)
        for i, src in enumerate((w_near, w_back, w_far))
    ]
    back_near, back_far = (
        [
            remote(src.at[r], x_buf.at[i, r], x_sems.at[0, i, r], x_sems.at[1, i, r], device)
            for r in range(2)
        ]
        for i, (src, device) in enumerate(((near, x_prev), (far, x_far)))
    )
    loads[0].wait()

    @pl.when(yh == 0)
    def _():
        for copy in back_far:
            copy.start()

    for copy in q_spread + [q_kin, q_keep] + w_on + w_in:
        copy.start()
    for copy in loads[1:]:
        copy.wait()

    def term(piece, rows):
        return nt(n_buf[rows, :], t_buf[piece * PIECE : (piece + 1) * PIECE, :])

    def compute(piece, slot, step):
        first_row = lax.rem(x + step, 4) * CHUNK

        def one(half, carry):
            to = pl.ds(pl.multiple_of(half * HALF, HALF), HALF)
            rows = pl.ds(pl.multiple_of(first_row + half * HALF, HALF), HALF)
            xs[piece, slot, to, :] = term(piece, rows).astype(BF)
            return carry

        lax.fori_loop(0, 2, one, 0)

    def ring(piece):
        out, come = xs.at[piece], xr.at[piece]
        top, low = pl.ds(0, HALF), pl.ds(HALF, HALF)
        spans = (
            (out.at[0, top], come.at[0, top], x_next),
            (out.at[0, low], come.at[0, low], x_prev),
            (out.at[1], come.at[1], x_next),
            (out.at[2], come.at[2], x_prev),
        )
        return [
            remote(src, dst, ring_send.at[piece, i], ring_recv.at[piece, i], device)
            for i, (src, dst, device) in enumerate(spans)
        ]

    rings = [ring(piece) for piece in range(2)]

    def launch(piece):
        compute(piece, 0, 2)
        rings[piece][0].start()
        rings[piece][1].start()

    def prepare(piece):
        compute(piece, 1, 1)
        compute(piece, 2, 3)

    def relay(piece):
        for way, rows in ((0, slice(0, HALF)), (1, slice(HALF, CHUNK))):
            rings[piece][way].wait()
            mine = xs[piece, 1 + way, rows, :].astype(F32)
            xs[piece, 1 + way, rows, :] = (mine + xr[piece, 0, rows, :].astype(F32)).astype(BF)
            rings[piece][2 + way].start()

    x0, x1, z0, z1 = jobs = ((0, 0), (0, 1), (1, 0), (1, 1))
    side, side_device, pair_buf = (yh, yl), (across, beside), (xy, zy)

    def pair(job):
        axis, piece = job
        buf = pair_buf[axis].at[piece]
        return remote(
            buf.at[0], buf.at[1], pair_sems.at[0, axis, piece], pair_sems.at[1, axis, piece], side_device[axis]
        )

    pairs_of = {job: pair(job) for job in jobs}

    def queries_part(half, carry):
        rows = pl.ds(pl.multiple_of(half * HALF, HALF), HALF)
        for piece in range(2):
            cols = slice(piece * PIECE, (piece + 1) * PIECE)
            total = jnp.zeros((HALF, PIECE), F32)
            for i in range(4):
                found = jnp.concatenate([gq_buf[i, head, :, cols] for head in range(2)], axis=0)
                total += nn(w_buf[i, rows, : 4 * HD], found)
            zq_buf[rows, cols] = total
        return carry

    def keys_part(piece, rows):
        total = zq_buf[rows, piece * PIECE : (piece + 1) * PIECE]
        for i in range(4):
            found = [
                g_buf[i, head, piece, kind * HD : (kind + 1) * HD, :] for kind in range(2) for head in range(2)
            ]
            total += nn(w_buf[i, rows, 4 * HD :], jnp.concatenate(found, axis=0))
        return total

    def cross(job):
        axis, piece = job
        if axis == 0:
            rings[piece][2].wait()
            rings[piece][3].wait()

        def summed(half):
            rows = pl.ds(pl.multiple_of(half * HALF, HALF), HALF)
            if axis == 1:
                return keys_part(piece, rows).astype(BF)
            return (
                xs[piece, 3, rows, :].astype(F32)
                + xr[piece, 1, rows, :].astype(F32)
                + xr[piece, 2, rows, :].astype(F32)
            ).astype(BF)

        pair_buf[axis][piece, 0] = summed(1 - side[axis])
        pairs_of[job].start()
        pair_buf[axis][piece, 2] = summed(side[axis])

    def total_of(job):
        axis, piece = job
        pairs_of[job].wait()
        return (pair_buf[axis][piece, 1].astype(F32) + pair_buf[axis][piece, 2].astype(F32)).astype(BF)

    my_rows = pl.ds(pl.multiple_of(core * QTR, QTR), QTR)
    its_rows = pl.ds(pl.multiple_of(other * QTR, QTR), QTR)
    lasts = [
        remote(half_buf.at[piece, its_rows], gw_out.at[piece, core], core_sems.at[0, piece], core_sems.at[1, piece], partner)
        for piece in range(2)
    ]

    def swap(piece):
        half_buf[piece] = total_of((0, piece))
        lasts[piece].start()
        gw_out[piece, core] = half_buf[piece, my_rows, :]


    def add_to(ref, index, r):
        ref[r] = (ref[r].astype(F32) + y_buf[index, r].astype(F32)).astype(BF)

    def further(r):
        y_copies[1][r].wait()

        @pl.when(yh == 0)
        def _():
            add_to(near, 1, r)
            back_near[r].start()

        @pl.when(yh == 1)
        def _():
            add_to(far, 1, r)
            back_far[r].start()

    def nearer(r):
        y_copies[0][r].wait()

        @pl.when(yh == 1)
        def _():
            add_to(near, 0, r)
            back_near[r].start()

    launch(0)
    prepare(0)
    compute(0, 3, 0)
    for r in range(2):
        further(r)
    for r in range(2):
        nearer(r)
    for copy in w_in + w_on + [q_kin, q_keep]:
        copy.wait()
    for i in range(3):
        for head in range(2):
            come = gq_buf.at[i, head]
            remote(come, come, gq_send.at[i, head], gq_recv.at[i, head], partner).wait_recv()
    lax.fori_loop(0, 2, queries_part, 0)
    keep = (yh == 0).astype(F32)
    for copy in back_far + back_near:
        copy.wait()
    for r in range(2):
        for kind in range(2):
            total = (
                own[r, kind]
                + y_buf[0, r, kind].astype(F32) * keep
                + x_buf[0, r, kind].astype(F32)
                + x_buf[1, r, kind].astype(F32)
            ).T
            if kind == 0:
                a, b = total[: HD // 2, :], total[HD // 2 :, :]
                c, s = cos[r], sin[r]
                total = jnp.concatenate([a * c + b * s, b * c - a * s], axis=0)
            total = total.astype(BF)
            t_buf[(2 + kind) * HD : (3 + kind) * HD, r * TOK : (r + 1) * TOK] = total
            for piece in range(2):
                dkv_t[r, piece, kind * HD : (kind + 1) * HD, :] = total[:, piece * PIECE : (piece + 1) * PIECE]
    spread = [
        [
            remote(dkv_t.at[r, piece], g_buf.at[i, core, piece], g_send.at[i, r, piece], g_recv.at[i, core, piece], round_z[i][r])
            for i in range(3)
            for r in range(2)
        ]
        for piece in range(2)
    ]
    kin = [
        remote(dkv_t.at[other, piece], g_buf.at[3, core, piece], dk_sems.at[0, piece], dk_sems.at[1, piece], partner)
        for piece in range(2)
    ]
    for piece in range(2):
        for copy in spread[piece] + [kin[piece]]:
            copy.start()
        g_buf[3, core, piece] = dkv_t[core, piece]

    def gathered(piece):
        kin[piece].wait()
        for i in range(3):
            for head in range(2):
                come = g_buf.at[i, head, piece]
                remote(come, come, g_send.at[i, head, piece], g_recv.at[i, head, piece], partner).wait_recv()

    launch(1)
    relay(0)
    prepare(1)
    compute(1, 3, 0)
    relay(1)
    gathered(0)
    cross(z0)
    cross(x0)
    gathered(1)
    cross(z1)
    swap(0)
    cross(x1)
    gx_out[:, :PIECE] = total_of(z0)
    swap(1)
    gx_out[:, PIECE:] = total_of(z1)
    for copy in lasts:
        copy.wait()
    for copy in q_spread + spread[0] + spread[1]:
        copy.wait_send()


def finish(dq, dkv, own, turned, weights, w_rows, cos, sin):
    vmem = pl.BlockSpec(memory_space=pltpu.VMEM)
    hbm = pl.BlockSpec(memory_space=pltpu.HBM)
    any_space = pl.BlockSpec(memory_space=pl.ANY)
    dma = pltpu.SemaphoreType.DMA
    return pl.pallas_call(
        finish_kernel,
        out_shape=(
            jax.ShapeDtypeStruct((HALF, TOK), BF),
            jax.ShapeDtypeStruct((2, 2, QTR, PIECE), BF),
        ),
        in_specs=[any_space] * 3 + [hbm] * 4 + [any_space] * 3 + [vmem, vmem],
        out_specs=(vmem,) * 2,
        scratch_shapes=[
            pltpu.VMEM((2, 2, TOK, HD), F32),
            pltpu.VMEM((D, 2 * TOK), BF),
            pltpu.VMEM((4, CHUNK, 8 * HD), BF),
            pltpu.VMEM((4 * HD, 2 * TOK), BF),
            pltpu.VMEM((2, 2, 2 * HD, PIECE), BF),
            pltpu.VMEM((4, 2, 2 * HD, TOK), BF),
            pltpu.VMEM((4, 2, 2, 2 * HD, PIECE), BF),
            pltpu.VMEM((CHUNK, TOK), F32),
            pltpu.VMEM((2, 2, 2, TOK, HD), BF),
            pltpu.VMEM((2, 2, 2, TOK, HD), BF),
            pltpu.VMEM((2, 2, TOK, HD), BF),
            pltpu.VMEM((2, 2, TOK, HD), BF),
            pltpu.VMEM((2, 4, CHUNK, PIECE), BF),
            pltpu.VMEM((2, 3, CHUNK, PIECE), BF),
            pltpu.VMEM((2, 3, HALF, PIECE), BF),
            pltpu.VMEM((2, 3, HALF, PIECE), BF),
            pltpu.VMEM((2, HALF, PIECE), BF),
            dma((8,)), dma((3,)), dma((2, 2)), dma((2, 2, 2)), dma((2, 2, 2)),
            dma((2, 4)), dma((2, 4)), dma((2, 2, 2)), dma((2, 2)), dma((3, 2, 2)), dma((3, 2, 2)),
            dma((3, 2)), dma((3, 2)), dma((6,)), dma((3,)), dma((3,)),
        ],
        compiler_params=pltpu.CompilerParams(
            collective_id=1, has_side_effects=True, vmem_limit_bytes=54 << 20
        ),
        name="finish",
    )(dq, dkv, own, turned, *weights, *w_rows, cos, sin)


def emit_kernel(gx, gw, gx_out, gq_out, gk_out, gv_out):
    gx_out[...] = gx[...]
    for head in range(2):
        gq_out[:, head * 2 * HD : (head + 1) * 2 * HD] = gw[0, head]
        gk_out[:, head * HD : (head + 1) * HD] = gw[1, head, :, :HD]
        gv_out[:, head * HD : (head + 1) * HD] = gw[1, head, :, HD:]


def emit(gx, gw):
    vmem = pl.BlockSpec(memory_space=pltpu.VMEM)
    return pl.pallas_call(
        emit_kernel,
        out_shape=(
            jax.ShapeDtypeStruct((HALF, TOK), BF),
            jax.ShapeDtypeStruct((QTR, 4 * HD), BF),
            jax.ShapeDtypeStruct((QTR, 2 * HD), BF),
            jax.ShapeDtypeStruct((QTR, 2 * HD), BF),
        ),
        in_specs=[vmem] * 2,
        out_specs=(vmem,) * 4,
        name="emit",
    )(gx, gw)


def body(queries, keys, values, out_grad, normed, w_query, w_key, w_value, valid_len):
    chip = lax.axis_index("seq") // 2
    inverse_freq = ROPE_BASE ** (-(jnp.arange(HD // 2, dtype=F32) * (2.0 / HD)))
    slots = (chip * 2 * TOK + jnp.arange(2 * TOK, dtype=jnp.int32)).astype(F32).reshape(2, 1, TOK)
    angles = slots * inverse_freq[None, :, None]
    cos, sin = jnp.cos(angles), jnp.sin(angles)
    base = (2 * chip - 8).astype(jnp.int32).reshape(1)
    core, z = lax.axis_index("seq") % 2, lax.axis_index("head") // 2
    weights = (w_query, w_key, w_value)
    w_rows = []
    for step in STEPS:
        start = ((z + 4 + step) % 4) * CHUNK + core * HALF
        rows = jnp.concatenate([lax.dynamic_slice_in_dim(w, start, HALF, 0) for w in weights], axis=1)
        turns = [(h, (h + 2 * step) % 8) for h in range(8)]
        w_rows.append(lax.ppermute(rows, "head", turns))
    qg, kv, turned = gather(queries, keys, values, out_grad, normed)
    dq, dkv, own = attend(valid_len, base, qg, kv, cos, sin)
    gx, gq, gk, gv = emit(*finish(dq, dkv, own, turned, weights, w_rows, cos, sin))
    return gx.T, gq, gk, gv


def solution(mesh):
    both = P("seq", "head")
    placed = (both, both, both, both, P("seq", None), P(None, "head"), P(None, "head"), P(None, "head"), P())
    return jax.shard_map(
        body, mesh=mesh, in_specs=placed, out_specs=(both,) * 4, check_vma=False
    )
```

```python
import functools

import jax
import jax.numpy as jnp
from jax import lax
from jax.experimental import pallas as pl
from jax.experimental.pallas import tpu as pltpu
from jax.sharding import PartitionSpec as P

D = 4608
H = 32
HD = 128
WINDOW = 4096
SOFT_CAP = 50.0
ROPE_BASE = 10000.0
SCALE = (D // H) ** (-0.5)

TOK = 512
NB = 10
TILE = 256
CHUNK = D // 4
HALF = CHUNK // 2
QTR = HALF // 2

BF = jnp.bfloat16
F32 = jnp.float32
MESH = pl.DeviceIdType.MESH
STEPS = (1, -1, 2)
LOG2E = 1.4426950408889634


def nt(left, right):
    return lax.dot_general(left, right, (((1,), (1,)), ((), ())), preferred_element_type=F32)


def nn(left, right):
    return lax.dot_general(left, right, (((1,), (0,)), ((), ())), preferred_element_type=F32)


def here():
    s, h = lax.axis_index("seq"), lax.axis_index("head")
    return s // 4, (s // 2) % 2, s % 2, h // 2, h % 2


def at_seq(x, yh, core):
    return {"seq": (lax.rem(x + 4, 4) * 2 + yh) * 2 + core, "head": lax.axis_index("head")}


def at_head(z, yl):
    return {"seq": lax.axis_index("seq"), "head": lax.rem(z + 4, 4) * 2 + yl}


def at_core(z, yl, core):
    s = lax.axis_index("seq")
    return {"seq": s - s % 2 + core, "head": lax.rem(z + 4, 4) * 2 + yl}


def remote(src, dst, send, recv, device):
    return pltpu.make_async_remote_copy(
        src_ref=src, dst_ref=dst, send_sem=send, recv_sem=recv, device_id=device, device_id_type=MESH
    )


def greet(devices):
    barrier = pltpu.get_barrier_semaphore()
    for device in devices:
        pl.semaphore_signal(barrier, inc=1, device_id=device, device_id_type=MESH)
    pl.semaphore_wait(barrier, len(devices))


def pack_kernel(wq, wk, wv, out, sem):
    _, _, core, _, _ = here()
    copies = []
    for i in range(4):
        rows = pl.ds(pl.multiple_of(i * CHUNK + core * HALF, HALF), HALF)
        for j, (ref, first, last) in enumerate(((wq, 0, 4), (wk, 4, 6), (wv, 6, 8))):
            to = out.at[i, :, first * HD : last * HD]
            copies.append(pltpu.make_async_copy(ref.at[rows], to, sem.at[i, j]))
    for copy in copies:
        copy.start()
    for copy in copies:
        copy.wait()


def pack(weights):
    hbm = pl.BlockSpec(memory_space=pltpu.HBM)
    return pl.pallas_call(
        pack_kernel,
        out_shape=jax.ShapeDtypeStruct((4, HALF, 8 * HD), BF),
        in_specs=[hbm] * 3,
        out_specs=hbm,
        scratch_shapes=[pltpu.SemaphoreType.DMA((4, 3))],
        name="pack",
    )(*weights)


def gather_kernel(
    q, g, k, v, n_hbm, qg, kv, nt_out, kv_own, qg_own, n_ref, turned,
    n_load_sem, kv_load, qg_load, kv_loc, qg_loc, swap_send, swap_recv,
    x_send, x_recv, y_send, y_recv, n_sem, n_send, n_recv,
):
    x, yh, core, _, _ = here()
    other = 1 - core
    partner = at_seq(x, yh, other)
    across = at_seq(x, 1 - yh, core)

    def stage(pair, to, width, sems):
        return [
            pltpu.make_async_copy(
                ref.at[:, head * width : (head + 1) * width], to.at[head, kind], sems.at[head, kind]
            )
            for head in range(2)
            for kind, ref in enumerate(pair)
        ]

    kv_stage = stage((k, v), kv_own, HD, kv_load)
    qg_stage = stage((q, g), qg_own, 2 * HD, qg_load)
    n_load = pltpu.make_async_copy(n_hbm, n_ref, n_load_sem)
    for copy in kv_stage + qg_stage + [n_load]:
        copy.start()
    greet(
        [partner, across]
        + [at_seq(x + step, yh, c) for step in (1, -1, 2) for c in range(2)]
    )
    for copy in kv_stage:
        copy.wait()
    along = [
        [
            remote(
                kv_own.at[head],
                kv.at[8 - 4 * step + core],
                x_send.at[step - 1, head],
                x_recv.at[step - 1, core],
                at_seq(x + step, yh, head),
            )
            for head in range(2)
        ]
        for step in (1, 2)
    ]
    kv_swap = remote(kv_own.at[other], kv.at[8 + core], swap_send.at[0], swap_recv.at[0], partner)
    kv_keep = pltpu.make_async_copy(kv_own.at[core], kv.at[8 + core], kv_loc)
    qg_swap = remote(qg_own.at[other], qg.at[core], swap_send.at[1], swap_recv.at[1], partner)
    qg_keep = pltpu.make_async_copy(qg_own.at[core], qg.at[core], qg_loc)
    kv_swap.start()
    kv_keep.start()
    for copy in along[0] + along[1]:
        copy.start()

    def arrived(step, c):
        dst = kv.at[8 - 4 * step + c]
        remote(dst, dst, x_send.at[step - 1, c], x_recv.at[step - 1, c], partner).wait_recv()

    def turn(i, carry):
        cols = pl.ds(pl.multiple_of(i * HD, HD), HD)
        turned[cols, :] = n_ref[:, cols].T
        return carry

    first_src = jnp.where(yh == 0, 8, 4)
    second_src = jnp.where(yh == 0, 4, 0)
    first = [
        remote(kv.at[first_src + c], kv.at[6 + c], y_send.at[0, c], y_recv.at[0, c], across)
        for c in range(2)
    ]
    second = [
        remote(kv.at[second_src + c], kv.at[2 + c], y_send.at[1, c], y_recv.at[1, c], across)
        for c in range(2)
    ]
    kv_keep.wait()
    kv_swap.wait_recv()

    @pl.when(yh == 0)
    def _():
        for copy in first:
            copy.start()

    for copy in qg_stage:
        copy.wait()
    qg_swap.start()
    qg_keep.start()
    n_load.wait()
    lax.fori_loop(0, D // HD // 2, turn, 0)
    for c in range(2):
        arrived(1, c)

        @pl.when(yh == 0)
        def _():
            second[c].start()

        @pl.when(yh == 1)
        def _():
            first[c].start()

    lax.fori_loop(D // HD // 2, D // HD, turn, 0)
    n_local = pltpu.make_async_copy(turned, nt_out.at[core], n_sem)
    n_swap = remote(turned, nt_out.at[core], n_send, n_recv, partner)
    n_local.start()
    n_swap.start()
    for c in range(2):
        arrived(2, c)

        @pl.when(yh == 1)
        def _():
            second[c].start()

    n_local.wait()
    n_swap.wait()
    qg_keep.wait()
    qg_swap.wait()
    for copy in first + second:
        copy.wait()
    kv_swap.wait_send()
    for copy in along[0] + along[1]:
        copy.wait_send()


def gather(queries, keys, values, grads, normed):
    hbm = pl.BlockSpec(memory_space=pltpu.HBM)
    dma = pltpu.SemaphoreType.DMA
    return pl.pallas_call(
        gather_kernel,
        out_shape=(
            jax.ShapeDtypeStruct((2, 2, TOK, 2 * HD), BF),
            jax.ShapeDtypeStruct((NB, 2, TOK, HD), BF),
            jax.ShapeDtypeStruct((2, D, TOK), BF),
        ),
        in_specs=[hbm] * 5,
        out_specs=(hbm,) * 3,
        scratch_shapes=[
            pltpu.VMEM((2, 2, TOK, HD), BF),
            pltpu.VMEM((2, 2, TOK, 2 * HD), BF),
            pltpu.VMEM((TOK, D), BF),
            pltpu.VMEM((D, TOK), BF),
            dma, dma((2, 2)), dma((2, 2)), dma, dma, dma((2,)), dma((2,)),
            dma((2, 2)), dma((2, 2)), dma((2, 2)), dma((2, 2)), dma, dma, dma,
        ],
        compiler_params=pltpu.CompilerParams(
            collective_id=0, has_side_effects=True, vmem_limit_bytes=60 << 20
        ),
        name="gather",
    )(queries, grads, keys, values, normed)


STEP = 8
PIECES = 4 * NB
EMPTY = PIECES
OWN = PIECES + STEP


def attend_kernel(
    valid, base, qg, kv_hbm, cos, sin, dq_out, dkv_out, own_out,
    kv, e_s, w_s, kt_s, vt_s, o_acc, dq_acc, dk_acc, dv_acc, listed, sem,
):
    first_shard = base[0]
    load = pltpu.make_async_copy(kv_hbm, kv.at[pl.ds(0, NB)], sem)
    load.start()
    dk_acc[...] = jnp.zeros_like(dk_acc)
    dv_acc[...] = jnp.zeros_like(dv_acc)
    for k in range(STEP):
        kv[NB + k // 4, 0, k % 4] = jnp.zeros((HD, HD), BF)
        kv[NB + k // 4, 1, k % 4] = jnp.zeros((HD, HD), BF)
        kt_s[EMPTY + k] = jnp.zeros((HD, HD), BF)
        vt_s[EMPTY + k] = jnp.zeros((HD + 16, HD), BF)
    load.wait()

    def valid_of(b):
        return valid[jnp.maximum(first_shard + b, 0)]

    def turn(b, carry):
        for k in range(4):
            live = lax.broadcasted_iota(jnp.int32, (HD + 16, HD), 1) + k * HD < valid_of(b)
            k_t = kv[b, 0, k].T
            v_t = jnp.concatenate([kv[b, 1, k].T, jnp.ones((16, HD), BF)], axis=0)
            kt_s[4 * b + k] = jnp.where(live[:HD], k_t.astype(F32), 0.0).astype(BF)
            vt_s[4 * b + k] = jnp.where(live, v_t.astype(F32), 0.0).astype(BF)

            @pl.when(b >= 8)
            def _():
                kt_s[OWN + 4 * (b - 8) + k] = k_t
                vt_s[OWN + 4 * (b - 8) + k] = v_t

        return carry

    lax.fori_loop(0, NB, turn, 0)
    key_iota = lax.broadcasted_iota(jnp.int32, (TILE, 2 * TILE), 0)
    query_iota = lax.rem(lax.broadcasted_iota(jnp.int32, (TILE, 2 * TILE), 1), TILE)

    def query_tile(i, carry):
        r, qt = i // 2, lax.rem(i, 2)
        q_valid = valid_of(8 + r)
        q_rows = pl.ds(pl.multiple_of(qt * TILE, TILE), TILE)
        lanes = q_rows

        @pl.when(qt * TILE >= q_valid)
        def _():
            dq_out[r, :, lanes] = jnp.zeros((2 * HD, TILE), BF)

        @pl.when(qt * TILE < q_valid)
        def _():
            def note(t, count):
                j, k = t // 4, lax.rem(t, 4)
                b = r + j
                wanted = (
                    (first_shard + b >= 0)
                    & (k * HD < valid_of(b))
                    & jnp.logical_not((j == 0) & (k < 2 * qt + 2))
                    & jnp.logical_not((j == 8) & (k >= 2 * qt))
                )
                listed[count] = jnp.where(wanted, 4 * b + k, EMPTY)
                return count + wanted.astype(jnp.int32)

            count = lax.fori_loop(0, 36, note, 0)
            for extra in range(STEP - 1):
                listed[count + extra] = EMPTY + extra
            steps = (count + STEP - 1) // STEP
            doubles = steps // 2

            q_two = qg[r, 0, q_rows, :]
            g_two = qg[r, 1, q_rows, :]
            q_rows2 = jnp.concatenate([q_two[:, :HD], q_two[:, HD:]], axis=0)
            q_t = q_rows2.T

            def keys_of(kind, pieces):
                return jnp.concatenate([kv[p // 4, kind, lax.rem(p, 4)] for p in pieces], axis=0)

            def turned_of(ref, pieces):
                return jnp.concatenate([ref[p] for p in pieces], axis=1)

            def forward(pieces, turned, slot, mask):
                parts = []
                for n in range(0, len(pieces), 2):
                    keys = keys_of(0, pieces[n : n + 2])
                    rows = pl.ds(pl.multiple_of(slot + n * HD, TILE), TILE)
                    heads = []
                    for head in range(2):
                        cols = slice(head * TILE, (head + 1) * TILE)
                        th = jnp.tanh(nn(keys, q_t[:, cols]) * (SCALE / SOFT_CAP))
                        e = jnp.exp2(th * (SOFT_CAP * LOG2E))
                        if mask is not None:
                            e = jnp.where(mask[n // 2][:, cols], e, 0.0)
                        eb = e.astype(BF)
                        e_s[rows, cols] = eb
                        w_s[rows, cols] = (e * (1.0 - th * th)).astype(BF)
                        heads.append(eb)
                    parts.append(heads)
                for head in range(2):
                    cols = slice(head * TILE, (head + 1) * TILE)
                    column = jnp.concatenate([p[head] for p in parts], axis=0)
                    o_acc[:, cols] += nn(turned_of(vt_s, turned), column)

            gap = query_iota - key_iota
            key_pos = key_iota + qt * TILE
            oldest_there = first_shard + r >= 0
            edge_mask = (
                gap + 8 * TOK < WINDOW,
                (gap >= 0) & ((key_pos < q_valid) | (gap == 0)),
            )
            old = jnp.where(oldest_there, 4 * r + 2 * qt, EMPTY)
            own = 4 * (8 + r) + 2 * qt
            edge = (old, old + 1, own, own + 1)
            edge_turned = (old, old + 1, OWN + 4 * r + 2 * qt, OWN + 4 * r + 2 * qt + 1)
            o_acc[...] = jnp.zeros_like(o_acc)
            forward(edge, edge_turned, 0, edge_mask)

            def forward_step(width, n, carry):
                pieces = tuple(listed[n * width + m] for m in range(width))
                forward(pieces, pieces, (4 + n * width) * HD, None)
                return carry

            lax.fori_loop(0, doubles, functools.partial(forward_step, 2 * STEP), 0)
            lax.fori_loop(2 * doubles, steps, functools.partial(forward_step, STEP), 0)
            inv = 1.0 / o_acc[HD : HD + 1, :]
            g_rows2 = jnp.concatenate([g_two[:, :HD], g_two[:, HD:]], axis=0).astype(F32)
            live = query_iota[:1, :] + qt * TILE < q_valid
            g_t = jnp.where(live, g_rows2.T, 0.0) * inv
            delta = jnp.sum(g_t * o_acc[:HD, :], axis=0, keepdims=True) * inv
            gs_t = g_t.astype(BF)
            gs = g_t.T.astype(BF)
            dq_acc[...] = jnp.zeros_like(dq_acc)

            def backward(pieces, turned, slot):
                rows = pl.ds(pl.multiple_of(slot, TILE), len(pieces) * HD)
                columns = []
                for head in range(2):
                    cols = slice(head * TILE, (head + 1) * TILE)
                    parts = []
                    for n in range(0, len(pieces), 2):
                        part = pl.ds(pl.multiple_of(slot + n * HD, TILE), TILE)
                        dp = nn(keys_of(1, pieces[n : n + 2]), gs_t[:, cols])
                        parts.append((w_s[part, cols].astype(F32) * (dp - delta[:, cols])).astype(BF))
                    columns.append(jnp.concatenate(parts, axis=0))
                ds = jnp.concatenate(columns, axis=1)
                dq_acc[...] += nn(turned_of(kt_s, turned), ds)
                dk = nn(ds, q_rows2)
                dv = nn(e_s[rows, :], gs)
                for n, p in enumerate(pieces):
                    dk_acc[p] += dk[n * HD : (n + 1) * HD]
                    dv_acc[p] += dv[n * HD : (n + 1) * HD]

            backward(edge, edge_turned, 0)

            def backward_step(width, n, carry):
                pieces = tuple(listed[n * width + m] for m in range(width))
                backward(pieces, pieces, (4 + n * width) * HD)
                return carry

            lax.fori_loop(0, doubles, functools.partial(backward_step, 2 * STEP), 0)
            lax.fori_loop(2 * doubles, steps, functools.partial(backward_step, STEP), 0)
            dq = dq_acc[...] * SCALE
            c, s = cos[r, :, lanes], sin[r, :, lanes]
            for head in range(2):
                a = dq[: HD // 2, head * TILE : (head + 1) * TILE]
                z = dq[HD // 2 :, head * TILE : (head + 1) * TILE]
                dq_out[r, head * HD : head * HD + HD // 2, lanes] = (a * c + z * s).astype(BF)
                dq_out[r, head * HD + HD // 2 : (head + 1) * HD, lanes] = (z * c - a * s).astype(BF)

        return carry

    lax.fori_loop(0, 4, query_tile, 0)

    def result(ref, b, k, scale):
        live = lax.broadcasted_iota(jnp.int32, (HD, HD), 0) + k * HD < valid_of(b)
        return jnp.where(live, ref[4 * b + k] * scale, 0.0)

    def give(b, carry):
        for k in range(4):
            rows = slice(k * HD, (k + 1) * HD)
            dkv_out[b, 0, rows, :] = result(dk_acc, b, k, SCALE).astype(BF)
            dkv_out[b, 1, rows, :] = result(dv_acc, b, k, 1.0).astype(BF)
        return carry

    lax.fori_loop(0, 8, give, 0)
    for r in range(2):
        for k in range(4):
            rows = slice(k * HD, (k + 1) * HD)
            own_out[r, 0, rows, :] = result(dk_acc, 8 + r, k, SCALE)
            own_out[r, 1, rows, :] = result(dv_acc, 8 + r, k, 1.0)


def attend(valid_len, base, qg, kv, cos, sin):
    vmem = pl.BlockSpec(memory_space=pltpu.VMEM)
    smem = pl.BlockSpec(memory_space=pltpu.SMEM)
    return pl.pallas_call(
        attend_kernel,
        out_shape=(
            jax.ShapeDtypeStruct((2, 2 * HD, TOK), BF),
            jax.ShapeDtypeStruct((8, 2, TOK, HD), BF),
            jax.ShapeDtypeStruct((2, 2, TOK, HD), F32),
        ),
        in_specs=[smem, smem, vmem, pl.BlockSpec(memory_space=pltpu.HBM), vmem, vmem],
        out_specs=(vmem,) * 3,
        scratch_shapes=[
            pltpu.VMEM((NB + STEP // 4, 2, 4, HD, HD), BF),
            pltpu.VMEM((44 * HD, 2 * TILE), BF),
            pltpu.VMEM((44 * HD, 2 * TILE), BF),
            pltpu.VMEM((OWN + 8, HD, HD), BF),
            pltpu.VMEM((OWN + 8, HD + 16, HD), BF),
            pltpu.VMEM((HD + 16, 2 * TILE), F32),
            pltpu.VMEM((HD, 2 * TILE), F32),
            pltpu.VMEM((PIECES + STEP, HD, HD), F32),
            pltpu.VMEM((PIECES + STEP, HD, HD), F32),
            pltpu.SMEM((48,), jnp.int32),
            pltpu.SemaphoreType.DMA,
        ],
        compiler_params=pltpu.CompilerParams(vmem_limit_bytes=58 << 20),
        cost_estimate=pl.CostEstimate(flops=26_000_000_000, bytes_accessed=8 << 20, transcendentals=20_000_000),
        name="attend",
    )(valid_len, base, qg, kv.reshape(NB, 2, 4, HD, HD), cos, sin)


PIECE = 256


def finish_kernel(
    dq, dkv, own_hbm, turned_hbm, wq, wk, wv, w_rows, cos, sin, gx_out, gw_out,
    own, n_buf, w_buf, t_buf, dkv_t, gq_buf, g_buf, zq_buf, y_buf, x_buf, near, far,
    xs, xr, xy, zy, half_buf,
    load_sem, dq_sems, dk_sems, y_sems, x_sems, ring_send, ring_recv, pair_sems, core_sems, g_send, g_recv,
    gq_send, gq_recv, w_load, w_send, w_recv,
):
    x, yh, core, z, yl = here()
    other = 1 - core
    partner = at_seq(x, yh, other)
    across = at_seq(x, 1 - yh, core)
    beside = at_head(z, 1 - yl)
    x_next, x_prev, x_far = at_seq(x + 1, yh, core), at_seq(x - 1, yh, core), at_seq(x + 2, yh, core)
    round_z = [[at_core(z + step, yl, c) for c in range(2)] for step in STEPS]
    greet([partner, across, beside, x_next, x_prev, x_far] + sum(round_z, []))

    y_copies = [
        [
            remote(dkv.at[6 - 4 * i + r], y_buf.at[i, r], y_sems.at[0, i, r], y_sems.at[1, i, r], across)
            for r in range(2)
        ]
        for i in range(2)
    ]
    for copy in y_copies[1] + y_copies[0]:
        copy.start()
    pairs = [
        (dkv.at[pl.ds(0, 2)], far),
        (dkv.at[pl.ds(4, 2)], near),
        (dq.at[0], t_buf.at[: 2 * HD, :TOK]),
        (dq.at[1], t_buf.at[: 2 * HD, TOK:]),
        (turned_hbm.at[0], n_buf.at[:, :TOK]),
        (turned_hbm.at[1], n_buf.at[:, TOK:]),
        (own_hbm, own),
    ]
    loads = [pltpu.make_async_copy(src, dst, load_sem.at[i]) for i, (src, dst) in enumerate(pairs)]
    for copy in loads:
        copy.start()
    q_spread = [
        remote(dq.at[r], gq_buf.at[i, core], gq_send.at[i, r], gq_recv.at[i, core], round_z[i][r])
        for i in range(3)
        for r in range(2)
    ]
    q_kin = remote(dq.at[other], gq_buf.at[3, core], dq_sems.at[0], dq_sems.at[1], partner)
    q_keep = pltpu.make_async_copy(dq.at[core], gq_buf.at[3, core], dq_sems.at[2])
    part = pl.ds(pl.multiple_of(core * HALF, HALF), HALF)
    own_rows = pl.ds(pl.multiple_of(z * CHUNK, CHUNK), CHUNK)
    w_from = [w_rows.at[lax.rem(z + 4 - step, 4)] for step in STEPS]
    w_in = [
        pltpu.make_async_copy(src, w_buf.at[i, part], w_load.at[i])
        for i, src in enumerate(w_from)
    ] + [
        pltpu.make_async_copy(ref.at[own_rows], w_buf.at[3, :, cols], w_load.at[3 + i])
        for i, (ref, cols) in enumerate(
            ((wq, slice(0, 4 * HD)), (wk, slice(4 * HD, 6 * HD)), (wv, slice(6 * HD, 8 * HD)))
        )
    ]
    w_on = [
        remote(src, w_buf.at[i, part], w_send.at[i], w_recv.at[i], partner)
        for i, src in enumerate(w_from)
    ]
    back_near, back_far = (
        [
            remote(src.at[r], x_buf.at[i, r], x_sems.at[0, i, r], x_sems.at[1, i, r], device)
            for r in range(2)
        ]
        for i, (src, device) in enumerate(((near, x_prev), (far, x_far)))
    )
    loads[0].wait()

    @pl.when(yh == 0)
    def _():
        for copy in back_far:
            copy.start()

    for copy in q_spread + [q_kin, q_keep] + w_on + w_in:
        copy.start()
    for copy in loads[1:]:
        copy.wait()

    def term(piece, rows):
        return nt(n_buf[rows, :], t_buf[piece * PIECE : (piece + 1) * PIECE, :])

    def compute(piece, slot, step):
        first_row = lax.rem(x + step, 4) * CHUNK

        def one(half, carry):
            to = pl.ds(pl.multiple_of(half * HALF, HALF), HALF)
            rows = pl.ds(pl.multiple_of(first_row + half * HALF, HALF), HALF)
            xs[piece, slot, to, :] = term(piece, rows).astype(BF)
            return carry

        lax.fori_loop(0, 2, one, 0)

    def ring(piece):
        out, come = xs.at[piece], xr.at[piece]
        top, low = pl.ds(0, HALF), pl.ds(HALF, HALF)
        spans = (
            (out.at[0, top], come.at[0, top], x_next),
            (out.at[0, low], come.at[0, low], x_prev),
            (out.at[1], come.at[1], x_next),
            (out.at[2], come.at[2], x_prev),
        )
        return [
            remote(src, dst, ring_send.at[piece, i], ring_recv.at[piece, i], device)
            for i, (src, dst, device) in enumerate(spans)
        ]

    rings = [ring(piece) for piece in range(2)]

    def launch(piece):
        compute(piece, 0, 2)
        rings[piece][0].start()
        rings[piece][1].start()

    def prepare(piece):
        compute(piece, 1, 1)
        compute(piece, 2, 3)

    def relay(piece):
        for way, rows in ((0, slice(0, HALF)), (1, slice(HALF, CHUNK))):
            rings[piece][way].wait()
            mine = xs[piece, 1 + way, rows, :].astype(F32)
            xs[piece, 1 + way, rows, :] = (mine + xr[piece, 0, rows, :].astype(F32)).astype(BF)
            rings[piece][2 + way].start()

    x0, x1, z0, z1 = jobs = ((0, 0), (0, 1), (1, 0), (1, 1))
    side, side_device, pair_buf = (yh, yl), (across, beside), (xy, zy)

    def pair(job):
        axis, piece = job
        buf = pair_buf[axis].at[piece]
        return remote(
            buf.at[0], buf.at[1], pair_sems.at[0, axis, piece], pair_sems.at[1, axis, piece], side_device[axis]
        )

    pairs_of = {job: pair(job) for job in jobs}

    def queries_part(half, carry):
        rows = pl.ds(pl.multiple_of(half * HALF, HALF), HALF)
        for piece in range(2):
            cols = slice(piece * PIECE, (piece + 1) * PIECE)
            total = jnp.zeros((HALF, PIECE), F32)
            for i in range(4):
                found = jnp.concatenate([gq_buf[i, head, :, cols] for head in range(2)], axis=0)
                total += nn(w_buf[i, rows, : 4 * HD], found)
            zq_buf[rows, cols] = total
        return carry

    def keys_part(piece, rows):
        total = zq_buf[rows, piece * PIECE : (piece + 1) * PIECE]
        for i in range(4):
            found = [
                g_buf[i, head, piece, kind * HD : (kind + 1) * HD, :] for kind in range(2) for head in range(2)
            ]
            total += nn(w_buf[i, rows, 4 * HD :], jnp.concatenate(found, axis=0))
        return total

    def cross(job):
        axis, piece = job
        if axis == 0:
            rings[piece][2].wait()
            rings[piece][3].wait()

        def summed(half):
            rows = pl.ds(pl.multiple_of(half * HALF, HALF), HALF)
            if axis == 1:
                return keys_part(piece, rows).astype(BF)
            return (
                xs[piece, 3, rows, :].astype(F32)
                + xr[piece, 1, rows, :].astype(F32)
                + xr[piece, 2, rows, :].astype(F32)
            ).astype(BF)

        pair_buf[axis][piece, 0] = summed(1 - side[axis])
        pairs_of[job].start()
        pair_buf[axis][piece, 2] = summed(side[axis])

    def total_of(job):
        axis, piece = job
        pairs_of[job].wait()
        return (pair_buf[axis][piece, 1].astype(F32) + pair_buf[axis][piece, 2].astype(F32)).astype(BF)

    my_rows = pl.ds(pl.multiple_of(core * QTR, QTR), QTR)
    its_rows = pl.ds(pl.multiple_of(other * QTR, QTR), QTR)
    lasts = [
        remote(half_buf.at[piece, its_rows], gw_out.at[piece, core], core_sems.at[0, piece], core_sems.at[1, piece], partner)
        for piece in range(2)
    ]

    def swap(piece):
        half_buf[piece] = total_of((0, piece))
        lasts[piece].start()
        gw_out[piece, core] = half_buf[piece, my_rows, :]


    def add_to(ref, index, r):
        ref[r] = (ref[r].astype(F32) + y_buf[index, r].astype(F32)).astype(BF)

    def further(r):
        y_copies[1][r].wait()

        @pl.when(yh == 0)
        def _():
            add_to(near, 1, r)
            back_near[r].start()

        @pl.when(yh == 1)
        def _():
            add_to(far, 1, r)
            back_far[r].start()

    def nearer(r):
        y_copies[0][r].wait()

        @pl.when(yh == 1)
        def _():
            add_to(near, 0, r)
            back_near[r].start()

    launch(0)
    prepare(0)
    compute(0, 3, 0)
    for r in range(2):
        further(r)
    for r in range(2):
        nearer(r)
    for copy in w_in + w_on + [q_kin, q_keep]:
        copy.wait()
    for i in range(3):
        for head in range(2):
            come = gq_buf.at[i, head]
            remote(come, come, gq_send.at[i, head], gq_recv.at[i, head], partner).wait_recv()
    lax.fori_loop(0, 2, queries_part, 0)
    keep = (yh == 0).astype(F32)
    for copy in back_far + back_near:
        copy.wait()
    for r in range(2):
        for kind in range(2):
            total = (
                own[r, kind]
                + y_buf[0, r, kind].astype(F32) * keep
                + x_buf[0, r, kind].astype(F32)
                + x_buf[1, r, kind].astype(F32)
            ).T
            if kind == 0:
                a, b = total[: HD // 2, :], total[HD // 2 :, :]
                c, s = cos[r], sin[r]
                total = jnp.concatenate([a * c + b * s, b * c - a * s], axis=0)
            total = total.astype(BF)
            t_buf[(2 + kind) * HD : (3 + kind) * HD, r * TOK : (r + 1) * TOK] = total
            for piece in range(2):
                dkv_t[r, piece, kind * HD : (kind + 1) * HD, :] = total[:, piece * PIECE : (piece + 1) * PIECE]
    spread = [
        [
            remote(dkv_t.at[r, piece], g_buf.at[i, core, piece], g_send.at[i, r, piece], g_recv.at[i, core, piece], round_z[i][r])
            for i in range(3)
            for r in range(2)
        ]
        for piece in range(2)
    ]
    kin = [
        remote(dkv_t.at[other, piece], g_buf.at[3, core, piece], dk_sems.at[0, piece], dk_sems.at[1, piece], partner)
        for piece in range(2)
    ]
    for piece in range(2):
        for copy in spread[piece] + [kin[piece]]:
            copy.start()
        g_buf[3, core, piece] = dkv_t[core, piece]

    def gathered(piece):
        kin[piece].wait()
        for i in range(3):
            for head in range(2):
                come = g_buf.at[i, head, piece]
                remote(come, come, g_send.at[i, head, piece], g_recv.at[i, head, piece], partner).wait_recv()

    launch(1)
    relay(0)
    prepare(1)
    compute(1, 3, 0)
    relay(1)
    gathered(0)
    cross(z0)
    cross(x0)
    gathered(1)
    cross(z1)
    swap(0)
    cross(x1)
    gx_out[:, :PIECE] = total_of(z0)
    swap(1)
    gx_out[:, PIECE:] = total_of(z1)
    for copy in lasts:
        copy.wait()
    for copy in q_spread + spread[0] + spread[1]:
        copy.wait_send()


def finish(dq, dkv, own, turned, weights, w_rows, cos, sin):
    vmem = pl.BlockSpec(memory_space=pltpu.VMEM)
    hbm = pl.BlockSpec(memory_space=pltpu.HBM)
    any_space = pl.BlockSpec(memory_space=pl.ANY)
    dma = pltpu.SemaphoreType.DMA
    return pl.pallas_call(
        finish_kernel,
        out_shape=(
            jax.ShapeDtypeStruct((HALF, TOK), BF),
            jax.ShapeDtypeStruct((2, 2, QTR, PIECE), BF),
        ),
        in_specs=[any_space] * 3 + [hbm] * 5 + [vmem, vmem],
        out_specs=(vmem,) * 2,
        scratch_shapes=[
            pltpu.VMEM((2, 2, TOK, HD), F32),
            pltpu.VMEM((D, 2 * TOK), BF),
            pltpu.VMEM((4, CHUNK, 8 * HD), BF),
            pltpu.VMEM((4 * HD, 2 * TOK), BF),
            pltpu.VMEM((2, 2, 2 * HD, PIECE), BF),
            pltpu.VMEM((4, 2, 2 * HD, TOK), BF),
            pltpu.VMEM((4, 2, 2, 2 * HD, PIECE), BF),
            pltpu.VMEM((CHUNK, TOK), F32),
            pltpu.VMEM((2, 2, 2, TOK, HD), BF),
            pltpu.VMEM((2, 2, 2, TOK, HD), BF),
            pltpu.VMEM((2, 2, TOK, HD), BF),
            pltpu.VMEM((2, 2, TOK, HD), BF),
            pltpu.VMEM((2, 4, CHUNK, PIECE), BF),
            pltpu.VMEM((2, 3, CHUNK, PIECE), BF),
            pltpu.VMEM((2, 3, HALF, PIECE), BF),
            pltpu.VMEM((2, 3, HALF, PIECE), BF),
            pltpu.VMEM((2, HALF, PIECE), BF),
            dma((8,)), dma((3,)), dma((2, 2)), dma((2, 2, 2)), dma((2, 2, 2)),
            dma((2, 4)), dma((2, 4)), dma((2, 2, 2)), dma((2, 2)), dma((3, 2, 2)), dma((3, 2, 2)),
            dma((3, 2)), dma((3, 2)), dma((6,)), dma((3,)), dma((3,)),
        ],
        compiler_params=pltpu.CompilerParams(
            collective_id=1, has_side_effects=True, vmem_limit_bytes=54 << 20
        ),
        name="finish",
    )(dq, dkv, own, turned, *weights, w_rows, cos, sin)


def emit_kernel(gx, gw, gx_out, gq_out, gk_out, gv_out):
    gx_out[...] = gx[...]
    for head in range(2):
        gq_out[:, head * 2 * HD : (head + 1) * 2 * HD] = gw[0, head]
        gk_out[:, head * HD : (head + 1) * HD] = gw[1, head, :, :HD]
        gv_out[:, head * HD : (head + 1) * HD] = gw[1, head, :, HD:]


def emit(gx, gw):
    vmem = pl.BlockSpec(memory_space=pltpu.VMEM)
    return pl.pallas_call(
        emit_kernel,
        out_shape=(
            jax.ShapeDtypeStruct((HALF, TOK), BF),
            jax.ShapeDtypeStruct((QTR, 4 * HD), BF),
            jax.ShapeDtypeStruct((QTR, 2 * HD), BF),
            jax.ShapeDtypeStruct((QTR, 2 * HD), BF),
        ),
        in_specs=[vmem] * 2,
        out_specs=(vmem,) * 4,
        name="emit",
    )(gx, gw)


def body(queries, keys, values, out_grad, normed, w_query, w_key, w_value, valid_len):
    chip = lax.axis_index("seq") // 2
    inverse_freq = ROPE_BASE ** (-(jnp.arange(HD // 2, dtype=F32) * (2.0 / HD)))
    slots = (chip * 2 * TOK + jnp.arange(2 * TOK, dtype=jnp.int32)).astype(F32).reshape(2, 1, TOK)
    angles = slots * inverse_freq[None, :, None]
    cos, sin = jnp.cos(angles), jnp.sin(angles)
    base = (2 * chip - 8).astype(jnp.int32).reshape(1)
    weights = (w_query, w_key, w_value)
    lines = [[2 * z + yl for z in range(4)] for yl in range(2)]
    w_rows = lax.all_to_all(pack(weights), "head", 0, 0, axis_index_groups=lines, tiled=True)
    qg, kv, turned = gather(queries, keys, values, out_grad, normed)
    dq, dkv, own = attend(valid_len, base, qg, kv, cos, sin)
    gx, gq, gk, gv = emit(*finish(dq, dkv, own, turned, weights, w_rows, cos, sin))
    return gx.T, gq, gk, gv


def solution(mesh):
    both = P("seq", "head")
    placed = (both, both, both, both, P("seq", None), P(None, "head"), P(None, "head"), P(None, "head"), P())
    return jax.shard_map(
        body, mesh=mesh, in_specs=placed, out_specs=(both,) * 4, check_vma=False
    )
```

```python
import functools

import jax
import jax.numpy as jnp
from jax import lax
from jax.experimental import pallas as pl
from jax.experimental.pallas import tpu as pltpu
from jax.sharding import PartitionSpec as P

D = 4608
H = 32
HD = 128
WINDOW = 4096
SOFT_CAP = 50.0
ROPE_BASE = 10000.0
SCALE = (D // H) ** (-0.5)

TOK = 512
NB = 10
TILE = 256
CHUNK = D // 4
HALF = CHUNK // 2
QTR = HALF // 2

BF = jnp.bfloat16
F32 = jnp.float32
MESH = pl.DeviceIdType.MESH
STEPS = (1, -1, 2)
LOG2E = 1.4426950408889634


def nt(left, right):
    return lax.dot_general(left, right, (((1,), (1,)), ((), ())), preferred_element_type=F32)


def nn(left, right):
    return lax.dot_general(left, right, (((1,), (0,)), ((), ())), preferred_element_type=F32)


def here():
    s, h = lax.axis_index("seq"), lax.axis_index("head")
    return s // 4, (s // 2) % 2, s % 2, h // 2, h % 2


def at_seq(x, yh, core):
    return {"seq": (lax.rem(x + 4, 4) * 2 + yh) * 2 + core, "head": lax.axis_index("head")}


def at_head(z, yl):
    return {"seq": lax.axis_index("seq"), "head": lax.rem(z + 4, 4) * 2 + yl}


def at_core(z, yl, core):
    s = lax.axis_index("seq")
    return {"seq": s - s % 2 + core, "head": lax.rem(z + 4, 4) * 2 + yl}


def remote(src, dst, send, recv, device):
    return pltpu.make_async_remote_copy(
        src_ref=src, dst_ref=dst, send_sem=send, recv_sem=recv, device_id=device, device_id_type=MESH
    )


def greet(devices):
    barrier = pltpu.get_barrier_semaphore()
    for device in devices:
        pl.semaphore_signal(barrier, inc=1, device_id=device, device_id_type=MESH)
    pl.semaphore_wait(barrier, len(devices))


def pack_kernel(wq, wk, wv, out, sem):
    _, _, core, _, _ = here()
    copies = []
    for i in range(4):
        rows = pl.ds(pl.multiple_of(i * CHUNK + core * HALF, HALF), HALF)
        for j, (ref, first, last) in enumerate(((wq, 0, 4), (wk, 4, 6), (wv, 6, 8))):
            to = out.at[i, :, first * HD : last * HD]
            copies.append(pltpu.make_async_copy(ref.at[rows], to, sem.at[i, j]))
    for copy in copies:
        copy.start()
    for copy in copies:
        copy.wait()


def pack(weights):
    hbm = pl.BlockSpec(memory_space=pltpu.HBM)
    return pl.pallas_call(
        pack_kernel,
        out_shape=jax.ShapeDtypeStruct((4, HALF, 8 * HD), BF),
        in_specs=[hbm] * 3,
        out_specs=pl.BlockSpec(memory_space=pltpu.VMEM),
        scratch_shapes=[pltpu.SemaphoreType.DMA((4, 3))],
        compiler_params=pltpu.CompilerParams(vmem_limit_bytes=60 << 20),
        name="pack",
    )(*weights)


def gather_kernel(
    q, g, k, v, n_hbm, qg, kv, nt_out, kv_own, qg_own, n_ref, turned,
    n_load_sem, kv_load, qg_load, kv_loc, qg_loc, swap_send, swap_recv,
    x_send, x_recv, y_send, y_recv, n_sem, n_send, n_recv,
):
    x, yh, core, _, _ = here()
    other = 1 - core
    partner = at_seq(x, yh, other)
    across = at_seq(x, 1 - yh, core)

    def stage(pair, to, width, sems):
        return [
            pltpu.make_async_copy(
                ref.at[:, head * width : (head + 1) * width], to.at[head, kind], sems.at[head, kind]
            )
            for head in range(2)
            for kind, ref in enumerate(pair)
        ]

    kv_stage = stage((k, v), kv_own, HD, kv_load)
    qg_stage = stage((q, g), qg_own, 2 * HD, qg_load)
    n_load = pltpu.make_async_copy(n_hbm, n_ref, n_load_sem)
    for copy in kv_stage + qg_stage + [n_load]:
        copy.start()
    greet(
        [partner, across]
        + [at_seq(x + step, yh, c) for step in (1, -1, 2) for c in range(2)]
    )
    for copy in kv_stage:
        copy.wait()
    along = [
        [
            remote(
                kv_own.at[head],
                kv.at[8 - 4 * step + core],
                x_send.at[step - 1, head],
                x_recv.at[step - 1, core],
                at_seq(x + step, yh, head),
            )
            for head in range(2)
        ]
        for step in (1, 2)
    ]
    kv_swap = remote(kv_own.at[other], kv.at[8 + core], swap_send.at[0], swap_recv.at[0], partner)
    kv_keep = pltpu.make_async_copy(kv_own.at[core], kv.at[8 + core], kv_loc)
    qg_swap = remote(qg_own.at[other], qg.at[core], swap_send.at[1], swap_recv.at[1], partner)
    qg_keep = pltpu.make_async_copy(qg_own.at[core], qg.at[core], qg_loc)
    kv_swap.start()
    kv_keep.start()
    for copy in along[0] + along[1]:
        copy.start()

    def arrived(step, c):
        dst = kv.at[8 - 4 * step + c]
        remote(dst, dst, x_send.at[step - 1, c], x_recv.at[step - 1, c], partner).wait_recv()

    def turn(i, carry):
        cols = pl.ds(pl.multiple_of(i * HD, HD), HD)
        turned[cols, :] = n_ref[:, cols].T
        return carry

    first_src = jnp.where(yh == 0, 8, 4)
    second_src = jnp.where(yh == 0, 4, 0)
    first = [
        remote(kv.at[first_src + c], kv.at[6 + c], y_send.at[0, c], y_recv.at[0, c], across)
        for c in range(2)
    ]
    second = [
        remote(kv.at[second_src + c], kv.at[2 + c], y_send.at[1, c], y_recv.at[1, c], across)
        for c in range(2)
    ]
    kv_keep.wait()
    kv_swap.wait_recv()

    @pl.when(yh == 0)
    def _():
        for copy in first:
            copy.start()

    for copy in qg_stage:
        copy.wait()
    qg_swap.start()
    qg_keep.start()
    n_load.wait()
    lax.fori_loop(0, D // HD // 2, turn, 0)
    for c in range(2):
        arrived(1, c)

        @pl.when(yh == 0)
        def _():
            second[c].start()

        @pl.when(yh == 1)
        def _():
            first[c].start()

    lax.fori_loop(D // HD // 2, D // HD, turn, 0)
    n_local = pltpu.make_async_copy(turned, nt_out.at[core], n_sem)
    n_swap = remote(turned, nt_out.at[core], n_send, n_recv, partner)
    n_local.start()
    n_swap.start()
    for c in range(2):
        arrived(2, c)

        @pl.when(yh == 1)
        def _():
            second[c].start()

    n_local.wait()
    n_swap.wait()
    qg_keep.wait()
    qg_swap.wait()
    for copy in first + second:
        copy.wait()
    kv_swap.wait_send()
    for copy in along[0] + along[1]:
        copy.wait_send()


def gather(queries, keys, values, grads, normed):
    hbm = pl.BlockSpec(memory_space=pltpu.HBM)
    dma = pltpu.SemaphoreType.DMA
    return pl.pallas_call(
        gather_kernel,
        out_shape=(
            jax.ShapeDtypeStruct((2, 2, TOK, 2 * HD), BF),
            jax.ShapeDtypeStruct((NB, 2, TOK, HD), BF),
            jax.ShapeDtypeStruct((2, D, TOK), BF),
        ),
        in_specs=[hbm] * 5,
        out_specs=(hbm,) * 3,
        scratch_shapes=[
            pltpu.VMEM((2, 2, TOK, HD), BF),
            pltpu.VMEM((2, 2, TOK, 2 * HD), BF),
            pltpu.VMEM((TOK, D), BF),
            pltpu.VMEM((D, TOK), BF),
            dma, dma((2, 2)), dma((2, 2)), dma, dma, dma((2,)), dma((2,)),
            dma((2, 2)), dma((2, 2)), dma((2, 2)), dma((2, 2)), dma, dma, dma,
        ],
        compiler_params=pltpu.CompilerParams(
            collective_id=0, has_side_effects=True, vmem_limit_bytes=60 << 20
        ),
        name="gather",
    )(queries, grads, keys, values, normed)


STEP = 8
PIECES = 4 * NB
EMPTY = PIECES
OWN = PIECES + STEP


def attend_kernel(
    valid, base, qg, kv_hbm, cos, sin, dq_out, dkv_out, own_out,
    kv, e_s, w_s, kt_s, vt_s, o_acc, dq_acc, dk_acc, dv_acc, listed, sem,
):
    first_shard = base[0]
    load = pltpu.make_async_copy(kv_hbm, kv.at[pl.ds(0, NB)], sem)
    load.start()
    dk_acc[...] = jnp.zeros_like(dk_acc)
    dv_acc[...] = jnp.zeros_like(dv_acc)
    for k in range(STEP):
        kv[NB + k // 4, 0, k % 4] = jnp.zeros((HD, HD), BF)
        kv[NB + k // 4, 1, k % 4] = jnp.zeros((HD, HD), BF)
        kt_s[EMPTY + k] = jnp.zeros((HD, HD), BF)
        vt_s[EMPTY + k] = jnp.zeros((HD + 16, HD), BF)
    load.wait()

    def valid_of(b):
        return valid[jnp.maximum(first_shard + b, 0)]

    def turn(b, carry):
        for k in range(4):
            live = lax.broadcasted_iota(jnp.int32, (HD + 16, HD), 1) + k * HD < valid_of(b)
            k_t = kv[b, 0, k].T
            v_t = jnp.concatenate([kv[b, 1, k].T, jnp.ones((16, HD), BF)], axis=0)
            kt_s[4 * b + k] = jnp.where(live[:HD], k_t.astype(F32), 0.0).astype(BF)
            vt_s[4 * b + k] = jnp.where(live, v_t.astype(F32), 0.0).astype(BF)

            @pl.when(b >= 8)
            def _():
                kt_s[OWN + 4 * (b - 8) + k] = k_t
                vt_s[OWN + 4 * (b - 8) + k] = v_t

        return carry

    lax.fori_loop(0, NB, turn, 0)
    key_iota = lax.broadcasted_iota(jnp.int32, (TILE, 2 * TILE), 0)
    query_iota = lax.rem(lax.broadcasted_iota(jnp.int32, (TILE, 2 * TILE), 1), TILE)

    def query_tile(i, carry):
        r, qt = i // 2, lax.rem(i, 2)
        q_valid = valid_of(8 + r)
        q_rows = pl.ds(pl.multiple_of(qt * TILE, TILE), TILE)
        lanes = q_rows

        @pl.when(qt * TILE >= q_valid)
        def _():
            dq_out[r, :, lanes] = jnp.zeros((2 * HD, TILE), BF)

        @pl.when(qt * TILE < q_valid)
        def _():
            def note(t, count):
                j, k = t // 4, lax.rem(t, 4)
                b = r + j
                wanted = (
                    (first_shard + b >= 0)
                    & (k * HD < valid_of(b))
                    & jnp.logical_not((j == 0) & (k < 2 * qt + 2))
                    & jnp.logical_not((j == 8) & (k >= 2 * qt))
                )
                listed[count] = jnp.where(wanted, 4 * b + k, EMPTY)
                return count + wanted.astype(jnp.int32)

            count = lax.fori_loop(0, 36, note, 0)
            for extra in range(STEP - 1):
                listed[count + extra] = EMPTY + extra
            steps = (count + STEP - 1) // STEP
            doubles = steps // 2

            q_two = qg[r, 0, q_rows, :]
            g_two = qg[r, 1, q_rows, :]
            q_rows2 = jnp.concatenate([q_two[:, :HD], q_two[:, HD:]], axis=0)
            q_t = q_rows2.T

            def keys_of(kind, pieces):
                return jnp.concatenate([kv[p // 4, kind, lax.rem(p, 4)] for p in pieces], axis=0)

            def turned_of(ref, pieces):
                return jnp.concatenate([ref[p] for p in pieces], axis=1)

            def forward(pieces, turned, slot, mask):
                parts = []
                for n in range(0, len(pieces), 2):
                    keys = keys_of(0, pieces[n : n + 2])
                    rows = pl.ds(pl.multiple_of(slot + n * HD, TILE), TILE)
                    heads = []
                    for head in range(2):
                        cols = slice(head * TILE, (head + 1) * TILE)
                        th = jnp.tanh(nn(keys, q_t[:, cols]) * (SCALE / SOFT_CAP))
                        e = jnp.exp2(th * (SOFT_CAP * LOG2E))
                        if mask is not None:
                            e = jnp.where(mask[n // 2][:, cols], e, 0.0)
                        eb = e.astype(BF)
                        e_s[rows, cols] = eb
                        w_s[rows, cols] = (e * (1.0 - th * th)).astype(BF)
                        heads.append(eb)
                    parts.append(heads)
                for head in range(2):
                    cols = slice(head * TILE, (head + 1) * TILE)
                    column = jnp.concatenate([p[head] for p in parts], axis=0)
                    o_acc[:, cols] += nn(turned_of(vt_s, turned), column)

            gap = query_iota - key_iota
            key_pos = key_iota + qt * TILE
            oldest_there = first_shard + r >= 0
            edge_mask = (
                gap + 8 * TOK < WINDOW,
                (gap >= 0) & ((key_pos < q_valid) | (gap == 0)),
            )
            old = jnp.where(oldest_there, 4 * r + 2 * qt, EMPTY)
            own = 4 * (8 + r) + 2 * qt
            edge = (old, old + 1, own, own + 1)
            edge_turned = (old, old + 1, OWN + 4 * r + 2 * qt, OWN + 4 * r + 2 * qt + 1)
            o_acc[...] = jnp.zeros_like(o_acc)
            forward(edge, edge_turned, 0, edge_mask)

            def forward_step(width, n, carry):
                pieces = tuple(listed[n * width + m] for m in range(width))
                forward(pieces, pieces, (4 + n * width) * HD, None)
                return carry

            lax.fori_loop(0, doubles, functools.partial(forward_step, 2 * STEP), 0)
            lax.fori_loop(2 * doubles, steps, functools.partial(forward_step, STEP), 0)
            inv = 1.0 / o_acc[HD : HD + 1, :]
            g_rows2 = jnp.concatenate([g_two[:, :HD], g_two[:, HD:]], axis=0).astype(F32)
            live = query_iota[:1, :] + qt * TILE < q_valid
            g_t = jnp.where(live, g_rows2.T, 0.0) * inv
            delta = jnp.sum(g_t * o_acc[:HD, :], axis=0, keepdims=True) * inv
            gs_t = g_t.astype(BF)
            gs = g_t.T.astype(BF)
            dq_acc[...] = jnp.zeros_like(dq_acc)

            def backward(pieces, turned, slot):
                rows = pl.ds(pl.multiple_of(slot, TILE), len(pieces) * HD)
                columns = []
                for head in range(2):
                    cols = slice(head * TILE, (head + 1) * TILE)
                    parts = []
                    for n in range(0, len(pieces), 2):
                        part = pl.ds(pl.multiple_of(slot + n * HD, TILE), TILE)
                        dp = nn(keys_of(1, pieces[n : n + 2]), gs_t[:, cols])
                        parts.append((w_s[part, cols].astype(F32) * (dp - delta[:, cols])).astype(BF))
                    columns.append(jnp.concatenate(parts, axis=0))
                ds = jnp.concatenate(columns, axis=1)
                dq_acc[...] += nn(turned_of(kt_s, turned), ds)
                dk = nn(ds, q_rows2)
                dv = nn(e_s[rows, :], gs)
                for n, p in enumerate(pieces):
                    dk_acc[p] += dk[n * HD : (n + 1) * HD]
                    dv_acc[p] += dv[n * HD : (n + 1) * HD]

            backward(edge, edge_turned, 0)

            def backward_step(width, n, carry):
                pieces = tuple(listed[n * width + m] for m in range(width))
                backward(pieces, pieces, (4 + n * width) * HD)
                return carry

            lax.fori_loop(0, doubles, functools.partial(backward_step, 2 * STEP), 0)
            lax.fori_loop(2 * doubles, steps, functools.partial(backward_step, STEP), 0)
            dq = dq_acc[...] * SCALE
            c, s = cos[r, :, lanes], sin[r, :, lanes]
            for head in range(2):
                a = dq[: HD // 2, head * TILE : (head + 1) * TILE]
                z = dq[HD // 2 :, head * TILE : (head + 1) * TILE]
                dq_out[r, head * HD : head * HD + HD // 2, lanes] = (a * c + z * s).astype(BF)
                dq_out[r, head * HD + HD // 2 : (head + 1) * HD, lanes] = (z * c - a * s).astype(BF)

        return carry

    lax.fori_loop(0, 4, query_tile, 0)

    def result(ref, b, k, scale):
        live = lax.broadcasted_iota(jnp.int32, (HD, HD), 0) + k * HD < valid_of(b)
        return jnp.where(live, ref[4 * b + k] * scale, 0.0)

    def give(b, carry):
        for k in range(4):
            rows = slice(k * HD, (k + 1) * HD)
            dkv_out[b, 0, rows, :] = result(dk_acc, b, k, SCALE).astype(BF)
            dkv_out[b, 1, rows, :] = result(dv_acc, b, k, 1.0).astype(BF)
        return carry

    lax.fori_loop(0, 8, give, 0)
    for r in range(2):
        for k in range(4):
            rows = slice(k * HD, (k + 1) * HD)
            own_out[r, 0, rows, :] = result(dk_acc, 8 + r, k, SCALE)
            own_out[r, 1, rows, :] = result(dv_acc, 8 + r, k, 1.0)


def attend(valid_len, base, qg, kv, cos, sin):
    vmem = pl.BlockSpec(memory_space=pltpu.VMEM)
    smem = pl.BlockSpec(memory_space=pltpu.SMEM)
    return pl.pallas_call(
        attend_kernel,
        out_shape=(
            jax.ShapeDtypeStruct((2, 2 * HD, TOK), BF),
            jax.ShapeDtypeStruct((8, 2, TOK, HD), BF),
            jax.ShapeDtypeStruct((2, 2, TOK, HD), F32),
        ),
        in_specs=[smem, smem, vmem, pl.BlockSpec(memory_space=pltpu.HBM), vmem, vmem],
        out_specs=(vmem,) * 3,
        scratch_shapes=[
            pltpu.VMEM((NB + STEP // 4, 2, 4, HD, HD), BF),
            pltpu.VMEM((44 * HD, 2 * TILE), BF),
            pltpu.VMEM((44 * HD, 2 * TILE), BF),
            pltpu.VMEM((OWN + 8, HD, HD), BF),
            pltpu.VMEM((OWN + 8, HD + 16, HD), BF),
            pltpu.VMEM((HD + 16, 2 * TILE), F32),
            pltpu.VMEM((HD, 2 * TILE), F32),
            pltpu.VMEM((PIECES + STEP, HD, HD), F32),
            pltpu.VMEM((PIECES + STEP, HD, HD), F32),
            pltpu.SMEM((48,), jnp.int32),
            pltpu.SemaphoreType.DMA,
        ],
        compiler_params=pltpu.CompilerParams(vmem_limit_bytes=58 << 20),
        cost_estimate=pl.CostEstimate(flops=26_000_000_000, bytes_accessed=8 << 20, transcendentals=20_000_000),
        name="attend",
    )(valid_len, base, qg, kv.reshape(NB, 2, 4, HD, HD), cos, sin)


PIECE = 256


def finish_kernel(
    dq, dkv, own_hbm, turned_hbm, wq, wk, wv, w_rows, cos, sin, gx_out, gw_out,
    own, n_buf, w_buf, t_buf, dkv_t, gq_buf, g_buf, zq_buf, y_buf, x_buf, near, far,
    xs, xr, xy, zy, half_buf,
    load_sem, dq_sems, dk_sems, y_sems, x_sems, ring_send, ring_recv, pair_sems, core_sems, g_send, g_recv,
    gq_send, gq_recv, w_load, w_send, w_recv,
):
    x, yh, core, z, yl = here()
    other = 1 - core
    partner = at_seq(x, yh, other)
    across = at_seq(x, 1 - yh, core)
    beside = at_head(z, 1 - yl)
    x_next, x_prev, x_far = at_seq(x + 1, yh, core), at_seq(x - 1, yh, core), at_seq(x + 2, yh, core)
    round_z = [[at_core(z + step, yl, c) for c in range(2)] for step in STEPS]
    greet([partner, across, beside, x_next, x_prev, x_far] + sum(round_z, []))

    y_copies = [
        [
            remote(dkv.at[6 - 4 * i + r], y_buf.at[i, r], y_sems.at[0, i, r], y_sems.at[1, i, r], across)
            for r in range(2)
        ]
        for i in range(2)
    ]
    for copy in y_copies[1] + y_copies[0]:
        copy.start()
    pairs = [
        (dkv.at[pl.ds(0, 2)], far),
        (dkv.at[pl.ds(4, 2)], near),
        (dq.at[0], t_buf.at[: 2 * HD, :TOK]),
        (dq.at[1], t_buf.at[: 2 * HD, TOK:]),
        (turned_hbm.at[0], n_buf.at[:, :TOK]),
        (turned_hbm.at[1], n_buf.at[:, TOK:]),
        (own_hbm, own),
    ]
    loads = [pltpu.make_async_copy(src, dst, load_sem.at[i]) for i, (src, dst) in enumerate(pairs)]
    for copy in loads:
        copy.start()
    q_spread = [
        remote(dq.at[r], gq_buf.at[i, core], gq_send.at[i, r], gq_recv.at[i, core], round_z[i][r])
        for i in range(3)
        for r in range(2)
    ]
    q_kin = remote(dq.at[other], gq_buf.at[3, core], dq_sems.at[0], dq_sems.at[1], partner)
    q_keep = pltpu.make_async_copy(dq.at[core], gq_buf.at[3, core], dq_sems.at[2])
    part = pl.ds(pl.multiple_of(core * HALF, HALF), HALF)
    own_rows = pl.ds(pl.multiple_of(z * CHUNK, CHUNK), CHUNK)
    w_from = [w_rows.at[lax.rem(z + 4 - step, 4)] for step in STEPS]
    w_in = [
        pltpu.make_async_copy(src, w_buf.at[i, part], w_load.at[i])
        for i, src in enumerate(w_from)
    ] + [
        pltpu.make_async_copy(ref.at[own_rows], w_buf.at[3, :, cols], w_load.at[3 + i])
        for i, (ref, cols) in enumerate(
            ((wq, slice(0, 4 * HD)), (wk, slice(4 * HD, 6 * HD)), (wv, slice(6 * HD, 8 * HD)))
        )
    ]
    w_on = [
        remote(src, w_buf.at[i, part], w_send.at[i], w_recv.at[i], partner)
        for i, src in enumerate(w_from)
    ]
    back_near, back_far = (
        [
            remote(src.at[r], x_buf.at[i, r], x_sems.at[0, i, r], x_sems.at[1, i, r], device)
            for r in range(2)
        ]
        for i, (src, device) in enumerate(((near, x_prev), (far, x_far)))
    )
    loads[0].wait()

    @pl.when(yh == 0)
    def _():
        for copy in back_far:
            copy.start()

    for copy in q_spread + [q_kin, q_keep] + w_on + w_in:
        copy.start()
    for copy in loads[1:]:
        copy.wait()

    def term(piece, rows):
        return nt(n_buf[rows, :], t_buf[piece * PIECE : (piece + 1) * PIECE, :])

    def compute(piece, slot, step):
        first_row = lax.rem(x + step, 4) * CHUNK

        def one(half, carry):
            to = pl.ds(pl.multiple_of(half * HALF, HALF), HALF)
            rows = pl.ds(pl.multiple_of(first_row + half * HALF, HALF), HALF)
            xs[piece, slot, to, :] = term(piece, rows).astype(BF)
            return carry

        lax.fori_loop(0, 2, one, 0)

    def ring(piece):
        out, come = xs.at[piece], xr.at[piece]
        top, low = pl.ds(0, HALF), pl.ds(HALF, HALF)
        spans = (
            (out.at[0, top], come.at[0, top], x_next),
            (out.at[0, low], come.at[0, low], x_prev),
            (out.at[1], come.at[1], x_next),
            (out.at[2], come.at[2], x_prev),
        )
        return [
            remote(src, dst, ring_send.at[piece, i], ring_recv.at[piece, i], device)
            for i, (src, dst, device) in enumerate(spans)
        ]

    rings = [ring(piece) for piece in range(2)]

    def launch(piece):
        compute(piece, 0, 2)
        rings[piece][0].start()
        rings[piece][1].start()

    def prepare(piece):
        compute(piece, 1, 1)
        compute(piece, 2, 3)

    def relay(piece):
        for way, rows in ((0, slice(0, HALF)), (1, slice(HALF, CHUNK))):
            rings[piece][way].wait()
            mine = xs[piece, 1 + way, rows, :].astype(F32)
            xs[piece, 1 + way, rows, :] = (mine + xr[piece, 0, rows, :].astype(F32)).astype(BF)
            rings[piece][2 + way].start()

    x0, x1, z0, z1 = jobs = ((0, 0), (0, 1), (1, 0), (1, 1))
    side, side_device, pair_buf = (yh, yl), (across, beside), (xy, zy)

    def pair(job):
        axis, piece = job
        buf = pair_buf[axis].at[piece]
        return remote(
            buf.at[0], buf.at[1], pair_sems.at[0, axis, piece], pair_sems.at[1, axis, piece], side_device[axis]
        )

    pairs_of = {job: pair(job) for job in jobs}

    def queries_part(half, carry):
        rows = pl.ds(pl.multiple_of(half * HALF, HALF), HALF)
        for piece in range(2):
            cols = slice(piece * PIECE, (piece + 1) * PIECE)
            total = jnp.zeros((HALF, PIECE), F32)
            for i in range(4):
                found = jnp.concatenate([gq_buf[i, head, :, cols] for head in range(2)], axis=0)
                total += nn(w_buf[i, rows, : 4 * HD], found)
            zq_buf[rows, cols] = total
        return carry

    def keys_part(piece, rows):
        total = zq_buf[rows, piece * PIECE : (piece + 1) * PIECE]
        for i in range(4):
            found = [
                g_buf[i, head, piece, kind * HD : (kind + 1) * HD, :] for kind in range(2) for head in range(2)
            ]
            total += nn(w_buf[i, rows, 4 * HD :], jnp.concatenate(found, axis=0))
        return total

    def cross(job):
        axis, piece = job
        if axis == 0:
            rings[piece][2].wait()
            rings[piece][3].wait()

        def summed(half):
            rows = pl.ds(pl.multiple_of(half * HALF, HALF), HALF)
            if axis == 1:
                return keys_part(piece, rows).astype(BF)
            return (
                xs[piece, 3, rows, :].astype(F32)
                + xr[piece, 1, rows, :].astype(F32)
                + xr[piece, 2, rows, :].astype(F32)
            ).astype(BF)

        pair_buf[axis][piece, 0] = summed(1 - side[axis])
        pairs_of[job].start()
        pair_buf[axis][piece, 2] = summed(side[axis])

    def total_of(job):
        axis, piece = job
        pairs_of[job].wait()
        return (pair_buf[axis][piece, 1].astype(F32) + pair_buf[axis][piece, 2].astype(F32)).astype(BF)

    my_rows = pl.ds(pl.multiple_of(core * QTR, QTR), QTR)
    its_rows = pl.ds(pl.multiple_of(other * QTR, QTR), QTR)
    lasts = [
        remote(half_buf.at[piece, its_rows], gw_out.at[piece, core], core_sems.at[0, piece], core_sems.at[1, piece], partner)
        for piece in range(2)
    ]

    def swap(piece):
        half_buf[piece] = total_of((0, piece))
        lasts[piece].start()
        gw_out[piece, core] = half_buf[piece, my_rows, :]


    def add_to(ref, index, r):
        ref[r] = (ref[r].astype(F32) + y_buf[index, r].astype(F32)).astype(BF)

    def further(r):
        y_copies[1][r].wait()

        @pl.when(yh == 0)
        def _():
            add_to(near, 1, r)
            back_near[r].start()

        @pl.when(yh == 1)
        def _():
            add_to(far, 1, r)
            back_far[r].start()

    def nearer(r):
        y_copies[0][r].wait()

        @pl.when(yh == 1)
        def _():
            add_to(near, 0, r)
            back_near[r].start()

    launch(0)
    prepare(0)
    compute(0, 3, 0)
    for r in range(2):
        further(r)
    for r in range(2):
        nearer(r)
    for copy in w_in + w_on + [q_kin, q_keep]:
        copy.wait()
    for i in range(3):
        for head in range(2):
            come = gq_buf.at[i, head]
            remote(come, come, gq_send.at[i, head], gq_recv.at[i, head], partner).wait_recv()
    lax.fori_loop(0, 2, queries_part, 0)
    keep = (yh == 0).astype(F32)
    for copy in back_far + back_near:
        copy.wait()
    for r in range(2):
        for kind in range(2):
            total = (
                own[r, kind]
                + y_buf[0, r, kind].astype(F32) * keep
                + x_buf[0, r, kind].astype(F32)
                + x_buf[1, r, kind].astype(F32)
            ).T
            if kind == 0:
                a, b = total[: HD // 2, :], total[HD // 2 :, :]
                c, s = cos[r], sin[r]
                total = jnp.concatenate([a * c + b * s, b * c - a * s], axis=0)
            total = total.astype(BF)
            t_buf[(2 + kind) * HD : (3 + kind) * HD, r * TOK : (r + 1) * TOK] = total
            for piece in range(2):
                dkv_t[r, piece, kind * HD : (kind + 1) * HD, :] = total[:, piece * PIECE : (piece + 1) * PIECE]
    spread = [
        [
            remote(dkv_t.at[r, piece], g_buf.at[i, core, piece], g_send.at[i, r, piece], g_recv.at[i, core, piece], round_z[i][r])
            for i in range(3)
            for r in range(2)
        ]
        for piece in range(2)
    ]
    kin = [
        remote(dkv_t.at[other, piece], g_buf.at[3, core, piece], dk_sems.at[0, piece], dk_sems.at[1, piece], partner)
        for piece in range(2)
    ]
    for piece in range(2):
        for copy in spread[piece] + [kin[piece]]:
            copy.start()
        g_buf[3, core, piece] = dkv_t[core, piece]

    def gathered(piece):
        kin[piece].wait()
        for i in range(3):
            for head in range(2):
                come = g_buf.at[i, head, piece]
                remote(come, come, g_send.at[i, head, piece], g_recv.at[i, head, piece], partner).wait_recv()

    launch(1)
    relay(0)
    prepare(1)
    compute(1, 3, 0)
    relay(1)
    gathered(0)
    cross(z0)
    cross(x0)
    gathered(1)
    cross(z1)
    swap(0)
    cross(x1)
    gx_out[:, :PIECE] = total_of(z0)
    swap(1)
    gx_out[:, PIECE:] = total_of(z1)
    for copy in lasts:
        copy.wait()
    for copy in q_spread + spread[0] + spread[1]:
        copy.wait_send()


def finish(dq, dkv, own, turned, weights, w_rows, cos, sin):
    vmem = pl.BlockSpec(memory_space=pltpu.VMEM)
    hbm = pl.BlockSpec(memory_space=pltpu.HBM)
    any_space = pl.BlockSpec(memory_space=pl.ANY)
    dma = pltpu.SemaphoreType.DMA
    return pl.pallas_call(
        finish_kernel,
        out_shape=(
            jax.ShapeDtypeStruct((HALF, TOK), BF),
            jax.ShapeDtypeStruct((2, 2, QTR, PIECE), BF),
        ),
        in_specs=[any_space] * 3 + [hbm] * 5 + [vmem, vmem],
        out_specs=(vmem,) * 2,
        scratch_shapes=[
            pltpu.VMEM((2, 2, TOK, HD), F32),
            pltpu.VMEM((D, 2 * TOK), BF),
            pltpu.VMEM((4, CHUNK, 8 * HD), BF),
            pltpu.VMEM((4 * HD, 2 * TOK), BF),
            pltpu.VMEM((2, 2, 2 * HD, PIECE), BF),
            pltpu.VMEM((4, 2, 2 * HD, TOK), BF),
            pltpu.VMEM((4, 2, 2, 2 * HD, PIECE), BF),
            pltpu.VMEM((CHUNK, TOK), F32),
            pltpu.VMEM((2, 2, 2, TOK, HD), BF),
            pltpu.VMEM((2, 2, 2, TOK, HD), BF),
            pltpu.VMEM((2, 2, TOK, HD), BF),
            pltpu.VMEM((2, 2, TOK, HD), BF),
            pltpu.VMEM((2, 4, CHUNK, PIECE), BF),
            pltpu.VMEM((2, 3, CHUNK, PIECE), BF),
            pltpu.VMEM((2, 3, HALF, PIECE), BF),
            pltpu.VMEM((2, 3, HALF, PIECE), BF),
            pltpu.VMEM((2, HALF, PIECE), BF),
            dma((8,)), dma((3,)), dma((2, 2)), dma((2, 2, 2)), dma((2, 2, 2)),
            dma((2, 4)), dma((2, 4)), dma((2, 2, 2)), dma((2, 2)), dma((3, 2, 2)), dma((3, 2, 2)),
            dma((3, 2)), dma((3, 2)), dma((6,)), dma((3,)), dma((3,)),
        ],
        compiler_params=pltpu.CompilerParams(
            collective_id=1, has_side_effects=True, vmem_limit_bytes=54 << 20
        ),
        name="finish",
    )(dq, dkv, own, turned, *weights, w_rows, cos, sin)


def emit_kernel(gx, gw, gx_out, gq_out, gk_out, gv_out):
    gx_out[...] = gx[...]
    for head in range(2):
        gq_out[:, head * 2 * HD : (head + 1) * 2 * HD] = gw[0, head]
        gk_out[:, head * HD : (head + 1) * HD] = gw[1, head, :, :HD]
        gv_out[:, head * HD : (head + 1) * HD] = gw[1, head, :, HD:]


def emit(gx, gw):
    vmem = pl.BlockSpec(memory_space=pltpu.VMEM)
    return pl.pallas_call(
        emit_kernel,
        out_shape=(
            jax.ShapeDtypeStruct((HALF, TOK), BF),
            jax.ShapeDtypeStruct((QTR, 4 * HD), BF),
            jax.ShapeDtypeStruct((QTR, 2 * HD), BF),
            jax.ShapeDtypeStruct((QTR, 2 * HD), BF),
        ),
        in_specs=[vmem] * 2,
        out_specs=(vmem,) * 4,
        name="emit",
    )(gx, gw)


def body(queries, keys, values, out_grad, normed, w_query, w_key, w_value, valid_len):
    chip = lax.axis_index("seq") // 2
    inverse_freq = ROPE_BASE ** (-(jnp.arange(HD // 2, dtype=F32) * (2.0 / HD)))
    slots = (chip * 2 * TOK + jnp.arange(2 * TOK, dtype=jnp.int32)).astype(F32).reshape(2, 1, TOK)
    angles = slots * inverse_freq[None, :, None]
    cos, sin = jnp.cos(angles), jnp.sin(angles)
    base = (2 * chip - 8).astype(jnp.int32).reshape(1)
    weights = (w_query, w_key, w_value)
    lines = [[2 * z + yl for z in range(4)] for yl in range(2)]
    w_rows = lax.all_to_all(pack(weights), "head", 0, 0, axis_index_groups=lines, tiled=True)
    qg, kv, turned = gather(queries, keys, values, out_grad, normed)
    dq, dkv, own = attend(valid_len, base, qg, kv, cos, sin)
    gx, gq, gk, gv = emit(*finish(dq, dkv, own, turned, weights, w_rows, cos, sin))
    return gx.T, gq, gk, gv


def solution(mesh):
    both = P("seq", "head")
    placed = (both, both, both, both, P("seq", None), P(None, "head"), P(None, "head"), P(None, "head"), P())
    return jax.shard_map(
        body, mesh=mesh, in_specs=placed, out_specs=(both,) * 4, check_vma=False
    )
```

```python
import functools

import jax
import jax.numpy as jnp
import numpy as np
from jax import lax
from jax.experimental import pallas as pl
from jax.experimental.pallas import tpu as pltpu
from jax.sharding import PartitionSpec as P

D = 4608
H = 32
HD = 128
WINDOW = 4096
SOFT_CAP = 50.0
ROPE_BASE = 10000.0
SCALE = (D // H) ** (-0.5)

TOK = 512
NB = 10
TILE = 256
CHUNK = D // 4
HALF = CHUNK // 2
QTR = HALF // 2

BF = jnp.bfloat16
F32 = jnp.float32
MESH = pl.DeviceIdType.MESH
STEPS = (1, -1, 2)
LOG2E = 1.4426950408889634


def nt(left, right):
    return lax.dot_general(left, right, (((1,), (1,)), ((), ())), preferred_element_type=F32)


def nn(left, right):
    return lax.dot_general(left, right, (((1,), (0,)), ((), ())), preferred_element_type=F32)


def here():
    s, h = lax.axis_index("seq"), lax.axis_index("head")
    return s // 4, (s // 2) % 2, s % 2, h // 2, h % 2


def at_seq(x, yh, core):
    return {"seq": (lax.rem(x + 4, 4) * 2 + yh) * 2 + core, "head": lax.axis_index("head")}


def at_head(z, yl):
    return {"seq": lax.axis_index("seq"), "head": lax.rem(z + 4, 4) * 2 + yl}


def at_core(z, yl, core):
    s = lax.axis_index("seq")
    return {"seq": s - s % 2 + core, "head": lax.rem(z + 4, 4) * 2 + yl}


def remote(src, dst, send, recv, device):
    return pltpu.make_async_remote_copy(
        src_ref=src, dst_ref=dst, send_sem=send, recv_sem=recv, device_id=device, device_id_type=MESH
    )


def greet(devices):
    barrier = pltpu.get_barrier_semaphore()
    for device in devices:
        pl.semaphore_signal(barrier, inc=1, device_id=device, device_id_type=MESH)
    pl.semaphore_wait(barrier, len(devices))


def pack_kernel(wq, wk, wv, out, sem):
    _, _, core, _, _ = here()
    copies = []
    for i in range(4):
        rows = pl.ds(pl.multiple_of(i * CHUNK + core * HALF, HALF), HALF)
        for j, (ref, first, last) in enumerate(((wq, 0, 4), (wk, 4, 6), (wv, 6, 8))):
            to = out.at[i, :, first * HD : last * HD]
            copies.append(pltpu.make_async_copy(ref.at[rows], to, sem.at[i, j]))
    for copy in copies:
        copy.start()
    for copy in copies:
        copy.wait()


def pack(weights):
    hbm = pl.BlockSpec(memory_space=pltpu.HBM)
    return pl.pallas_call(
        pack_kernel,
        out_shape=jax.ShapeDtypeStruct((4, HALF, 8 * HD), BF),
        in_specs=[hbm] * 3,
        out_specs=pl.BlockSpec(memory_space=pltpu.VMEM),
        scratch_shapes=[pltpu.SemaphoreType.DMA((4, 3))],
        compiler_params=pltpu.CompilerParams(vmem_limit_bytes=60 << 20),
        name="pack",
    )(*weights)


def gather_kernel(
    q, g, k, v, n_hbm, qg, kv, nt_out, kv_own, qg_own, n_ref, turned,
    n_load_sem, kv_load, qg_load, kv_loc, qg_loc, swap_send, swap_recv,
    x_send, x_recv, y_send, y_recv, n_sem, n_send, n_recv,
):
    x, yh, core, _, _ = here()
    other = 1 - core
    partner = at_seq(x, yh, other)
    across = at_seq(x, 1 - yh, core)

    def stage(pair, to, width, sems):
        return [
            pltpu.make_async_copy(
                ref.at[:, head * width : (head + 1) * width], to.at[head, kind], sems.at[head, kind]
            )
            for head in range(2)
            for kind, ref in enumerate(pair)
        ]

    kv_stage = stage((k, v), kv_own, HD, kv_load)
    qg_stage = stage((q, g), qg_own, 2 * HD, qg_load)
    n_load = pltpu.make_async_copy(n_hbm, n_ref, n_load_sem)
    for copy in kv_stage + qg_stage + [n_load]:
        copy.start()
    greet(
        [partner, across]
        + [at_seq(x + step, yh, c) for step in (1, -1, 2) for c in range(2)]
    )
    for copy in kv_stage:
        copy.wait()
    along = [
        [
            remote(
                kv_own.at[head],
                kv.at[8 - 4 * step + core],
                x_send.at[step - 1, head],
                x_recv.at[step - 1, core],
                at_seq(x + step, yh, head),
            )
            for head in range(2)
        ]
        for step in (1, 2)
    ]
    kv_swap = remote(kv_own.at[other], kv.at[8 + core], swap_send.at[0], swap_recv.at[0], partner)
    kv_keep = pltpu.make_async_copy(kv_own.at[core], kv.at[8 + core], kv_loc)
    qg_swap = remote(qg_own.at[other], qg.at[core], swap_send.at[1], swap_recv.at[1], partner)
    qg_keep = pltpu.make_async_copy(qg_own.at[core], qg.at[core], qg_loc)
    kv_swap.start()
    kv_keep.start()
    for copy in along[0] + along[1]:
        copy.start()

    def arrived(step, c):
        dst = kv.at[8 - 4 * step + c]
        remote(dst, dst, x_send.at[step - 1, c], x_recv.at[step - 1, c], partner).wait_recv()

    def turn(i, carry):
        cols = pl.ds(pl.multiple_of(i * HD, HD), HD)
        turned[cols, :] = n_ref[:, cols].T
        return carry

    first_src = jnp.where(yh == 0, 8, 4)
    second_src = jnp.where(yh == 0, 4, 0)
    first = [
        remote(kv.at[first_src + c], kv.at[6 + c], y_send.at[0, c], y_recv.at[0, c], across)
        for c in range(2)
    ]
    second = [
        remote(kv.at[second_src + c], kv.at[2 + c], y_send.at[1, c], y_recv.at[1, c], across)
        for c in range(2)
    ]
    kv_keep.wait()
    kv_swap.wait_recv()

    @pl.when(yh == 0)
    def _():
        for copy in first:
            copy.start()

    for copy in qg_stage:
        copy.wait()
    qg_swap.start()
    qg_keep.start()
    n_load.wait()
    lax.fori_loop(0, D // HD // 2, turn, 0)
    for c in range(2):
        arrived(1, c)

        @pl.when(yh == 0)
        def _():
            second[c].start()

        @pl.when(yh == 1)
        def _():
            first[c].start()

    lax.fori_loop(D // HD // 2, D // HD, turn, 0)
    n_local = pltpu.make_async_copy(turned, nt_out.at[core], n_sem)
    n_swap = remote(turned, nt_out.at[core], n_send, n_recv, partner)
    n_local.start()
    n_swap.start()
    for c in range(2):
        arrived(2, c)

        @pl.when(yh == 1)
        def _():
            second[c].start()

    n_local.wait()
    n_swap.wait()
    qg_keep.wait()
    qg_swap.wait()
    for copy in first + second:
        copy.wait()
    kv_swap.wait_send()
    for copy in along[0] + along[1]:
        copy.wait_send()


def gather(queries, keys, values, grads, normed):
    hbm = pl.BlockSpec(memory_space=pltpu.HBM)
    dma = pltpu.SemaphoreType.DMA
    return pl.pallas_call(
        gather_kernel,
        out_shape=(
            jax.ShapeDtypeStruct((2, 2, TOK, 2 * HD), BF),
            jax.ShapeDtypeStruct((NB, 2, TOK, HD), BF),
            jax.ShapeDtypeStruct((2, D, TOK), BF),
        ),
        in_specs=[hbm] * 5,
        out_specs=(hbm,) * 3,
        scratch_shapes=[
            pltpu.VMEM((2, 2, TOK, HD), BF),
            pltpu.VMEM((2, 2, TOK, 2 * HD), BF),
            pltpu.VMEM((TOK, D), BF),
            pltpu.VMEM((D, TOK), BF),
            dma, dma((2, 2)), dma((2, 2)), dma, dma, dma((2,)), dma((2,)),
            dma((2, 2)), dma((2, 2)), dma((2, 2)), dma((2, 2)), dma, dma, dma,
        ],
        compiler_params=pltpu.CompilerParams(
            collective_id=0, has_side_effects=True, vmem_limit_bytes=60 << 20
        ),
        name="gather",
    )(queries, grads, keys, values, normed)


STEP = 8
PIECES = 4 * NB
EMPTY = PIECES
OWN = PIECES + STEP


def attend_kernel(
    valid, base, qg, kv_hbm, cos, sin, dq_out, dkv_out, own_out,
    kv, e_s, w_s, kt_s, vt_s, o_acc, dq_acc, dk_acc, dv_acc, listed, sem,
):
    first_shard = base[0]
    load = pltpu.make_async_copy(kv_hbm, kv.at[pl.ds(0, NB)], sem)
    load.start()
    dk_acc[...] = jnp.zeros_like(dk_acc)
    dv_acc[...] = jnp.zeros_like(dv_acc)
    for k in range(STEP):
        kv[NB + k // 4, 0, k % 4] = jnp.zeros((HD, HD), BF)
        kv[NB + k // 4, 1, k % 4] = jnp.zeros((HD, HD), BF)
        kt_s[EMPTY + k] = jnp.zeros((HD, HD), BF)
        vt_s[EMPTY + k] = jnp.zeros((HD + 16, HD), BF)
    load.wait()

    def valid_of(b):
        return valid[jnp.maximum(first_shard + b, 0)]

    def turn(b, carry):
        for k in range(4):
            live = lax.broadcasted_iota(jnp.int32, (HD + 16, HD), 1) + k * HD < valid_of(b)
            k_t = kv[b, 0, k].T
            v_t = jnp.concatenate([kv[b, 1, k].T, jnp.ones((16, HD), BF)], axis=0)
            kt_s[4 * b + k] = jnp.where(live[:HD], k_t.astype(F32), 0.0).astype(BF)
            vt_s[4 * b + k] = jnp.where(live, v_t.astype(F32), 0.0).astype(BF)

            @pl.when(b >= 8)
            def _():
                kt_s[OWN + 4 * (b - 8) + k] = k_t
                vt_s[OWN + 4 * (b - 8) + k] = v_t

        return carry

    lax.fori_loop(0, NB, turn, 0)
    key_iota = lax.broadcasted_iota(jnp.int32, (TILE, 2 * TILE), 0)
    query_iota = lax.rem(lax.broadcasted_iota(jnp.int32, (TILE, 2 * TILE), 1), TILE)

    def query_tile(i, carry):
        r, qt = i // 2, lax.rem(i, 2)
        q_valid = valid_of(8 + r)
        q_rows = pl.ds(pl.multiple_of(qt * TILE, TILE), TILE)
        lanes = q_rows

        @pl.when(qt * TILE >= q_valid)
        def _():
            dq_out[r, :, lanes] = jnp.zeros((2 * HD, TILE), BF)

        @pl.when(qt * TILE < q_valid)
        def _():
            def note(t, count):
                j, k = t // 4, lax.rem(t, 4)
                b = r + j
                wanted = (
                    (first_shard + b >= 0)
                    & (k * HD < valid_of(b))
                    & jnp.logical_not((j == 0) & (k < 2 * qt + 2))
                    & jnp.logical_not((j == 8) & (k >= 2 * qt))
                )
                listed[count] = jnp.where(wanted, 4 * b + k, EMPTY)
                return count + wanted.astype(jnp.int32)

            count = lax.fori_loop(0, 36, note, 0)
            for extra in range(STEP - 1):
                listed[count + extra] = EMPTY + extra
            steps = (count + STEP - 1) // STEP
            doubles = steps // 2

            q_two = qg[r, 0, q_rows, :]
            g_two = qg[r, 1, q_rows, :]
            q_rows2 = jnp.concatenate([q_two[:, :HD], q_two[:, HD:]], axis=0)
            q_t = q_rows2.T

            def keys_of(kind, pieces):
                return jnp.concatenate([kv[p // 4, kind, lax.rem(p, 4)] for p in pieces], axis=0)

            def turned_of(ref, pieces):
                return jnp.concatenate([ref[p] for p in pieces], axis=1)

            def forward(pieces, turned, slot, mask):
                parts = []
                for n in range(0, len(pieces), 2):
                    keys = keys_of(0, pieces[n : n + 2])
                    rows = pl.ds(pl.multiple_of(slot + n * HD, TILE), TILE)
                    heads = []
                    for head in range(2):
                        cols = slice(head * TILE, (head + 1) * TILE)
                        th = jnp.tanh(nn(keys, q_t[:, cols]) * (SCALE / SOFT_CAP))
                        e = jnp.exp2(th * (SOFT_CAP * LOG2E))
                        if mask is not None:
                            e = jnp.where(mask[n // 2][:, cols], e, 0.0)
                        eb = e.astype(BF)
                        e_s[rows, cols] = eb
                        w_s[rows, cols] = (e * (1.0 - th * th)).astype(BF)
                        heads.append(eb)
                    parts.append(heads)
                for head in range(2):
                    cols = slice(head * TILE, (head + 1) * TILE)
                    column = jnp.concatenate([p[head] for p in parts], axis=0)
                    o_acc[:, cols] += nn(turned_of(vt_s, turned), column)

            gap = query_iota - key_iota
            key_pos = key_iota + qt * TILE
            oldest_there = first_shard + r >= 0
            edge_mask = (
                gap + 8 * TOK < WINDOW,
                (gap >= 0) & ((key_pos < q_valid) | (gap == 0)),
            )
            old = jnp.where(oldest_there, 4 * r + 2 * qt, EMPTY)
            own = 4 * (8 + r) + 2 * qt
            edge = (old, old + 1, own, own + 1)
            edge_turned = (old, old + 1, OWN + 4 * r + 2 * qt, OWN + 4 * r + 2 * qt + 1)
            o_acc[...] = jnp.zeros_like(o_acc)
            forward(edge, edge_turned, 0, edge_mask)

            def forward_step(width, n, carry):
                pieces = tuple(listed[n * width + m] for m in range(width))
                forward(pieces, pieces, (4 + n * width) * HD, None)
                return carry

            lax.fori_loop(0, doubles, functools.partial(forward_step, 2 * STEP), 0)
            lax.fori_loop(2 * doubles, steps, functools.partial(forward_step, STEP), 0)
            inv = 1.0 / o_acc[HD : HD + 1, :]
            g_rows2 = jnp.concatenate([g_two[:, :HD], g_two[:, HD:]], axis=0).astype(F32)
            live = query_iota[:1, :] + qt * TILE < q_valid
            g_t = jnp.where(live, g_rows2.T, 0.0) * inv
            delta = jnp.sum(g_t * o_acc[:HD, :], axis=0, keepdims=True) * inv
            gs_t = g_t.astype(BF)
            gs = g_t.T.astype(BF)
            dq_acc[...] = jnp.zeros_like(dq_acc)

            def backward(pieces, turned, slot):
                rows = pl.ds(pl.multiple_of(slot, TILE), len(pieces) * HD)
                columns = []
                for head in range(2):
                    cols = slice(head * TILE, (head + 1) * TILE)
                    parts = []
                    for n in range(0, len(pieces), 2):
                        part = pl.ds(pl.multiple_of(slot + n * HD, TILE), TILE)
                        dp = nn(keys_of(1, pieces[n : n + 2]), gs_t[:, cols])
                        parts.append((w_s[part, cols].astype(F32) * (dp - delta[:, cols])).astype(BF))
                    columns.append(jnp.concatenate(parts, axis=0))
                ds = jnp.concatenate(columns, axis=1)
                dq_acc[...] += nn(turned_of(kt_s, turned), ds)
                dk = nn(ds, q_rows2)
                dv = nn(e_s[rows, :], gs)
                for n, p in enumerate(pieces):
                    dk_acc[p] += dk[n * HD : (n + 1) * HD]
                    dv_acc[p] += dv[n * HD : (n + 1) * HD]

            backward(edge, edge_turned, 0)

            def backward_step(width, n, carry):
                pieces = tuple(listed[n * width + m] for m in range(width))
                backward(pieces, pieces, (4 + n * width) * HD)
                return carry

            lax.fori_loop(0, doubles, functools.partial(backward_step, 2 * STEP), 0)
            lax.fori_loop(2 * doubles, steps, functools.partial(backward_step, STEP), 0)
            dq = dq_acc[...] * SCALE
            c, s = cos[r, :, lanes], sin[r, :, lanes]
            for head in range(2):
                a = dq[: HD // 2, head * TILE : (head + 1) * TILE]
                z = dq[HD // 2 :, head * TILE : (head + 1) * TILE]
                dq_out[r, head * HD : head * HD + HD // 2, lanes] = (a * c + z * s).astype(BF)
                dq_out[r, head * HD + HD // 2 : (head + 1) * HD, lanes] = (z * c - a * s).astype(BF)

        return carry

    lax.fori_loop(0, 4, query_tile, 0)

    def result(ref, b, k, scale):
        live = lax.broadcasted_iota(jnp.int32, (HD, HD), 0) + k * HD < valid_of(b)
        return jnp.where(live, ref[4 * b + k] * scale, 0.0)

    def give(b, carry):
        for k in range(4):
            rows = slice(k * HD, (k + 1) * HD)
            dkv_out[b, 0, rows, :] = result(dk_acc, b, k, SCALE).astype(BF)
            dkv_out[b, 1, rows, :] = result(dv_acc, b, k, 1.0).astype(BF)
        return carry

    lax.fori_loop(0, 8, give, 0)
    for r in range(2):
        for k in range(4):
            rows = slice(k * HD, (k + 1) * HD)
            own_out[r, 0, rows, :] = result(dk_acc, 8 + r, k, SCALE)
            own_out[r, 1, rows, :] = result(dv_acc, 8 + r, k, 1.0)


def attend(valid_len, base, qg, kv, cos, sin):
    vmem = pl.BlockSpec(memory_space=pltpu.VMEM)
    smem = pl.BlockSpec(memory_space=pltpu.SMEM)
    return pl.pallas_call(
        attend_kernel,
        out_shape=(
            jax.ShapeDtypeStruct((2, 2 * HD, TOK), BF),
            jax.ShapeDtypeStruct((8, 2, TOK, HD), BF),
            jax.ShapeDtypeStruct((2, 2, TOK, HD), F32),
        ),
        in_specs=[smem, smem, vmem, pl.BlockSpec(memory_space=pltpu.HBM), vmem, vmem],
        out_specs=(vmem,) * 3,
        scratch_shapes=[
            pltpu.VMEM((NB + STEP // 4, 2, 4, HD, HD), BF),
            pltpu.VMEM((44 * HD, 2 * TILE), BF),
            pltpu.VMEM((44 * HD, 2 * TILE), BF),
            pltpu.VMEM((OWN + 8, HD, HD), BF),
            pltpu.VMEM((OWN + 8, HD + 16, HD), BF),
            pltpu.VMEM((HD + 16, 2 * TILE), F32),
            pltpu.VMEM((HD, 2 * TILE), F32),
            pltpu.VMEM((PIECES + STEP, HD, HD), F32),
            pltpu.VMEM((PIECES + STEP, HD, HD), F32),
            pltpu.SMEM((48,), jnp.int32),
            pltpu.SemaphoreType.DMA,
        ],
        compiler_params=pltpu.CompilerParams(vmem_limit_bytes=58 << 20),
        cost_estimate=pl.CostEstimate(flops=26_000_000_000, bytes_accessed=8 << 20, transcendentals=20_000_000),
        name="attend",
    )(valid_len, base, qg, kv.reshape(NB, 2, 4, HD, HD), cos, sin)


PIECE = 256


def finish_kernel(
    dq, dkv, own_hbm, turned_hbm, wq, wk, wv, w_rows, cos, sin, gx_out, gw_out,
    own, n_buf, w_buf, t_buf, dkv_t, gq_buf, g_buf, zq_buf, y_buf, x_buf, near, far,
    xs, xr, xy, zy, half_buf,
    load_sem, dq_sems, dk_sems, y_sems, x_sems, ring_send, ring_recv, pair_sems, core_sems, g_send, g_recv,
    gq_send, gq_recv, w_load, w_send, w_recv,
):
    x, yh, core, z, yl = here()
    other = 1 - core
    partner = at_seq(x, yh, other)
    across = at_seq(x, 1 - yh, core)
    beside = at_head(z, 1 - yl)
    x_next, x_prev, x_far = at_seq(x + 1, yh, core), at_seq(x - 1, yh, core), at_seq(x + 2, yh, core)
    round_z = [[at_core(z + step, yl, c) for c in range(2)] for step in STEPS]
    greet([partner, across, beside, x_next, x_prev, x_far] + sum(round_z, []))

    y_copies = [
        [
            remote(dkv.at[6 - 4 * i + r], y_buf.at[i, r], y_sems.at[0, i, r], y_sems.at[1, i, r], across)
            for r in range(2)
        ]
        for i in range(2)
    ]
    for copy in y_copies[1] + y_copies[0]:
        copy.start()
    pairs = [
        (dkv.at[pl.ds(0, 2)], far),
        (dkv.at[pl.ds(4, 2)], near),
        (dq.at[0], t_buf.at[: 2 * HD, :TOK]),
        (dq.at[1], t_buf.at[: 2 * HD, TOK:]),
        (turned_hbm.at[0], n_buf.at[:, :TOK]),
        (turned_hbm.at[1], n_buf.at[:, TOK:]),
        (own_hbm, own),
    ]
    loads = [pltpu.make_async_copy(src, dst, load_sem.at[i]) for i, (src, dst) in enumerate(pairs)]
    for copy in loads:
        copy.start()
    q_spread = [
        remote(dq.at[r], gq_buf.at[i, core], gq_send.at[i, r], gq_recv.at[i, core], round_z[i][r])
        for i in range(3)
        for r in range(2)
    ]
    q_kin = remote(dq.at[other], gq_buf.at[3, core], dq_sems.at[0], dq_sems.at[1], partner)
    q_keep = pltpu.make_async_copy(dq.at[core], gq_buf.at[3, core], dq_sems.at[2])
    part = pl.ds(pl.multiple_of(core * HALF, HALF), HALF)
    own_rows = pl.ds(pl.multiple_of(z * CHUNK, CHUNK), CHUNK)
    w_from = [w_rows.at[lax.rem(z + 4 - step, 4)] for step in STEPS]
    w_in = [
        pltpu.make_async_copy(src, w_buf.at[i, part], w_load.at[i])
        for i, src in enumerate(w_from)
    ] + [
        pltpu.make_async_copy(ref.at[own_rows], w_buf.at[3, :, cols], w_load.at[3 + i])
        for i, (ref, cols) in enumerate(
            ((wq, slice(0, 4 * HD)), (wk, slice(4 * HD, 6 * HD)), (wv, slice(6 * HD, 8 * HD)))
        )
    ]
    w_on = [
        remote(src, w_buf.at[i, part], w_send.at[i], w_recv.at[i], partner)
        for i, src in enumerate(w_from)
    ]
    back_near, back_far = (
        [
            remote(src.at[r], x_buf.at[i, r], x_sems.at[0, i, r], x_sems.at[1, i, r], device)
            for r in range(2)
        ]
        for i, (src, device) in enumerate(((near, x_prev), (far, x_far)))
    )
    loads[0].wait()

    @pl.when(yh == 0)
    def _():
        for copy in back_far:
            copy.start()

    for copy in q_spread + [q_kin, q_keep] + w_on + w_in:
        copy.start()
    for copy in loads[1:]:
        copy.wait()

    def term(piece, rows):
        return nt(n_buf[rows, :], t_buf[piece * PIECE : (piece + 1) * PIECE, :])

    def compute(piece, slot, step):
        first_row = lax.rem(x + step, 4) * CHUNK

        def one(half, carry):
            to = pl.ds(pl.multiple_of(half * HALF, HALF), HALF)
            rows = pl.ds(pl.multiple_of(first_row + half * HALF, HALF), HALF)
            xs[piece, slot, to, :] = term(piece, rows).astype(BF)
            return carry

        lax.fori_loop(0, 2, one, 0)

    def ring(piece):
        out, come = xs.at[piece], xr.at[piece]
        top, low = pl.ds(0, HALF), pl.ds(HALF, HALF)
        spans = (
            (out.at[0, top], come.at[0, top], x_next),
            (out.at[0, low], come.at[0, low], x_prev),
            (out.at[1], come.at[1], x_next),
            (out.at[2], come.at[2], x_prev),
        )
        return [
            remote(src, dst, ring_send.at[piece, i], ring_recv.at[piece, i], device)
            for i, (src, dst, device) in enumerate(spans)
        ]

    rings = [ring(piece) for piece in range(2)]

    def launch(piece):
        compute(piece, 0, 2)
        rings[piece][0].start()
        rings[piece][1].start()

    def prepare(piece):
        compute(piece, 1, 1)
        compute(piece, 2, 3)

    def relay(piece):
        for way, rows in ((0, slice(0, HALF)), (1, slice(HALF, CHUNK))):
            rings[piece][way].wait()
            mine = xs[piece, 1 + way, rows, :].astype(F32)
            xs[piece, 1 + way, rows, :] = (mine + xr[piece, 0, rows, :].astype(F32)).astype(BF)
            rings[piece][2 + way].start()

    x0, x1, z0, z1 = jobs = ((0, 0), (0, 1), (1, 0), (1, 1))
    side, side_device, pair_buf = (yh, yl), (across, beside), (xy, zy)

    def pair(job):
        axis, piece = job
        buf = pair_buf[axis].at[piece]
        return remote(
            buf.at[0], buf.at[1], pair_sems.at[0, axis, piece], pair_sems.at[1, axis, piece], side_device[axis]
        )

    pairs_of = {job: pair(job) for job in jobs}

    def queries_part(half, carry):
        rows = pl.ds(pl.multiple_of(half * HALF, HALF), HALF)
        for piece in range(2):
            cols = slice(piece * PIECE, (piece + 1) * PIECE)
            total = jnp.zeros((HALF, PIECE), F32)
            for i in range(4):
                found = jnp.concatenate([gq_buf[i, head, :, cols] for head in range(2)], axis=0)
                total += nn(w_buf[i, rows, : 4 * HD], found)
            zq_buf[rows, cols] = total
        return carry

    def keys_part(piece, rows):
        total = zq_buf[rows, piece * PIECE : (piece + 1) * PIECE]
        for i in range(4):
            found = [
                g_buf[i, head, piece, kind * HD : (kind + 1) * HD, :] for kind in range(2) for head in range(2)
            ]
            total += nn(w_buf[i, rows, 4 * HD :], jnp.concatenate(found, axis=0))
        return total

    def cross(job):
        axis, piece = job
        if axis == 0:
            rings[piece][2].wait()
            rings[piece][3].wait()

        def summed(half):
            rows = pl.ds(pl.multiple_of(half * HALF, HALF), HALF)
            if axis == 1:
                return keys_part(piece, rows).astype(BF)
            return (
                xs[piece, 3, rows, :].astype(F32)
                + xr[piece, 1, rows, :].astype(F32)
                + xr[piece, 2, rows, :].astype(F32)
            ).astype(BF)

        pair_buf[axis][piece, 0] = summed(1 - side[axis])
        pairs_of[job].start()
        pair_buf[axis][piece, 2] = summed(side[axis])

    def total_of(job):
        axis, piece = job
        pairs_of[job].wait()
        return (pair_buf[axis][piece, 1].astype(F32) + pair_buf[axis][piece, 2].astype(F32)).astype(BF)

    my_rows = pl.ds(pl.multiple_of(core * QTR, QTR), QTR)
    its_rows = pl.ds(pl.multiple_of(other * QTR, QTR), QTR)
    lasts = [
        remote(half_buf.at[piece, its_rows], gw_out.at[piece, core], core_sems.at[0, piece], core_sems.at[1, piece], partner)
        for piece in range(2)
    ]

    def swap(piece):
        half_buf[piece] = total_of((0, piece))
        lasts[piece].start()
        gw_out[piece, core] = half_buf[piece, my_rows, :]


    def add_to(ref, index, r):
        ref[r] = (ref[r].astype(F32) + y_buf[index, r].astype(F32)).astype(BF)

    def further(r):
        y_copies[1][r].wait()

        @pl.when(yh == 0)
        def _():
            add_to(near, 1, r)
            back_near[r].start()

        @pl.when(yh == 1)
        def _():
            add_to(far, 1, r)
            back_far[r].start()

    def nearer(r):
        y_copies[0][r].wait()

        @pl.when(yh == 1)
        def _():
            add_to(near, 0, r)
            back_near[r].start()

    launch(0)
    prepare(0)
    compute(0, 3, 0)
    for r in range(2):
        further(r)
    for r in range(2):
        nearer(r)
    for copy in w_in + w_on + [q_kin, q_keep]:
        copy.wait()
    for i in range(3):
        for head in range(2):
            come = gq_buf.at[i, head]
            remote(come, come, gq_send.at[i, head], gq_recv.at[i, head], partner).wait_recv()
    lax.fori_loop(0, 2, queries_part, 0)
    keep = (yh == 0).astype(F32)
    for copy in back_far + back_near:
        copy.wait()
    for r in range(2):
        for kind in range(2):
            total = (
                own[r, kind]
                + y_buf[0, r, kind].astype(F32) * keep
                + x_buf[0, r, kind].astype(F32)
                + x_buf[1, r, kind].astype(F32)
            ).T
            if kind == 0:
                a, b = total[: HD // 2, :], total[HD // 2 :, :]
                c, s = cos[r], sin[r]
                total = jnp.concatenate([a * c + b * s, b * c - a * s], axis=0)
            total = total.astype(BF)
            t_buf[(2 + kind) * HD : (3 + kind) * HD, r * TOK : (r + 1) * TOK] = total
            for piece in range(2):
                dkv_t[r, piece, kind * HD : (kind + 1) * HD, :] = total[:, piece * PIECE : (piece + 1) * PIECE]
    spread = [
        [
            remote(dkv_t.at[r, piece], g_buf.at[i, core, piece], g_send.at[i, r, piece], g_recv.at[i, core, piece], round_z[i][r])
            for i in range(3)
            for r in range(2)
        ]
        for piece in range(2)
    ]
    kin = [
        remote(dkv_t.at[other, piece], g_buf.at[3, core, piece], dk_sems.at[0, piece], dk_sems.at[1, piece], partner)
        for piece in range(2)
    ]
    for piece in range(2):
        for copy in spread[piece] + [kin[piece]]:
            copy.start()
        g_buf[3, core, piece] = dkv_t[core, piece]

    def gathered(piece):
        kin[piece].wait()
        for i in range(3):
            for head in range(2):
                come = g_buf.at[i, head, piece]
                remote(come, come, g_send.at[i, head, piece], g_recv.at[i, head, piece], partner).wait_recv()

    launch(1)
    relay(0)
    prepare(1)
    compute(1, 3, 0)
    relay(1)
    gathered(0)
    cross(z0)
    cross(x0)
    gathered(1)
    cross(z1)
    swap(0)
    cross(x1)
    gx_out[:, :PIECE] = total_of(z0)
    swap(1)
    gx_out[:, PIECE:] = total_of(z1)
    for copy in lasts:
        copy.wait()
    for copy in q_spread + spread[0] + spread[1]:
        copy.wait_send()


def finish(dq, dkv, own, turned, weights, w_rows, cos, sin):
    vmem = pl.BlockSpec(memory_space=pltpu.VMEM)
    hbm = pl.BlockSpec(memory_space=pltpu.HBM)
    any_space = pl.BlockSpec(memory_space=pl.ANY)
    dma = pltpu.SemaphoreType.DMA
    return pl.pallas_call(
        finish_kernel,
        out_shape=(
            jax.ShapeDtypeStruct((HALF, TOK), BF),
            jax.ShapeDtypeStruct((2, 2, QTR, PIECE), BF),
        ),
        in_specs=[any_space] * 3 + [hbm] * 5 + [vmem, vmem],
        out_specs=(vmem,) * 2,
        scratch_shapes=[
            pltpu.VMEM((2, 2, TOK, HD), F32),
            pltpu.VMEM((D, 2 * TOK), BF),
            pltpu.VMEM((4, CHUNK, 8 * HD), BF),
            pltpu.VMEM((4 * HD, 2 * TOK), BF),
            pltpu.VMEM((2, 2, 2 * HD, PIECE), BF),
            pltpu.VMEM((4, 2, 2 * HD, TOK), BF),
            pltpu.VMEM((4, 2, 2, 2 * HD, PIECE), BF),
            pltpu.VMEM((CHUNK, TOK), F32),
            pltpu.VMEM((2, 2, 2, TOK, HD), BF),
            pltpu.VMEM((2, 2, 2, TOK, HD), BF),
            pltpu.VMEM((2, 2, TOK, HD), BF),
            pltpu.VMEM((2, 2, TOK, HD), BF),
            pltpu.VMEM((2, 4, CHUNK, PIECE), BF),
            pltpu.VMEM((2, 3, CHUNK, PIECE), BF),
            pltpu.VMEM((2, 3, HALF, PIECE), BF),
            pltpu.VMEM((2, 3, HALF, PIECE), BF),
            pltpu.VMEM((2, HALF, PIECE), BF),
            dma((8,)), dma((3,)), dma((2, 2)), dma((2, 2, 2)), dma((2, 2, 2)),
            dma((2, 4)), dma((2, 4)), dma((2, 2, 2)), dma((2, 2)), dma((3, 2, 2)), dma((3, 2, 2)),
            dma((3, 2)), dma((3, 2)), dma((6,)), dma((3,)), dma((3,)),
        ],
        compiler_params=pltpu.CompilerParams(
            collective_id=1, has_side_effects=True, vmem_limit_bytes=54 << 20
        ),
        name="finish",
    )(dq, dkv, own, turned, *weights, w_rows, cos, sin)


def emit_kernel(gx, gw, gx_out, gq_out, gk_out, gv_out):
    gx_out[...] = gx[...]
    for head in range(2):
        gq_out[:, head * 2 * HD : (head + 1) * 2 * HD] = gw[0, head]
        gk_out[:, head * HD : (head + 1) * HD] = gw[1, head, :, :HD]
        gv_out[:, head * HD : (head + 1) * HD] = gw[1, head, :, HD:]


def emit(gx, gw):
    vmem = pl.BlockSpec(memory_space=pltpu.VMEM)
    return pl.pallas_call(
        emit_kernel,
        out_shape=(
            jax.ShapeDtypeStruct((HALF, TOK), BF),
            jax.ShapeDtypeStruct((QTR, 4 * HD), BF),
            jax.ShapeDtypeStruct((QTR, 2 * HD), BF),
            jax.ShapeDtypeStruct((QTR, 2 * HD), BF),
        ),
        in_specs=[vmem] * 2,
        out_specs=(vmem,) * 4,
        name="emit",
    )(gx, gw)


def body(queries, keys, values, out_grad, normed, w_query, w_key, w_value, valid_len):
    chip = lax.axis_index("seq") // 2
    inverse_freq = ROPE_BASE ** (-(jnp.arange(HD // 2, dtype=F32) * (2.0 / HD)))
    first = (chip * 2 * TOK + TOK * jnp.arange(2, dtype=jnp.int32)).astype(F32).reshape(2, 1, 1)
    angles = first * inverse_freq[None, :, None]
    within = np.arange(TOK) * (ROPE_BASE ** (-(np.arange(HD // 2) * (2.0 / HD))))[:, None]
    cos_in, sin_in = np.cos(within).astype(np.float32), np.sin(within).astype(np.float32)
    cos_at, sin_at = jnp.cos(angles), jnp.sin(angles)
    cos = cos_at * cos_in - sin_at * sin_in
    sin = sin_at * cos_in + cos_at * sin_in
    base = (2 * chip - 8).astype(jnp.int32).reshape(1)
    weights = (w_query, w_key, w_value)
    lines = [[2 * z + yl for z in range(4)] for yl in range(2)]
    w_rows = lax.all_to_all(pack(weights), "head", 0, 0, axis_index_groups=lines, tiled=True)
    qg, kv, turned = gather(queries, keys, values, out_grad, normed)
    dq, dkv, own = attend(valid_len, base, qg, kv, cos, sin)
    gx, gq, gk, gv = emit(*finish(dq, dkv, own, turned, weights, w_rows, cos, sin))
    return gx.T, gq, gk, gv


def solution(mesh):
    both = P("seq", "head")
    placed = (both, both, both, both, P("seq", None), P(None, "head"), P(None, "head"), P(None, "head"), P())
    return jax.shard_map(
        body, mesh=mesh, in_specs=placed, out_specs=(both,) * 4, check_vma=False
    )
```
